256 devices in a mesh: feat: 8 (over y, core), dom: 32 (over z, x).
Axes of the slice: x: 4, y: 4, z: 8, core: 2. Of those that a mesh axis runs over, the one named last changes fastest.
Arguments:
- features: bfloat16 [8, 4096, 4096], P(None, 'dom', 'feat'), may hold values from -6 to 6
- w_one: bfloat16 [4096, 1024], P('feat'), may hold values from -0.09375 to 0.09375
- w_two: bfloat16 [1024, 512], replicated, may hold values from -0.25 to 0.25
- neighbor: int32 [8, 4096, 10], P('feat', 'dom'), may hold values from 0 to 383
- degree: int32 [8, 4096], P('feat', 'dom'), may hold values from 1 to 10
- send_rows: int32 [8, 1024, 8], P('feat', 'dom'), may hold values from 0 to 127
- grad_out: bfloat16 [8, 4096, 512], P('feat', 'dom'), may hold values from -6 to 6
Outputs:
- out_two: bfloat16 [8, 4096, 512], P('feat', 'dom')
- grad_one: float32 [4096, 1024], P('feat')
- grad_two: float32 [1024, 512], replicated
The draws below stay inside these ranges and needn't reach their ends.
All inputs are finite; a program needn't handle non-finite values.
Results may differ from the reference program's by a relative error of at most 0.015.
Values may be sent and summed in bfloat16 or wider, within the bound.
No kernel may reach another device: no remote copies, remote signals or barrier semaphores. Data moves between devices by JAX's collectives and lax.ppermute only.
A program may use at most 64 MiB of HBM per device.

```python
import math
import jax
import jax.numpy as jnp
from jax import lax

D = 4096
HID = 512
FANOUT = 10
NODES_DEV = 128
KMAX = 8
NODES = 32768
N_FEAT = 8
N_DOM = 32


def place_ends(drawn, own_key, smallest, top_value):
    longest = drawn.shape.index(max(drawn.shape))
    spots = []
    for shift in (0, 1):
        where = [jax.random.randint(jax.random.fold_in(own_key, axis), (), 0, length) for axis, length in enumerate(drawn.shape)]
        where[longest] = (where[longest] + shift) % drawn.shape[longest]
        spots.append(tuple(where))
    return drawn.at[spots[0]].set(smallest).at[spots[1]].set(top_value)


def steps_of(stream_key, shape, cuts, least, largest):
    loudness, own = 1.0, jax.random.fold_in(stream_key, 6)
    for axis_at, shards_of in cuts:
        steps = jnp.exp(jax.random.uniform(jax.random.fold_in(own, axis_at), (shards_of,), jnp.float32, least / len(cuts), largest / len(cuts)))
        loudness = loudness * jnp.repeat(steps, shape[axis_at] // shards_of).reshape([-1 if axis == axis_at else 1 for axis in range(len(shape))])
    return loudness


def gaussian(stream_key, dims, deviation, limit, pieces=(), kind=jnp.bfloat16):
    array = deviation * jax.random.normal(stream_key, dims, jnp.float32)
    if pieces:
        array = array * steps_of(stream_key, dims, pieces, -0.22, 0.18)
    return jnp.clip(array, -limit, limit).astype(kind)


def setup_inputs(seed: int = 0) -> dict:
    keys = jax.random.split(jax.random.key(seed), 8)
    return {
        "features": gaussian(keys[0], (N_FEAT, N_DOM * NODES_DEV, D), 1.0, 6.0, ((1, 32), (2, 8))),
        "w_one": gaussian(keys[1], (D, 2 * HID), D ** -0.5, 0.09375, ((0, 8),)),
        "w_two": gaussian(keys[2], (2 * HID, HID), HID ** -0.5, 0.25),
        "neighbor": place_ends(jax.random.randint(keys[3], (N_FEAT, N_DOM * NODES_DEV, FANOUT), 0, NODES_DEV + N_DOM * KMAX), jax.random.fold_in(keys[3], 1), 0, (NODES_DEV + N_DOM * KMAX) - 1).astype(jnp.int32),
        "degree": place_ends(jax.random.randint(keys[4], (N_FEAT, N_DOM * NODES_DEV), 1, FANOUT + 1), jax.random.fold_in(keys[4], 1), 1, FANOUT).astype(jnp.int32),
        "send_rows": place_ends(jax.random.randint(keys[5], (N_FEAT, N_DOM * N_DOM, KMAX), 0, NODES_DEV), jax.random.fold_in(keys[5], 1), 0, NODES_DEV - 1).astype(jnp.int32),
        "grad_out": gaussian(keys[6], (N_FEAT, N_DOM * NODES_DEV, HID), 1.0, 6.0, ((0, 8), (1, 32))),
    }


def mean_weights(degree):
    slots = jnp.arange(FANOUT, dtype=jnp.int32)
    used = (slots[None, None, :] < degree[:, :, None]).astype(jnp.float32)
    return used / degree[:, :, None].astype(jnp.float32)

def spread(values, neighbor, weight, sends):
    width = values.shape[-1]
    boxes = jax.vmap(lambda rows, index: rows[index])(values, sends)
    recv = jnp.swapaxes(boxes, 0, 1).reshape(N_DOM, N_DOM * KMAX, width)
    table = jnp.concatenate([values, recv], axis=1)
    gathered = jax.vmap(lambda rows, index: rows[index])(table, neighbor)
    return lax.optimization_barrier(jnp.sum(gathered.astype(jnp.float32) * weight[..., None], axis=2))

def gather_back(grads, neighbor, weight, sends):
    width = grads.shape[-1]
    terms = weight[..., None] * grads[:, :, None, :]

    def collect(index, vals):
        empty = jnp.zeros((NODES_DEV + N_DOM * KMAX, width), jnp.float32)
        return empty.at[index.reshape(-1)].add(vals.reshape(-1, width))
    table = jax.vmap(collect)(neighbor, terms)
    local = table[:, :NODES_DEV]
    slots = table[:, NODES_DEV:].astype(jnp.bfloat16).reshape(N_DOM, N_DOM, KMAX, width)
    returned = jnp.swapaxes(slots, 0, 1)

    def home(index, vals):
        empty = jnp.zeros((NODES_DEV, width), jnp.float32)
        return empty.at[index.reshape(-1)].add(vals.reshape(-1, width).astype(jnp.float32))
    return local + jax.vmap(home)(sends, returned)

def reference(features, w_one, w_two, neighbor, degree, send_rows, grad_out):

    def group(items):
        feats, nbrs, degs, sends, grads = items
        nbrs = nbrs.reshape(N_DOM, NODES_DEV, FANOUT)
        degs = degs.reshape(N_DOM, NODES_DEV)
        sends = sends.reshape(N_DOM, N_DOM, KMAX)
        weight = mean_weights(degs)
        proj = jnp.dot(feats, w_one, preferred_element_type=jnp.float32).reshape(N_DOM, NODES_DEV, 2 * HID)
        p_self = proj[..., :HID]
        p_near = proj[..., HID:].astype(jnp.bfloat16)
        pre = p_self + spread(p_near, nbrs, weight, sends)
        hidden = (pre * jax.nn.sigmoid(pre)).astype(jnp.bfloat16)
        agg = spread(hidden, nbrs, weight, sends).astype(jnp.bfloat16)
        joined = jnp.concatenate([hidden, agg], axis=-1).reshape(N_DOM * NODES_DEV, 2 * HID)
        out = jnp.dot(joined, w_two, preferred_element_type=jnp.float32).astype(jnp.bfloat16)
        two_sum = jnp.dot(joined.T, grads, preferred_element_type=jnp.float32)
        dcat = jnp.dot(grads, w_two.T, preferred_element_type=jnp.float32).reshape(N_DOM, NODES_DEV, 2 * HID)
        d_hidden = dcat[..., :HID] + gather_back(dcat[..., HID:], nbrs, weight, sends)
        sig = jax.nn.sigmoid(pre)
        d_pre = d_hidden * sig * (1.0 + pre * (1.0 - sig))
        d_near = gather_back(d_pre, nbrs, weight, sends)
        d_proj = jnp.concatenate([d_pre, d_near], axis=-1).astype(jnp.bfloat16).reshape(N_DOM * NODES_DEV, 2 * HID)
        one_sum = jnp.dot(feats.T, d_proj, preferred_element_type=jnp.float32)
        return (out, one_sum, two_sum)
    outs, one_sums, two_sums = lax.map(group, (features, neighbor, degree, send_rows, grad_out))
    scale = 1.0 / math.sqrt(NODES)
    return (outs, lax.optimization_barrier(jnp.sum(one_sums, axis=0)) * scale, lax.optimization_barrier(jnp.sum(two_sums, axis=0)) * scale)
```

```python
import math

import jax
import jax.numpy as jnp
from jax import lax
from jax.experimental import pallas as pl
from jax.experimental.pallas import tpu as pltpu
from jax.sharding import PartitionSpec as P

F32 = jnp.float32
BF16 = jnp.bfloat16
CHIPS = 4
NT = (((1,), (1,)), ((), ()))
TN = (((0,), (0,)), ((), ()))


def step(core):
    return 1 if core == 0 else -1


FORWARD = [(y * 2 + c, (y + step(c)) % CHIPS * 2 + c) for y in range(CHIPS) for c in range(2)]
BACKWARD = [(y * 2 + c, (y - step(c)) % CHIPS * 2 + c) for y in range(CHIPS) for c in range(2)]
SWAP = [(i, i ^ 1) for i in range(2 * CHIPS)]


def mm(a, b, dims=(((1,), (0,)), ((), ()))):
    return lax.dot_general(a, b, dims, preferred_element_type=F32)


def whole(name, body, outs, *args):
    return pl.pallas_call(body, out_shape=outs, name=name)(*args)


def shape(dims, kind=BF16):
    return jax.ShapeDtypeStruct(dims, kind)


def trade(boxes):
    return lax.all_to_all(boxes, "dom", split_axis=0, concat_axis=0, tiled=True)


def tables_body(nbr_t, nbr, deg_row, deg_col, send_col, send_row, give, take, own, own_t):
    nodes = nbr.shape[0]
    fan = nbr.shape[1]
    span = give.shape[0]

    def entries(axis, dims):
        r = lax.broadcasted_iota(jnp.int32, dims, axis)
        return nodes + (r // 16) * 8 + r % 16, r % 16

    down, down_j = entries(0, (span, nodes))
    down = jnp.where(down_j < 8, down, -2)
    side, side_j = entries(1, (nodes, span))
    side = jnp.where(side_j >= 8, side - 8, -2)
    row = lax.broadcasted_iota(jnp.int32, (nodes, nodes), 0)
    col = lax.broadcasted_iota(jnp.int32, (nodes, nodes), 1)
    give_sum = jnp.zeros((span, nodes), F32)
    take_sum = jnp.zeros((nodes, span), F32)
    own_sum = jnp.zeros((nodes, nodes), F32)
    own_t_sum = jnp.zeros((nodes, nodes), F32)
    for s in range(fan):
        as_row = jnp.where(s < deg_row[...], nbr_t[s : s + 1, :], -1)
        as_col = jnp.where(s < deg_col[...], nbr[:, s : s + 1], -1)
        give_sum += jnp.where(down == as_row, 1.0, 0.0)
        take_sum += jnp.where(side == as_col, 1.0, 0.0)
        own_sum += jnp.where(col == as_col, 1.0, 0.0)
        own_t_sum += jnp.where(row == as_row, 1.0, 0.0)
    give[:, :nodes] = give_sum.astype(BF16)
    node_lane = lax.broadcasted_iota(jnp.int32, (span, nodes), 1)
    give[:, nodes:] = jnp.where(node_lane == send_col[...], 1.0, 0.0).astype(BF16)
    take[:nodes, :] = take_sum.astype(BF16)
    node_row = lax.broadcasted_iota(jnp.int32, (nodes, span), 0)
    take[nodes:, :] = jnp.where(node_row == send_row[...], 1.0, 0.0).astype(BF16)
    own[...] = own_sum.astype(BF16)
    own_t[...] = own_t_sum.astype(BF16)


def project(order, flat, w_one, kind):
    groups, nodes, cols = flat.shape
    width = w_one.shape[1]
    picks = order.shape[0]

    def body(order_ref, rows, w, out):
        out[0] = mm(rows[0], w[...]).astype(kind)

    return pl.pallas_call(
        body,
        out_shape=shape((picks, nodes, width), kind),
        grid_spec=pltpu.PrefetchScalarGridSpec(
            num_scalar_prefetch=1,
            grid=(picks,),
            in_specs=[
                pl.BlockSpec((1, nodes, cols), lambda i, o: (o[i], 0, 0)),
                pl.BlockSpec((cols, width), lambda i, o: (0, 0)),
            ],
            out_specs=pl.BlockSpec((1, nodes, width), lambda i, o: (i, 0, 0)),
        ),
        name="project",
        cost_estimate=pl.CostEstimate(
            flops=2 * picks * nodes * cols * width,
            bytes_accessed=2 * picks * nodes * (cols + width),
            transcendentals=0,
        ),
    )(order, flat, w_one)


def forward_body(part, got, near, far, grads, inv, give, p_self, p_near, boxes):
    width = grads.shape[1]
    total = (
        part[...] + got[...].astype(F32) + near[...].astype(F32) + far[...].astype(F32)
    )
    p_self[...] = total[:, :width]
    mine = total[:, width:].astype(BF16)
    p_near[...] = mine
    scaled = (grads[...].astype(F32) * inv[...]).astype(BF16)
    boxes[...] = mm(give[...], jnp.concatenate([scaled, mine], axis=0)).astype(BF16)


def middle_body(
    recv, p_self, p_near, grads, inv, w_two, give, take, own, own_t,
    boxes, d_pre_out, near_local, hidden_out, back_out,
):
    nodes, width = grads.shape
    both = mm(take[...], recv[...])
    grad = grads[...]
    scaled = (grad.astype(F32) * inv[...]).astype(BF16)
    pre = p_self[...] + inv[...] * (both[:nodes] + mm(own[...], p_near[...]))
    back = (both[nodes:] + mm(own_t[...], scaled)).astype(BF16)
    back_out[...] = back
    d_hidden = mm(grad, w_two[:width, :], NT) + mm(back, w_two[width:, :], NT)
    sig = jax.nn.sigmoid(pre)
    hidden = (pre * sig).astype(BF16)
    hidden_out[...] = hidden
    d_pre = d_hidden * sig * (1.0 + pre * (1.0 - sig))
    d_pre_out[...] = d_pre.astype(BF16)
    term = (d_pre * inv[...]).astype(BF16)
    boxes[...] = mm(give[...], jnp.concatenate([term, hidden], axis=0)).astype(BF16)
    near_local[...] = mm(own_t[...], term)


def near_body(recv, near_local, take, out):
    out[...] = (near_local[...] + mm(take[...], recv[...])).astype(BF16)


def out_body(recv, hidden, inv, take, own, w_two, out):
    width = hidden.shape[1]
    agg = (inv[...] * (mm(take[...], recv[...]) + mm(own[...], hidden[...]))).astype(BF16)
    out[...] = (mm(hidden[...], w_two[:width, :]) + mm(agg, w_two[width:, :])).astype(BF16)


def two_body(hidden, grads, back, out):
    width = hidden.shape[1]
    out[:width, :] = mm(hidden[...], grads[...], TN)
    out[width:, :] = mm(hidden[...], back[...], TN)


def weight_grad(name, order, flat, mine, other, *extra, finish, out):
    groups, nodes, cols = flat.shape
    width = mine.shape[2]
    half = groups // 2

    def body(order_ref, rows, a, b, *rest):
        acc = rest[-1]
        i = pl.program_id(0)

        @pl.when(i == 0)
        def _():
            acc[...] = jnp.zeros_like(acc)

        @pl.when(i < half)
        def _():
            acc[...] += mm(rows[0], a[0], TN)

        @pl.when(i >= half)
        def _():
            acc[...] += mm(rows[0], b[0], TN)

        @pl.when(i == groups - 1)
        def _():
            finish(acc, *rest[:-1])

    fixed = [pl.BlockSpec(e.shape, lambda i, o, n=e.ndim: (0,) * n) for e in extra]
    return pl.pallas_call(
        body,
        out_shape=out,
        grid_spec=pltpu.PrefetchScalarGridSpec(
            num_scalar_prefetch=1,
            grid=(groups,),
            in_specs=[
                pl.BlockSpec((1, nodes, cols), lambda i, o: (o[i], 0, 0)),
                pl.BlockSpec((1, nodes, width), lambda i, o: (jnp.minimum(i, half - 1), 0, 0)),
                pl.BlockSpec((1, nodes, width), lambda i, o: (jnp.maximum(i - half, 0), 0, 0)),
                *fixed,
            ],
            out_specs=pl.BlockSpec(out.shape, lambda i, o, n=len(out.shape): (0,) * n),
            scratch_shapes=[pltpu.VMEM((cols, width), F32)],
        ),
        name=name,
        cost_estimate=pl.CostEstimate(
            flops=2 * groups * nodes * cols * width,
            bytes_accessed=2 * groups * nodes * (cols + width),
            transcendentals=0,
        ),
    )(order, flat, mine, other, *extra)


def self_finish(acc, out):
    out[...] = acc[...].astype(BF16)


def near_finish(acc, first, out):
    parts, rows, width = out.shape
    half = rows // 2
    out[:, :half, :] = first[...].reshape(parts, half, width)
    out[:, half:, :] = acc[...].astype(BF16).reshape(parts, half, width)


def sum_body(scale, recv, out):
    total = recv[0].astype(F32)
    for k in range(1, recv.shape[0]):
        total += recv[k].astype(F32)
    out[...] = jnp.broadcast_to((total * scale).astype(BF16)[None], out.shape)


def on_device(features, w_one, w_two, neighbor, degree, send_rows, grad_out):
    groups, nodes, cols = features.shape
    width = w_two.shape[1]
    parts = lax.axis_size("dom")
    feat = lax.axis_index("feat")
    y, core = feat // 2, feat % 2
    turn = 1 - 2 * core
    nbr = neighbor[0]
    deg = degree[0]
    sends = send_rows[0]
    kmax = sends.shape[1]
    grads = grad_out[0]
    scale = 1.0 / math.sqrt(groups * nodes * parts)

    def group_ids(offsets, on_core):
        return jnp.stack([(y + o + CHIPS) % CHIPS * 2 + on_core for o in offsets])

    theirs = project(group_ids([2, turn, -turn, 0], 1 - core), features, w_one, BF16)
    got = lax.ppermute(theirs, "feat", SWAP)
    mine = project(group_ids([2, -turn, turn, 0], core), features, w_one, F32)

    inv = (1.0 / deg.astype(F32))[:, None]
    blank = jnp.full_like(sends, -1)
    send_col = jnp.concatenate([blank, sends], axis=1).reshape(-1, 1)
    send_row = jnp.concatenate([sends, blank], axis=1).reshape(1, -1)
    span = 2 * sends.size
    give, take, own, own_t = whole(
        "tables",
        tables_body,
        (
            shape((span, 2 * nodes)),
            shape((2 * nodes, span)),
            shape((nodes, nodes)),
            shape((nodes, nodes)),
        ),
        nbr.T, nbr, deg[None, :], deg[:, None], send_col, send_row,
    )

    def sent(k):
        return mine[k] + got[k].astype(F32)

    relay = lax.ppermute(sent(0).astype(BF16), "feat", FORWARD)
    near = lax.ppermute(sent(1).astype(BF16), "feat", BACKWARD)
    far = lax.ppermute((sent(2) + relay.astype(F32)).astype(BF16), "feat", FORWARD)
    p_self, p_near, boxes = whole(
        "forward",
        forward_body,
        (shape((nodes, width), F32), shape((nodes, width)), shape((span, width))),
        mine[3], got[3], near, far, grads, inv, give,
    )
    recv = trade(boxes.reshape(parts, 2 * kmax, width)).reshape(span, width)
    boxes, d_pre, near_local, hidden, back = whole(
        "middle",
        middle_body,
        (
            shape((span, width)),
            shape((nodes, width)),
            shape((nodes, width), F32),
            shape((nodes, width)),
            shape((nodes, width)),
        ),
        recv, p_self, p_near, grads, inv, w_two, give, take, own, own_t,
    )
    recv = trade(boxes.reshape(parts, 2 * kmax, width)).reshape(span, width)

    two_sum = whole("two_sum", two_body, shape((2 * width, width), F32), hidden, grads, back)
    two_sum = lax.psum_scatter(two_sum, "feat", scatter_dimension=0, tiled=True)
    two_sum = lax.psum(two_sum, "dom")
    two_sum = lax.all_gather(two_sum * scale, "feat", axis=0, tiled=True)

    def gather(block):
        one = lax.ppermute(block, "feat", FORWARD)
        two = lax.ppermute(block, "feat", BACKWARD)
        three = lax.ppermute(one, "feat", FORWARD)
        held = jnp.stack([block, one, two, three])
        return held, lax.ppermute(held, "feat", SWAP)

    order = jnp.concatenate(
        [group_ids([0, -turn, turn, 2], core), group_ids([0, turn, -turn, 2], 1 - core)]
    )
    first = weight_grad(
        "self_grad", order, features, *gather(d_pre), finish=self_finish, out=shape((cols, width))
    )
    d_near = whole(
        "near", near_body, shape((nodes, width)), recv, near_local, take[nodes:, :]
    )
    out = whole(
        "out", out_body, shape((nodes, width)), recv, hidden, inv, take[:nodes, :], own, w_two
    )
    rows = 2 * cols // parts
    terms = weight_grad(
        "near_grad", order, features, *gather(d_near), first,
        finish=near_finish, out=shape((parts, rows, width)),
    )
    terms = trade(terms)
    chunk = whole(
        "sum", lambda recv, out: sum_body(scale, recv, out), shape((parts, rows, width)), terms
    )
    full = trade(chunk).astype(F32)
    one_sum = jnp.concatenate([full[:, : rows // 2], full[:, rows // 2 :]], axis=2)
    return out[None], one_sum.reshape(cols, 2 * width), two_sum


def solution(mesh):
    in_specs = (
        P(None, "dom", "feat"),
        P("feat", None),
        P(),
        P("feat", "dom", None),
        P("feat", "dom"),
        P("feat", "dom", None),
        P("feat", "dom", None),
    )
    out_specs = (P("feat", "dom", None), P("feat", None), P())
    return jax.shard_map(
        on_device, mesh=mesh, in_specs=in_specs, out_specs=out_specs, check_vma=False
    )
```

```python
import math

import jax
import jax.numpy as jnp
from jax import lax
from jax.experimental import pallas as pl
from jax.experimental.pallas import tpu as pltpu
from jax.sharding import PartitionSpec as P

F32 = jnp.float32
BF16 = jnp.bfloat16
CHIPS = 4
NT = (((1,), (1,)), ((), ()))
TN = (((0,), (0,)), ((), ()))


def step(core):
    return 1 if core == 0 else -1


FORWARD = [(y * 2 + c, (y + step(c)) % CHIPS * 2 + c) for y in range(CHIPS) for c in range(2)]
BACKWARD = [(y * 2 + c, (y - step(c)) % CHIPS * 2 + c) for y in range(CHIPS) for c in range(2)]
SWAP = [(i, i ^ 1) for i in range(2 * CHIPS)]


def mm(a, b, dims=(((1,), (0,)), ((), ()))):
    return lax.dot_general(a, b, dims, preferred_element_type=F32)


def whole(name, body, outs, *args):
    return pl.pallas_call(body, out_shape=outs, name=name)(*args)


def shape(dims, kind=BF16):
    return jax.ShapeDtypeStruct(dims, kind)


def trade(boxes):
    return lax.all_to_all(boxes, "dom", split_axis=0, concat_axis=0, tiled=True)


def tables_body(nbr_t, nbr, deg_row, deg_col, send_col, send_row, give, take, own, own_t):
    nodes = nbr.shape[0]
    fan = nbr.shape[1]
    span = give.shape[0]

    def entries(axis, dims):
        r = lax.broadcasted_iota(jnp.int32, dims, axis)
        return nodes + (r // 16) * 8 + r % 16, r % 16

    down, down_j = entries(0, (span, nodes))
    down = jnp.where(down_j < 8, down, -2)
    side, side_j = entries(1, (nodes, span))
    side = jnp.where(side_j >= 8, side - 8, -2)
    row = lax.broadcasted_iota(jnp.int32, (nodes, nodes), 0)
    col = lax.broadcasted_iota(jnp.int32, (nodes, nodes), 1)
    give_sum = jnp.zeros((span, nodes), F32)
    take_sum = jnp.zeros((nodes, span), F32)
    own_sum = jnp.zeros((nodes, nodes), F32)
    own_t_sum = jnp.zeros((nodes, nodes), F32)
    for s in range(fan):
        as_row = jnp.where(s < deg_row[...], nbr_t[s : s + 1, :], -1)
        as_col = jnp.where(s < deg_col[...], nbr[:, s : s + 1], -1)
        give_sum += jnp.where(down == as_row, 1.0, 0.0)
        take_sum += jnp.where(side == as_col, 1.0, 0.0)
        own_sum += jnp.where(col == as_col, 1.0, 0.0)
        own_t_sum += jnp.where(row == as_row, 1.0, 0.0)
    give[:, :nodes] = give_sum.astype(BF16)
    node_lane = lax.broadcasted_iota(jnp.int32, (span, nodes), 1)
    give[:, nodes:] = jnp.where(node_lane == send_col[...], 1.0, 0.0).astype(BF16)
    take[:nodes, :] = take_sum.astype(BF16)
    node_row = lax.broadcasted_iota(jnp.int32, (nodes, span), 0)
    take[nodes:, :] = jnp.where(node_row == send_row[...], 1.0, 0.0).astype(BF16)
    own[...] = own_sum.astype(BF16)
    own_t[...] = own_t_sum.astype(BF16)


def places(offsets, other):
    feat = lax.axis_index("feat")
    y, core = feat // 2, feat % 2
    turn = 1 - 2 * core
    held = 1 - core if other else core
    return [(y + CHIPS + o * (turn if t else 1)) % CHIPS * 2 + held for o, t in offsets]


SUM_MINE = ((2, False), (-1, True), (1, True), (0, False))
SUM_OTHER = ((2, False), (1, True), (-1, True), (0, False))
GET_MINE = ((0, False), (-1, True), (1, True), (2, False))
GET_OTHER = ((0, False), (1, True), (-1, True), (2, False))


def project(flat, w_one, other, kind):
    groups, nodes, cols = flat.shape
    width = w_one.shape[1]

    def body(rows, w, out):
        ids = places(SUM_OTHER if other else SUM_MINE, other)
        picked = jnp.concatenate([rows[g] for g in ids], axis=0)
        out[...] = mm(picked, w[...]).astype(kind).reshape(out.shape)

    return pl.pallas_call(
        body,
        out_shape=shape((CHIPS, nodes, width), kind),
        name="project",
        cost_estimate=pl.CostEstimate(
            flops=2 * CHIPS * nodes * cols * width,
            bytes_accessed=2 * (groups * nodes * cols + cols * width),
            transcendentals=0,
        ),
    )(flat, w_one)


def forward_body(part, got, near, far, grads, inv, give, p_self, p_near, boxes):
    width = grads.shape[1]
    total = (
        part[...] + got[...].astype(F32) + near[...].astype(F32) + far[...].astype(F32)
    )
    p_self[...] = total[:, :width]
    mine = total[:, width:].astype(BF16)
    p_near[...] = mine
    scaled = (grads[...].astype(F32) * inv[...]).astype(BF16)
    boxes[...] = mm(give[...], jnp.concatenate([scaled, mine], axis=0)).astype(BF16)


def middle_body(
    recv, p_self, p_near, grads, inv, w_two, give, take, own, own_t,
    boxes, d_pre_out, near_local, hidden_out, back_out,
):
    nodes, width = grads.shape
    both = mm(take[...], recv[...])
    grad = grads[...]
    scaled = (grad.astype(F32) * inv[...]).astype(BF16)
    pre = p_self[...] + inv[...] * (both[:nodes] + mm(own[...], p_near[...]))
    back = (both[nodes:] + mm(own_t[...], scaled)).astype(BF16)
    back_out[...] = back
    d_hidden = mm(grad, w_two[:width, :], NT) + mm(back, w_two[width:, :], NT)
    sig = jax.nn.sigmoid(pre)
    hidden = (pre * sig).astype(BF16)
    hidden_out[...] = hidden
    d_pre = d_hidden * sig * (1.0 + pre * (1.0 - sig))
    d_pre_out[...] = d_pre.astype(BF16)
    term = (d_pre * inv[...]).astype(BF16)
    boxes[...] = mm(give[...], jnp.concatenate([term, hidden], axis=0)).astype(BF16)
    near_local[...] = mm(own_t[...], term)


def near_body(recv, near_local, take, out):
    out[...] = (near_local[...] + mm(take[...], recv[...])).astype(BF16)


def out_body(recv, hidden, inv, take, own, w_two, out):
    width = hidden.shape[1]
    agg = (inv[...] * (mm(take[...], recv[...]) + mm(own[...], hidden[...]))).astype(BF16)
    out[...] = (mm(hidden[...], w_two[:width, :]) + mm(agg, w_two[width:, :])).astype(BF16)


def two_body(hidden, grads, back, mine, theirs):
    width = hidden.shape[1]
    nodes = mine.shape[1]
    both = jnp.concatenate([grads[...], back[...]], axis=1)
    pair = mm(hidden[...], both, TN)
    total = jnp.concatenate([pair[:, :width], pair[:, width:]], axis=0)
    total = total.reshape(2 * CHIPS, nodes, width)

    def run(scratch):
        scratch[...] = total
        for k, g in enumerate(places(SUM_MINE, False)):
            mine[k] = scratch[g]
        for k, g in enumerate(places(SUM_OTHER, True)):
            theirs[k] = scratch[g].astype(BF16)

    pl.run_scoped(run, pltpu.VMEM(total.shape, F32))


def mix_body(mine, got, block, ahead, behind):
    ahead[0] = block[...]
    behind[0] = block[...]
    ahead[1] = (mine[0] + got[0].astype(F32)).astype(BF16)
    behind[1] = (mine[1] + got[1].astype(F32)).astype(BF16)


def pass_body(mine, got, relay, ahead):
    ahead[0] = relay[0]
    ahead[1] = (mine[2] + got[2].astype(F32) + relay[1].astype(F32)).astype(BF16)


def turn_body(flat, out):
    groups, nodes, cols = flat.shape
    for g in range(groups):
        out[:, g * nodes : (g + 1) * nodes] = flat[g].T


def grad_of(flat_t, blocks, other, stack):
    for g, block in zip(places(GET_MINE, False), blocks):
        stack[g] = block
    for k, g in enumerate(places(GET_OTHER, True)):
        stack[g] = other[k]
    groups, nodes, width = stack.shape
    return mm(flat_t[...], stack[...].reshape(groups * nodes, width))


def self_body(flat_t, b0, b1, b2, b3, other, out, stack):
    out[...] = grad_of(flat_t, (b0[...], b1[0], b2[0], b3[0]), other, stack).astype(BF16)


def near_grad_body(flat_t, b0, b1, b2, b3, other, first, mine, got, near, far, out, stack):
    parts, rows, width = out.shape
    part = rows // 9 * 2
    total = grad_of(flat_t, (b0[...], b1[...], b2[...], b3[...]), other, stack).astype(BF16)
    for k in range(2):
        cut = slice(k * width, (k + 1) * width)
        out[:, k * part : (k + 1) * part, :] = first[:, cut].reshape(parts, part, width)
        out[:, (k + 2) * part : (k + 3) * part, :] = total[:, cut].reshape(parts, part, width)
    two = mine[3] + got[3].astype(F32) + near[1].astype(F32) + far[1].astype(F32)
    half = parts // 2
    for k in range(2):
        cut = two[:, k * width : (k + 1) * width].astype(BF16)
        out[k * half : (k + 1) * half, 4 * part :, :] = cut.reshape(half, part // 2, width)


def sum_body(scale, recv, out):
    total = recv[0].astype(F32)
    for k in range(1, recv.shape[0]):
        total += recv[k].astype(F32)
    out[...] = jnp.broadcast_to((total * scale).astype(BF16)[None], out.shape)


def spread_body(full, out):
    parts, rows, width = full.shape
    part = out.shape[0] // parts
    for k in range(4):
        piece = full[:, k * part : (k + 1) * part, :].astype(F32)
        out[:, k * width : (k + 1) * width] = piece.reshape(parts * part, width)


def join_body(b0, b1, b2, b3, other, out):
    nodes = b0.shape[0]

    def put(g, block):
        out[pl.ds(pl.multiple_of(g * nodes, nodes), nodes), :] = block.astype(F32)

    for g, block in zip(places(GET_MINE, False), (b0, b1, b2, b3)):
        put(g, block[...])
    for k, g in enumerate(places(GET_OTHER, True)):
        put(g, other[k])


def on_device(features, w_one, w_two, neighbor, degree, send_rows, grad_out):
    groups, nodes, cols = features.shape
    width = w_two.shape[1]
    parts = lax.axis_size("dom")
    nbr = neighbor[0]
    deg = degree[0]
    sends = send_rows[0]
    kmax = sends.shape[1]
    grads = grad_out[0]
    scale = 1.0 / math.sqrt(groups * nodes * parts)

    def forward(block):
        return lax.ppermute(block, "feat", FORWARD)

    def backward(block):
        return lax.ppermute(block, "feat", BACKWARD)

    def swap(block):
        return lax.ppermute(block, "feat", SWAP)

    got = swap(project(features, w_one, True, BF16))
    mine = project(features, w_one, False, F32)

    inv = (1.0 / deg.astype(F32))[:, None]
    blank = jnp.full_like(sends, -1)
    send_col = jnp.concatenate([blank, sends], axis=1).reshape(-1, 1)
    send_row = jnp.concatenate([sends, blank], axis=1).reshape(1, -1)
    span = 2 * sends.size
    give, take, own, own_t = whole(
        "tables",
        tables_body,
        (
            shape((span, 2 * nodes)),
            shape((2 * nodes, span)),
            shape((nodes, nodes)),
            shape((nodes, nodes)),
        ),
        nbr.T, nbr, deg[None, :], deg[:, None], send_col, send_row,
    )
    flat_t = whole("turn", turn_body, shape((cols, groups * nodes)), features)

    def sent(k):
        return mine[k] + got[k].astype(F32)

    relay = forward(sent(0).astype(BF16))
    near = backward(sent(1).astype(BF16))
    far = forward((sent(2) + relay.astype(F32)).astype(BF16))
    p_self, p_near, boxes = whole(
        "forward",
        forward_body,
        (shape((nodes, width), F32), shape((nodes, width)), shape((span, width))),
        mine[3], got[3], near, far, grads, inv, give,
    )
    recv = trade(boxes.reshape(parts, 2 * kmax, width)).reshape(span, width)
    boxes, d_pre, near_local, hidden, back = whole(
        "middle",
        middle_body,
        (
            shape((span, width)),
            shape((nodes, width)),
            shape((nodes, width), F32),
            shape((nodes, width)),
            shape((nodes, width)),
        ),
        recv, p_self, p_near, grads, inv, w_two, give, take, own, own_t,
    )
    recv = trade(boxes.reshape(parts, 2 * kmax, width)).reshape(span, width)

    block = 2 * width // groups
    mine, theirs = whole(
        "two_sum",
        two_body,
        (shape((CHIPS, block, width), F32), shape((CHIPS, block, width))),
        hidden, grads, back,
    )
    got = swap(theirs)
    pair = shape((2, nodes, width))
    ahead, behind = whole("mix", mix_body, (pair, pair), mine, got, d_pre)
    relay = forward(ahead)
    near = backward(behind)
    far = forward(whole("pass", pass_body, pair, mine, got, relay))
    other = swap(jnp.stack([d_pre, relay[0], near[0], far[0]]))
    stack = [pltpu.VMEM((groups, nodes, width), BF16)]
    first = pl.pallas_call(
        self_body, out_shape=shape((cols, width)), scratch_shapes=stack, name="self_grad"
    )(flat_t, d_pre, relay, near, far, other)

    d_near = whole("near", near_body, shape((nodes, width)), recv, near_local, take[nodes:, :])

    def gather(block):
        one = forward(block)
        two = backward(block)
        three = forward(one)
        return block, one, two, three, swap(jnp.stack([block, one, two, three]))

    rows = 9 * cols // parts // 2
    terms = pl.pallas_call(
        near_grad_body,
        out_shape=shape((parts, rows, width // 2)),
        scratch_shapes=stack,
        name="near_grad",
    )(flat_t, *gather(d_near), first, mine, got, near, far)
    terms = trade(terms)
    out = whole(
        "out", out_body, shape((nodes, width)), recv, hidden, inv, take[:nodes, :], own, w_two
    )
    full = trade(
        whole("sum", lambda recv, out: sum_body(scale, recv, out), shape(terms.shape), terms)
    )
    tail = full[:, 8 * rows // 9 :, :]
    half = parts // 2
    chunk = jnp.concatenate(
        [tail[:half].reshape(block, -1), tail[half:].reshape(block, -1)], axis=1
    )
    two = whole("join", join_body, shape((2 * width, width), F32), *gather(chunk))
    one = whole("spread", spread_body, shape((cols, 2 * width), F32), full)
    return out[None], one, two


def solution(mesh):
    in_specs = (
        P(None, "dom", "feat"),
        P("feat", None),
        P(),
        P("feat", "dom", None),
        P("feat", "dom"),
        P("feat", "dom", None),
        P("feat", "dom", None),
    )
    out_specs = (P("feat", "dom", None), P("feat", None), P())
    return jax.shard_map(
        on_device, mesh=mesh, in_specs=in_specs, out_specs=out_specs, check_vma=False
    )
```

```python
import math

import jax
import jax.numpy as jnp
from jax import lax
from jax.experimental import pallas as pl
from jax.experimental.pallas import tpu as pltpu
from jax.sharding import PartitionSpec as P

F32 = jnp.float32
BF16 = jnp.bfloat16
CHIPS = 4
NT = (((1,), (1,)), ((), ()))
TN = (((0,), (0,)), ((), ()))


def step(core):
    return 1 if core == 0 else -1


def along_y(sign):
    return [
        (y * 2 + c, (y + sign * step(c)) % CHIPS * 2 + c) for y in range(CHIPS) for c in range(2)
    ]


def along_x(sign, parts, feats):
    def device(f, z, x):
        return f * parts + z * CHIPS + x % CHIPS

    return [
        (device(f, z, x), device(f, z, x + sign * step(f % 2)))
        for f in range(feats)
        for z in range(parts // CHIPS)
        for x in range(CHIPS)
    ]


SWAP = [(i, i ^ 1) for i in range(2 * CHIPS)]


def mm(a, b, dims=(((1,), (0,)), ((), ()))):
    return lax.dot_general(a, b, dims, preferred_element_type=F32)


def whole(name, body, outs, *args, flops=0, scratch=()):
    every = list(args) + list(outs if isinstance(outs, tuple) else (outs,))
    moved = sum(math.prod(e.shape) * jnp.dtype(e.dtype).itemsize for e in every)
    return pl.pallas_call(
        body,
        out_shape=outs,
        scratch_shapes=scratch,
        name=name,
        cost_estimate=pl.CostEstimate(
            flops=flops, bytes_accessed=moved + (4 << 20), transcendentals=0
        ),
    )(*args)


def shape(dims, kind=BF16):
    return jax.ShapeDtypeStruct(dims, kind)


def trade(boxes, groups=None):
    return lax.all_to_all(
        boxes, "dom", split_axis=0, concat_axis=0, axis_index_groups=groups, tiled=True
    )


def tables_body(
    nbr_t, nbr, deg_row, deg_col, send_col, send_row, two_col, two_row, flat,
    give, take, own, own_t, back, home, pick, mean, flat_t,
):
    nodes = nbr.shape[0]
    fan = nbr.shape[1]
    span = give.shape[0]
    half = span // 2

    def entries(axis, dims):
        r = lax.broadcasted_iota(jnp.int32, dims, axis)
        return nodes + (r // 16) * 8 + r % 16, r % 16

    down, down_j = entries(0, (span, nodes))
    down = jnp.where(down_j < 8, down, -2)
    side, side_j = entries(1, (nodes, span))
    side = jnp.where(side_j >= 8, side - 8, -2)
    row = lax.broadcasted_iota(jnp.int32, (nodes + half, nodes), 0)
    col = lax.broadcasted_iota(jnp.int32, (nodes, nodes + half), 1)
    give_sum = jnp.zeros((span, nodes), F32)
    take_sum = jnp.zeros((nodes, span), F32)
    by_col = jnp.zeros((nodes, nodes + half), F32)
    by_row = jnp.zeros((nodes + half, nodes), F32)
    for s in range(fan):
        as_row = jnp.where(s < deg_row[...], nbr_t[s : s + 1, :], -1)
        as_col = jnp.where(s < deg_col[...], nbr[:, s : s + 1], -1)
        give_sum += jnp.where(down == as_row, 1.0, 0.0)
        take_sum += jnp.where(side == as_col, 1.0, 0.0)
        by_col += jnp.where(col == as_col, 1.0, 0.0)
        by_row += jnp.where(row == as_row, 1.0, 0.0)

    def lane(rows):
        return lax.broadcasted_iota(jnp.int32, (rows, nodes), 1)

    def sub(cols):
        return lax.broadcasted_iota(jnp.int32, (nodes, cols), 0)

    give[:, :nodes] = give_sum.astype(BF16)
    give[:, nodes:] = jnp.where(lane(span) == two_col[...], 1.0, 0.0).astype(BF16)
    take[:nodes, :] = take_sum.astype(BF16)
    take[nodes:, :] = jnp.where(sub(span) == two_row[...], 1.0, 0.0).astype(BF16)
    own[...] = by_col[:, :nodes].astype(BF16)
    mean[...] = by_col[:, nodes:].astype(BF16)
    own_t[...] = by_row[:nodes].astype(BF16)
    back[...] = by_row[nodes:].astype(BF16)
    pick[...] = jnp.where(lane(half) == send_col[...], 1.0, 0.0).astype(BF16)
    home[...] = jnp.where(sub(half) == send_row[...], 1.0, 0.0).astype(BF16)
    for g in range(flat.shape[0]):
        flat_t[:, g * nodes : (g + 1) * nodes] = flat[g].T


def ring_place(at, turn, offset):
    o, turned = offset
    return (at + CHIPS + o * (turn if turned else 1)) % CHIPS


def places(offsets, other):
    feat = lax.axis_index("feat")
    y, core = feat // 2, feat % 2
    held = 1 - core if other else core
    return [ring_place(y, 1 - 2 * core, o) * 2 + held for o in offsets]


def places_x(offsets):
    core = lax.axis_index("feat") % 2
    x = lax.axis_index("dom") % CHIPS
    return [ring_place(x, 1 - 2 * core, o) for o in offsets]


SUM_MINE = ((2, False), (-1, True), (1, True), (0, False))
SUM_OTHER = ((2, False), (1, True), (-1, True), (0, False))
GET_MINE = ((0, False), (-1, True), (1, True), (2, False))
GET_OTHER = ((0, False), (1, True), (-1, True), (2, False))


def project(flat, w_one, other):
    groups, nodes, cols = flat.shape
    width = w_one.shape[1]
    cut = width // 4

    def body(rows, w, out):
        ids = places(SUM_OTHER if other else SUM_MINE, other)
        picked = jnp.concatenate([rows[g] for g in ids], axis=0)
        out[...] = mm(picked, w[...]).astype(BF16).reshape(out.shape)

    return pl.pallas_call(
        body,
        out_shape=shape((CHIPS, nodes, width)),
        grid=(width // cut,),
        in_specs=[
            pl.BlockSpec(flat.shape, lambda i: (0, 0, 0)),
            pl.BlockSpec((cols, cut), lambda i: (0, i)),
        ],
        out_specs=pl.BlockSpec((CHIPS, nodes, cut), lambda i: (0, 0, i)),
        name="project",
        cost_estimate=pl.CostEstimate(
            flops=2 * CHIPS * nodes * cols * width,
            bytes_accessed=2 * (groups * nodes * cols + 2 * cols * width) + (4 << 20),
            transcendentals=0,
        ),
    )(flat, w_one)


def add(*terms):
    total = terms[0].astype(F32)
    for term in terms[1:]:
        total += term.astype(F32)
    return total


def send_body(mine, got, ahead, behind):
    ahead[...] = add(mine[0], got[0]).astype(BF16)
    behind[...] = add(mine[1], got[1]).astype(BF16)


def relay_body(mine, got, relay, ahead):
    ahead[...] = add(mine[2], got[2], relay[...]).astype(BF16)


def forward_body(part, got, near, far, grads, inv, give, p_self, p_near, boxes):
    width = grads.shape[1]
    total = add(part[3], got[3], near[...], far[...])
    p_self[...] = total[:, :width]
    mine = total[:, width:].astype(BF16)
    p_near[...] = mine
    scaled = (grads[...].astype(F32) * inv[...]).astype(BF16)
    boxes[...] = mm(give[...], jnp.concatenate([scaled, mine], axis=0)).astype(BF16)


def middle_body(
    recv, p_self, p_near, grads, inv, w_two, take, own, own_t, back_t,
    boxes, d_pre_out, term_out, hidden_out, back_out,
):
    nodes, width = grads.shape
    both = mm(take[...], recv[...])
    grad = grads[...]
    scaled = (grad.astype(F32) * inv[...]).astype(BF16)
    pre = p_self[...] + inv[...] * (both[:nodes] + mm(own[...], p_near[...]))
    back = (both[nodes:] + mm(own_t[...], scaled)).astype(BF16)
    back_out[...] = back
    d_hidden = mm(grad, w_two[:width, :], NT) + mm(back, w_two[width:, :], NT)
    sig = jax.nn.sigmoid(pre)
    hidden_out[...] = (pre * sig).astype(BF16)
    d_pre = d_hidden * sig * (1.0 + pre * (1.0 - sig))
    d_pre_out[...] = d_pre.astype(BF16)
    term = (d_pre * inv[...]).astype(BF16)
    term_out[...] = term
    boxes[...] = mm(back_t[...], term).astype(BF16)


def near_body(recv, term, own_t, home, out):
    out[...] = (mm(own_t[...], term[...]) + mm(home[...], recv[...])).astype(BF16)


def out_body(recv, hidden, inv, mean, own, w_two, out):
    width = hidden.shape[1]
    parts, rows, cut = recv.shape
    rows = rows // 3
    got = jnp.concatenate(
        [recv[:, k * rows : (k + 1) * rows, :].reshape(parts * rows, cut) for k in range(2)],
        axis=1,
    )
    agg = (inv[...] * (mm(mean[...], got) + mm(own[...], hidden[...]))).astype(BF16)
    out[...] = (mm(hidden[...], w_two[:width, :]) + mm(agg, w_two[width:, :])).astype(BF16)


def two_body(hidden, grads, back, mine, theirs, scratch):
    width = hidden.shape[1]
    both = jnp.concatenate([grads[...], back[...]], axis=1)
    pair = mm(hidden[...], both, TN)
    half = scratch.shape[0] // 2
    for k in range(2):
        piece = pair[:, k * width : (k + 1) * width]
        scratch[k * half : (k + 1) * half] = piece.reshape(half, -1, width)
    for k, g in enumerate(places(SUM_MINE, False)):
        mine[k] = scratch[g]
    for k, g in enumerate(places(SUM_OTHER, True)):
        theirs[k] = scratch[g].astype(BF16)


def mix_body(mine, got, block, ahead, behind):
    ahead[0] = block[...]
    behind[0] = block[...]
    ahead[1] = add(mine[0], got[0]).astype(BF16)
    behind[1] = add(mine[1], got[1]).astype(BF16)


def pass_body(mine, got, relay, ahead):
    ahead[0] = relay[0]
    ahead[1] = add(mine[2], got[2], relay[1]).astype(BF16)


def pack_body(pick, hidden, mine, got, near, far, out):
    parts, rows, cut = out.shape
    rows = rows // 3
    boxes = mm(pick[...], hidden[...]).astype(BF16)
    for k in range(2):
        piece = boxes[:, k * cut : (k + 1) * cut].reshape(parts, rows, cut)
        out[:, k * rows : (k + 1) * rows, :] = piece
    two = add(mine[3], got[3], near[1], far[1]).astype(BF16)
    half = parts // 2
    for k in range(2):
        piece = two[:, k * cut : (k + 1) * cut].reshape(half, rows, cut)
        out[k * half : (k + 1) * half, 2 * rows :, :] = piece


def two_sum_body(scale, recv, out):
    parts, rows, cut = recv.shape
    out[...] = (add(*[recv[k, 2 * rows // 3 :, :] for k in range(parts)]) * scale).astype(BF16)


def grad_of(flat_t, blocks, other, stack):
    for g, block in zip(places(GET_MINE, False), blocks):
        stack[g] = block
    for k, g in enumerate(places(GET_OTHER, True)):
        stack[g] = other[k]
    groups, nodes, width = stack.shape
    return mm(flat_t[...], stack[...].reshape(groups * nodes, width))


def self_body(flat_t, b0, b1, b2, b3, other, out, stack):
    out[...] = grad_of(flat_t, (b0[...], b1[0], b2[0], b3[0]), other, stack).astype(BF16)


def near_grad_body(
    flat_t, b0, b1, b2, b3, other, first, chunk, ahead, behind, third, own, stack, total
):
    width = first.shape[1]
    total[:, :width] = first[...]
    blocks = (b0[...], b1[...], b2[...], b3[...])
    total[:, width:] = grad_of(flat_t, blocks, other, stack).astype(BF16)
    rows = own.shape[0]
    for x, target in zip(places_x(SUM_MINE), (ahead, behind, third, own)):
        target[:rows, :] = total[pl.ds(pl.multiple_of(x * rows, rows), rows), :]
    for target in (ahead, behind):
        target[rows:, :] = jnp.zeros_like(target[rows:, :])
        target[rows:, : chunk.shape[1]] = chunk[...]


def x_relay_body(third, relay, out):
    rows = third.shape[0]
    out[:rows, :] = add(third[...], relay[:rows, :]).astype(BF16)
    out[rows:, :] = relay[rows:, :]


def x_sum_body(own, relay, near, far, chunk, out):
    rows = own.shape[0]
    parts, deep, _ = out.shape
    cut = chunk.shape[1]
    tail = chunk.shape[0]
    total = add(own[...], near[:rows, :], far[:rows, :]).astype(BF16)
    out[:, : deep - tail, :] = total.reshape(parts, deep - tail, -1)
    held = [chunk[...], relay[rows:, :cut], near[rows:, :cut], far[rows:, :cut]]
    both = jnp.concatenate(held, axis=1)
    out[:, deep - tail :, :] = jnp.broadcast_to(both[None], (parts, *both.shape))


def z_sum_body(scale, recv, out, chunk, scratch):
    parts, deep, _ = recv.shape
    rows = out.shape[1]
    tail = deep - rows
    total = (add(*[recv[k, :rows, :] for k in range(parts)]) * scale).astype(BF16)
    out[...] = jnp.broadcast_to(total[None], out.shape)
    cut = scratch.shape[1] // 2
    half = parts // 2
    for k, x in enumerate(places_x(GET_MINE)):
        for z in range(parts):
            at = pl.multiple_of((z % half * CHIPS + x) * tail, tail)
            side = slice(z // half * cut, (z // half + 1) * cut)
            piece = recv[z, rows:, k * cut : (k + 1) * cut]
            scratch[pl.ds(at, tail), side] = piece.astype(F32)
    chunk[...] = scratch[...].astype(BF16)


def spread_body(b0, b1, b2, b3, out):
    rows = b0.shape[0]
    for x, block in zip(places_x(GET_MINE), (b0, b1, b2, b3)):
        out[pl.ds(pl.multiple_of(x * rows, rows), rows), :] = block[...].astype(F32)


def join_body(b0, b1, b2, b3, other, out):
    nodes = b0.shape[0]

    def put(g, block):
        out[pl.ds(pl.multiple_of(g * nodes, nodes), nodes), :] = block.astype(F32)

    for g, block in zip(places(GET_MINE, False), (b0, b1, b2, b3)):
        put(g, block[...])
    for k, g in enumerate(places(GET_OTHER, True)):
        put(g, other[k])


def on_device(features, w_one, w_two, neighbor, degree, send_rows, grad_out):
    groups, nodes, cols = features.shape
    width = w_two.shape[1]
    parts = lax.axis_size("dom")
    deep = parts // CHIPS
    nbr = neighbor[0]
    deg = degree[0]
    sends = send_rows[0]
    kmax = sends.shape[1]
    half = sends.size
    span = 2 * half
    grads = grad_out[0]
    scale = 1.0 / math.sqrt(groups * nodes * parts)
    y_ahead, y_behind = along_y(1), along_y(-1)
    x_ahead, x_behind = along_x(1, parts, groups), along_x(-1, parts, groups)
    lines = [[z * CHIPS + x for z in range(deep)] for x in range(CHIPS)]

    def forward(block):
        return lax.ppermute(block, "feat", y_ahead)

    def backward(block):
        return lax.ppermute(block, "feat", y_behind)

    def swap(block):
        return lax.ppermute(block, "feat", SWAP)

    def x_forward(block):
        return lax.ppermute(block, ("feat", "dom"), x_ahead)

    def x_backward(block):
        return lax.ppermute(block, ("feat", "dom"), x_behind)

    def gather(block, after=None):
        one = forward(block)
        two = backward(block)
        three = forward(one)
        held = jnp.stack([block, one, two, three])
        if after is not None:
            held, after = lax.optimization_barrier((held, after))
        return (block, one, two, three, swap(held)), after

    got = swap(project(features, w_one, True))
    mine = project(features, w_one, False)

    inv = (1.0 / deg.astype(F32))[:, None]
    blank = jnp.full_like(sends, -1)
    two_col = jnp.concatenate([blank, sends], axis=1).reshape(-1, 1)
    two_row = jnp.concatenate([sends, blank], axis=1).reshape(1, -1)
    give, take, own, own_t, back_t, home, pick, mean, flat_t = whole(
        "tables",
        tables_body,
        (
            shape((span, 2 * nodes)),
            shape((2 * nodes, span)),
            shape((nodes, nodes)),
            shape((nodes, nodes)),
            shape((half, nodes)),
            shape((nodes, half)),
            shape((half, nodes)),
            shape((nodes, half)),
            shape((cols, groups * nodes)),
        ),
        nbr.T, nbr, deg[None, :], deg[:, None], sends.reshape(-1, 1), sends.reshape(1, -1),
        two_col, two_row, features,
    )

    rows = shape((nodes, 2 * width))
    ahead, behind = whole("send", send_body, (rows, rows), mine, got)
    relay = forward(ahead)
    near = backward(behind)
    far = forward(whole("relay", relay_body, rows, mine, got, relay))
    p_self, p_near, boxes = whole(
        "forward",
        forward_body,
        (shape((nodes, width), F32), shape((nodes, width)), shape((span, width))),
        mine, got, near, far, grads, inv, give,
    )
    recv = trade(boxes.reshape(parts, 2 * kmax, width)).reshape(span, width)
    block = shape((nodes, width))
    boxes, d_pre, term, hidden, back = whole(
        "middle",
        middle_body,
        (shape((half, width)), block, block, block, block),
        recv, p_self, p_near, grads, inv, w_two, take, own, own_t, back_t,
    )
    recv = trade(boxes.reshape(parts, kmax, width)).reshape(half, width)

    rows = 2 * width // groups
    mine, theirs = whole(
        "two_sum",
        two_body,
        (shape((CHIPS, rows, width), F32), shape((CHIPS, rows, width))),
        hidden, grads, back,
        scratch=[pltpu.VMEM((groups, rows, width), F32)],
    )
    got = swap(theirs)
    pair = shape((2, nodes, width))
    ahead, behind = whole("mix", mix_body, (pair, pair), mine, got, d_pre)
    relay = forward(ahead)
    near = backward(behind)
    far = forward(whole("pass", pass_body, pair, mine, got, relay))
    other = swap(jnp.stack([d_pre, relay[0], near[0], far[0]]))
    stack = pltpu.VMEM((groups, nodes, width), BF16)
    first = whole(
        "self_grad", self_body, shape((cols, width)), flat_t, d_pre, relay, near, far, other,
        scratch=[stack], flops=2 * groups * nodes * cols * width,
    )
    packed = whole(
        "pack", pack_body, shape((parts, 3 * kmax, width // 2)),
        pick, hidden, mine, got, near, far,
    )

    d_near = whole("near", near_body, block, recv, term, own_t, home)
    gathered, first = gather(d_near, first)
    packed = trade(packed)
    out = whole("out", out_body, block, packed, hidden, inv, mean, own, w_two)
    chunk = whole(
        "two_scale",
        lambda recv, out: two_sum_body(scale, recv, out),
        shape((kmax, width // 2)),
        packed,
    )

    rows = cols // CHIPS
    message = shape((rows + kmax, 2 * width))
    plain = shape((rows, 2 * width))
    ahead, behind, third, mine = whole(
        "near_grad",
        near_grad_body,
        (message, message, plain, plain),
        flat_t, *gathered, first, chunk,
        scratch=[stack, pltpu.VMEM((cols, 2 * width), BF16)],
        flops=2 * groups * nodes * cols * width,
    )
    relay = x_forward(ahead)
    near = x_backward(behind)
    far = x_forward(whole("x_relay", x_relay_body, message, third, relay))
    terms = whole(
        "x_sum",
        x_sum_body,
        shape((deep, rows // deep + kmax, 2 * width)),
        mine, relay, near, far, chunk,
    )
    terms = trade(terms, lines)
    total, chunk = whole(
        "z_sum",
        lambda *refs: z_sum_body(scale, *refs),
        (shape((deep, rows // deep, 2 * width)), block),
        terms,
        scratch=[pltpu.VMEM((nodes, width), F32)],
    )
    total = trade(total, lines).reshape(rows, 2 * width)
    relay = x_forward(total)
    near = x_backward(total)
    far = x_forward(relay)
    two = whole("join", join_body, shape((2 * width, width), F32), *gather(chunk)[0])
    one = whole("spread", spread_body, shape((cols, 2 * width), F32), total, relay, near, far)
    return out[None], one, two


def solution(mesh):
    in_specs = (
        P(None, "dom", "feat"),
        P("feat", None),
        P(),
        P("feat", "dom", None),
        P("feat", "dom"),
        P("feat", "dom", None),
        P("feat", "dom", None),
    )
    out_specs = (P("feat", "dom", None), P("feat", None), P())
    return jax.shard_map(
        on_device, mesh=mesh, in_specs=in_specs, out_specs=out_specs, check_vma=False
    )
```

```python
import math

import jax
import jax.numpy as jnp
from jax import lax
from jax.experimental import pallas as pl
from jax.experimental.pallas import tpu as pltpu
from jax.sharding import PartitionSpec as P

F32 = jnp.float32
BF16 = jnp.bfloat16
CHIPS = 4
NT = (((1,), (1,)), ((), ()))
TN = (((0,), (0,)), ((), ()))


def step(core):
    return 1 if core == 0 else -1


def along_y(sign):
    return [
        (y * 2 + c, (y + sign * step(c)) % CHIPS * 2 + c) for y in range(CHIPS) for c in range(2)
    ]


def along_x(sign, parts, feats):
    def device(f, z, x):
        return f * parts + z * CHIPS + x % CHIPS

    return [
        (device(f, z, x), device(f, z, x + sign * step(f % 2)))
        for f in range(feats)
        for z in range(parts // CHIPS)
        for x in range(CHIPS)
    ]


SWAP = [(i, i ^ 1) for i in range(2 * CHIPS)]


def mm(a, b, dims=(((1,), (0,)), ((), ()))):
    return lax.dot_general(a, b, dims, preferred_element_type=F32)


def whole(name, body, outs, *args, scratch=()):
    return pl.pallas_call(body, out_shape=outs, scratch_shapes=scratch, name=name)(*args)


def shape(dims, kind=BF16):
    return jax.ShapeDtypeStruct(dims, kind)


def trade(boxes, groups=None):
    return lax.all_to_all(
        boxes, "dom", split_axis=0, concat_axis=0, axis_index_groups=groups, tiled=True
    )


def tables_body(nbr_t, deg, sends_t, give, take, own, own_t, inv):
    fan, nodes = nbr_t.shape
    kmax, parts = sends_t.shape
    span = 2 * kmax * parts
    r = lax.broadcasted_iota(jnp.int32, (span, nodes), 0)
    j = r % (2 * kmax)
    entry = nodes + r // (2 * kmax) * kmax + j
    leave = jnp.where(j < kmax, entry, -2)
    arrive = jnp.where(j >= kmax, entry - kmax, -2)
    row = lax.broadcasted_iota(jnp.int32, (nodes, nodes), 0)
    leave_sum = jnp.zeros((span, nodes), F32)
    arrive_sum = jnp.zeros((span, nodes), F32)
    own_sum = jnp.zeros((nodes, nodes), F32)
    for s in range(fan):
        used = jnp.where(s < deg[...], nbr_t[s : s + 1, :], -1)
        leave_sum += jnp.where(leave == used, 1.0, 0.0)
        arrive_sum += jnp.where(arrive == used, 1.0, 0.0)
        own_sum += jnp.where(row == used, 1.0, 0.0)
    own_t[...] = own_sum.astype(BF16)
    own[...] = own_sum.T.astype(BF16)
    part = lax.broadcasted_iota(jnp.int32, (parts, span), 0)
    lane = lax.broadcasted_iota(jnp.int32, (parts, span), 1)
    spread = jnp.where(lane // (2 * kmax) == part, 1.0, 0.0).astype(BF16)
    ids = mm(sends_t[...].astype(F32).astype(BF16), spread)
    slot = lax.broadcasted_iota(jnp.int32, (kmax, span), 0)
    at = lax.broadcasted_iota(jnp.int32, (kmax, span), 1) % (2 * kmax)
    back_id = jnp.sum(jnp.where(slot == at, ids + 1.0, 0.0), axis=0, keepdims=True) - 1.0
    pick_id = jnp.sum(jnp.where(slot + kmax == at, ids + 1.0, 0.0), axis=0, keepdims=True) - 1.0
    node = lax.broadcasted_iota(jnp.int32, (nodes, span), 0).astype(F32)
    home = jnp.where(node == back_id, 1.0, 0.0)
    pick = jnp.where(node == pick_id, 1.0, 0.0)
    give[:, :nodes] = leave_sum.astype(BF16)
    give[:, nodes:] = pick.T.astype(BF16)
    take[:nodes, :] = arrive_sum.T.astype(BF16)
    take[nodes:, :] = home.astype(BF16)
    inv[...] = jnp.broadcast_to(1.0 / deg[...].astype(F32), (nodes, nodes)).T


def turn_body(flat, out):
    groups, nodes, cols = flat.shape
    for g in range(groups):
        out[:, g * nodes : (g + 1) * nodes] = flat[g].T


def ring_place(at, turn, offset):
    o, turned = offset
    return (at + CHIPS + o * (turn if turned else 1)) % CHIPS


def places(offsets, other):
    feat = lax.axis_index("feat")
    y, core = feat // 2, feat % 2
    held = 1 - core if other else core
    return [ring_place(y, 1 - 2 * core, o) * 2 + held for o in offsets]


def places_x(offsets):
    core = lax.axis_index("feat") % 2
    x = lax.axis_index("dom") % CHIPS
    return [ring_place(x, 1 - 2 * core, o) for o in offsets]


SUM_MINE = ((2, False), (-1, True), (1, True), (0, False))
SUM_OTHER = ((2, False), (1, True), (-1, True), (0, False))
GET_MINE = ((0, False), (-1, True), (1, True), (2, False))
GET_OTHER = ((0, False), (1, True), (-1, True), (2, False))


def project(flat, w_one, other):
    groups, nodes, cols = flat.shape

    def body(rows, w, out):
        ids = places(SUM_OTHER if other else SUM_MINE, other)
        picked = jnp.concatenate([rows[g] for g in ids], axis=0)
        out[...] = mm(picked, w[...]).astype(BF16).reshape(out.shape)

    return whole("project", body, shape((CHIPS, nodes, w_one.shape[1])), flat, w_one)


def add(*terms):
    total = terms[0].astype(F32)
    for term in terms[1:]:
        total += term.astype(F32)
    return total


def forward_body(part, got, near, far, grads, inv, give, p_self, p_near, boxes):
    width = grads.shape[1]
    total = add(part[...], got[...], near[...], far[...])
    p_self[...] = total[:, :width]
    mine = total[:, width:].astype(BF16)
    p_near[...] = mine
    scaled = (grads[...].astype(F32) * inv[:, :1]).astype(BF16)
    boxes[...] = mm(give[...], jnp.concatenate([scaled, mine], axis=0)).astype(BF16)


def middle_body(
    recv, p_self, p_near, grads, inv, w_two, give, take, own, own_t,
    boxes, near_local, hidden_out, ahead, behind, third, mine, scratch,
):
    nodes, width = grads.shape
    scales = inv[:, :1]
    both = mm(take[...], recv[...])
    grad = grads[...]
    scaled = (grad.astype(F32) * scales).astype(BF16)
    pre = p_self[...] + scales * (both[:nodes] + mm(own[...], p_near[...]))
    back = (both[nodes:] + mm(own_t[...], scaled)).astype(BF16)
    d_hidden = mm(grad, w_two[:width, :], NT) + mm(back, w_two[width:, :], NT)
    sig = jax.nn.sigmoid(pre)
    hidden = (pre * sig).astype(BF16)
    hidden_out[...] = hidden
    d_pre = d_hidden * sig * (1.0 + pre * (1.0 - sig))
    term = (d_pre * scales).astype(BF16)
    boxes[...] = mm(give[...], jnp.concatenate([term, hidden], axis=0)).astype(BF16)
    near_local[...] = mm(own_t[...], term)
    half = scratch.shape[0] // 2
    for k, right in enumerate((grad, back)):
        piece = mm(hidden, right, TN).astype(BF16)
        scratch[k * half : (k + 1) * half] = piece.reshape(half, -1, width)
    ahead[0] = d_pre.astype(BF16)
    behind[0] = d_pre.astype(BF16)
    for k, other in enumerate((True, False)):
        away, back_to, on_to, here = places(SUM_MINE, other)
        ahead[1 + k] = scratch[away]
        behind[1 + k] = scratch[back_to]
        third[k] = scratch[on_to]
        mine[k] = scratch[here]


def near_body(recv, near_local, take, out):
    nodes = out.shape[0]
    out[...] = (near_local[...] + mm(take[nodes:, :], recv[...])).astype(BF16)


def out_body(recv, hidden, inv, take, own, w_two, out):
    nodes, width = hidden.shape
    total = mm(take[:nodes, :], recv[...]) + mm(own[...], hidden[...])
    agg = (inv[:, :1] * total).astype(BF16)
    out[...] = (mm(hidden[...], w_two[:width, :]) + mm(agg, w_two[width:, :])).astype(BF16)


def grad_of(flat_t, held, other, stack):
    for k, g in enumerate(places(GET_MINE, False)):
        stack[g] = held[k]
    for k, g in enumerate(places(GET_OTHER, True)):
        stack[g] = other[k]
    groups, nodes, width = stack.shape
    return mm(flat_t[...], stack[...].reshape(groups * nodes, width)).astype(BF16)


def self_body(flat_t, held, other, out, stack):
    out[...] = grad_of(flat_t, held, other, stack)


def near_grad_body(
    flat_t, held, other, first, two_mine, two_other, ahead, behind, third, own, stack, boxes
):
    width = first.shape[1]
    chips, deep, rows, cut = boxes.shape
    block = first.shape[0] // chips
    part = block // deep
    sides = (first[...], grad_of(flat_t, held, other, stack))
    two = add(two_mine[...], two_other[...]).astype(BF16)
    tail = rows - 4 * part
    slab = deep * tail
    for x in range(chips):
        for q in range(4):
            at = q % 2 * cut
            piece = sides[q // 2][x * block : (x + 1) * block, at : at + cut]
            boxes[x, :, q * part : (q + 1) * part, :] = piece.reshape(deep, part, cut)
        piece = two[x % 2 * slab : (x % 2 + 1) * slab, x // 2 * cut : (x // 2 + 1) * cut]
        boxes[x, :, 4 * part :, :] = piece.reshape(deep, tail, cut)
    for x, target in zip(places_x(SUM_MINE), (ahead, behind, third, own)):
        target[...] = boxes[x]


def chunk_body(b0, b1, b2, b3, out, scratch):
    deep, rows, cut = b0.shape
    chips, slab, _ = scratch.shape
    tail = slab // deep
    for x, block in zip(places_x(GET_MINE), (b0, b1, b2, b3)):
        scratch[x] = block[:, rows - tail :, :].reshape(slab, cut)
    for x in range(chips):
        at = x % 2 * slab
        out[at : at + slab, x // 2 * cut : (x // 2 + 1) * cut] = scratch[x]


def spread_body(b0, b1, b2, b3, out):
    deep, rows, cut = b0.shape
    block = out.shape[0] // CHIPS
    part = block // deep
    for x, held in zip(places_x(GET_MINE), (b0, b1, b2, b3)):
        at = pl.ds(pl.multiple_of(x * block, block), block)
        for q in range(4):
            piece = held[:, q * part : (q + 1) * part, :].astype(F32)
            out[at, q * cut : (q + 1) * cut] = piece.reshape(block, cut)


def join_body(held, other, out):
    nodes = held.shape[1]

    def put(g, block):
        out[pl.ds(pl.multiple_of(g * nodes, nodes), nodes), :] = block.astype(F32)

    for k, g in enumerate(places(GET_MINE, False)):
        put(g, held[k])
    for k, g in enumerate(places(GET_OTHER, True)):
        put(g, other[k])


def on_device(features, w_one, w_two, neighbor, degree, send_rows, grad_out):
    groups, nodes, cols = features.shape
    width = w_two.shape[1]
    parts = lax.axis_size("dom")
    deep = parts // CHIPS
    sends = send_rows[0]
    kmax = sends.shape[1]
    span = 2 * sends.size
    grads = grad_out[0]
    scale = 1.0 / math.sqrt(groups * nodes * parts)
    y_ahead, y_behind = along_y(1), along_y(-1)
    x_ahead, x_behind = along_x(1, parts, groups), along_x(-1, parts, groups)
    lines = [[z * CHIPS + x for z in range(deep)] for x in range(CHIPS)]

    def forward(block):
        return lax.ppermute(block, "feat", y_ahead)

    def backward(block):
        return lax.ppermute(block, "feat", y_behind)

    def swap(block):
        return lax.ppermute(block, "feat", SWAP)

    def x_forward(block):
        return lax.ppermute(block, ("feat", "dom"), x_ahead)

    def x_backward(block):
        return lax.ppermute(block, ("feat", "dom"), x_behind)

    def gather(block):
        one = forward(block)
        two = backward(block)
        return jnp.stack([block, one, two, forward(one)])

    got = swap(project(features, w_one, True))
    mine = project(features, w_one, False)
    give, take, own, own_t, inv = whole(
        "tables",
        tables_body,
        (
            shape((span, 2 * nodes)),
            shape((2 * nodes, span)),
            shape((nodes, nodes)),
            shape((nodes, nodes)),
            shape((nodes, nodes), F32),
        ),
        neighbor[0].T, degree, sends.T,
    )
    flat_t = whole("turn", turn_body, shape((cols, groups * nodes)), features)
    relay = forward(add(mine[0], got[0]).astype(BF16))
    near = backward(add(mine[1], got[1]).astype(BF16))
    far = forward(add(mine[2], got[2], relay).astype(BF16))
    block = shape((nodes, width))
    p_self, p_near, boxes = whole(
        "forward",
        forward_body,
        (shape((nodes, width), F32), block, shape((span, width))),
        mine[3], got[3], near, far, grads, inv, give,
    )
    recv = trade(boxes.reshape(parts, 2 * kmax, width)).reshape(span, width)
    rows = 2 * width // groups
    boxes, near_local, hidden, ahead, behind, third, mine = whole(
        "middle",
        middle_body,
        (
            shape((span, width)),
            shape((nodes, width), F32),
            block,
            shape((3, rows, width)),
            shape((3, rows, width)),
            shape((2, rows, width)),
            shape((2, rows, width)),
        ),
        recv, p_self, p_near, grads, inv, w_two, give, take, own, own_t,
        scratch=[pltpu.VMEM((groups, rows, width), BF16)],
    )
    recv = trade(boxes.reshape(parts, 2 * kmax, width)).reshape(span, width)

    relay = forward(ahead)
    near = backward(behind)
    far = forward(jnp.concatenate([relay[:1], add(third, relay[1:]).astype(BF16)]))
    sums = add(mine, near[1:], far[1:])
    held = jnp.stack([ahead[0], relay[0], near[0], far[0], sums[0].astype(BF16)])
    other = swap(held)
    stack = pltpu.VMEM((groups, nodes, width), BF16)
    first = whole("self_grad", self_body, shape((cols, width)), flat_t, held, other, scratch=[stack])
    two_mine, two_other = sums[1], other[4]

    d_near = whole("near", near_body, block, recv, near_local, take)
    held, first = lax.optimization_barrier((gather(d_near), first))
    other = swap(held)
    out = whole("out", out_body, block, recv, hidden, inv, take, own, w_two)

    lot = shape((deep, 9 * cols // parts // 2, width // 2))
    ahead, behind, third, mine = whole(
        "near_grad",
        near_grad_body,
        (lot, lot, lot, lot),
        flat_t, held, other, first, two_mine, two_other,
        scratch=[stack, pltpu.VMEM((CHIPS, *lot.shape), BF16)],
    )
    relay = x_forward(ahead)
    near = x_backward(behind)
    far = x_forward(add(third, relay).astype(BF16))
    terms = trade(add(mine, near, far).astype(BF16), lines)
    total = (jnp.sum(terms.astype(F32), axis=0) * scale).astype(BF16)
    total = trade(jnp.broadcast_to(total[None], terms.shape), lines)
    relay = x_forward(total)
    near = x_backward(total)
    lots = (total, relay, near, x_forward(relay))
    slab = 2 * width // groups // 2
    chunk = whole(
        "chunk", chunk_body, block, *lots, scratch=[pltpu.VMEM((CHIPS, slab, width // 2), BF16)]
    )
    held = gather(chunk)
    one = whole("spread", spread_body, shape((cols, 2 * width), F32), *lots)
    two = whole("join", join_body, shape((2 * width, width), F32), held, swap(held))
    return out[None], one, two


def solution(mesh):
    in_specs = (
        P(None, "dom", "feat"),
        P("feat", None),
        P(),
        P("feat", "dom", None),
        P("feat", "dom"),
        P("feat", "dom", None),
        P("feat", "dom", None),
    )
    out_specs = (P("feat", "dom", None), P("feat", None), P())
    return jax.shard_map(
        on_device, mesh=mesh, in_specs=in_specs, out_specs=out_specs, check_vma=False
    )
```

```python
import math

import jax
import jax.numpy as jnp
from jax import lax
from jax.experimental import pallas as pl
from jax.experimental.pallas import tpu as pltpu
from jax.sharding import PartitionSpec as P

F32 = jnp.float32
BF16 = jnp.bfloat16
CHIPS = 4
NT = (((1,), (1,)), ((), ()))
TN = (((0,), (0,)), ((), ()))


def step(core):
    return 1 if core == 0 else -1


def along_y(sign):
    return [
        (y * 2 + c, (y + sign * step(c)) % CHIPS * 2 + c) for y in range(CHIPS) for c in range(2)
    ]


def along_x(sign, parts, feats):
    def device(f, z, x):
        return f * parts + z * CHIPS + x % CHIPS

    return [
        (device(f, z, x), device(f, z, x + sign * step(f % 2)))
        for f in range(feats)
        for z in range(parts // CHIPS)
        for x in range(CHIPS)
    ]


SWAP = [(i, i ^ 1) for i in range(2 * CHIPS)]


def mm(a, b, dims=(((1,), (0,)), ((), ()))):
    return lax.dot_general(a, b, dims, preferred_element_type=F32)


def whole(name, body, outs, *args, scratch=()):
    return pl.pallas_call(body, out_shape=outs, scratch_shapes=scratch, name=name)(*args)


def shape(dims, kind=BF16):
    return jax.ShapeDtypeStruct(dims, kind)


def trade(boxes, groups=None):
    return lax.all_to_all(
        boxes, "dom", split_axis=0, concat_axis=0, axis_index_groups=groups, tiled=True
    )


def tables_body(nbr_t, deg, sends_t, give, take, own, own_t, inv):
    fan, nodes = nbr_t.shape
    kmax, parts = sends_t.shape
    span = 2 * kmax * parts
    r = lax.broadcasted_iota(jnp.int32, (span, nodes), 0)
    j = r % (2 * kmax)
    entry = nodes + r // (2 * kmax) * kmax + j
    leave = jnp.where(j < kmax, entry, -2)
    arrive = jnp.where(j >= kmax, entry - kmax, -2)
    row = lax.broadcasted_iota(jnp.int32, (nodes, nodes), 0)
    leave_sum = jnp.zeros((span, nodes), F32)
    arrive_sum = jnp.zeros((span, nodes), F32)
    own_sum = jnp.zeros((nodes, nodes), F32)
    for s in range(fan):
        used = jnp.where(s < deg[...], nbr_t[s : s + 1, :], -1)
        leave_sum += jnp.where(leave == used, 1.0, 0.0)
        arrive_sum += jnp.where(arrive == used, 1.0, 0.0)
        own_sum += jnp.where(row == used, 1.0, 0.0)
    own_t[...] = own_sum.astype(BF16)
    own[...] = own_sum.T.astype(BF16)
    part = lax.broadcasted_iota(jnp.int32, (parts, span), 0)
    lane = lax.broadcasted_iota(jnp.int32, (parts, span), 1)
    spread = jnp.where(lane // (2 * kmax) == part, 1.0, 0.0).astype(BF16)
    ids = mm(sends_t[...].astype(F32).astype(BF16), spread)
    slot = lax.broadcasted_iota(jnp.int32, (kmax, span), 0)
    at = lax.broadcasted_iota(jnp.int32, (kmax, span), 1) % (2 * kmax)
    back_id = jnp.sum(jnp.where(slot == at, ids + 1.0, 0.0), axis=0, keepdims=True) - 1.0
    pick_id = jnp.sum(jnp.where(slot + kmax == at, ids + 1.0, 0.0), axis=0, keepdims=True) - 1.0
    node = lax.broadcasted_iota(jnp.int32, (nodes, span), 0).astype(F32)
    home = jnp.where(node == back_id, 1.0, 0.0)
    pick = jnp.where(node == pick_id, 1.0, 0.0)
    give[:, :nodes] = leave_sum.astype(BF16)
    give[:, nodes:] = pick.T.astype(BF16)
    take[:nodes, :] = arrive_sum.T.astype(BF16)
    take[nodes:, :] = home.astype(BF16)
    inv[...] = jnp.broadcast_to(1.0 / deg[...].astype(F32), (nodes, nodes)).T


def turn_body(flat, out):
    groups, nodes, cols = flat.shape
    for g in range(groups):
        out[:, g * nodes : (g + 1) * nodes] = flat[g].T


def ring_place(at, turn, offset):
    o, turned = offset
    return (at + CHIPS + o * (turn if turned else 1)) % CHIPS


def places(offsets, other):
    feat = lax.axis_index("feat")
    y, core = feat // 2, feat % 2
    held = 1 - core if other else core
    return [ring_place(y, 1 - 2 * core, o) * 2 + held for o in offsets]


def places_x(offsets):
    core = lax.axis_index("feat") % 2
    x = lax.axis_index("dom") % CHIPS
    return [ring_place(x, 1 - 2 * core, o) for o in offsets]


SUM_MINE = ((2, False), (-1, True), (1, True), (0, False))
SUM_OTHER = ((2, False), (1, True), (-1, True), (0, False))
GET_MINE = ((0, False), (-1, True), (1, True), (2, False))
GET_OTHER = ((0, False), (1, True), (-1, True), (2, False))


def project(flat, w_one, other):
    groups, nodes, cols = flat.shape

    def body(rows, w, out):
        ids = places(SUM_OTHER if other else SUM_MINE, other)
        picked = jnp.concatenate([rows[g] for g in ids], axis=0)
        out[...] = mm(picked, w[...]).astype(BF16).reshape(out.shape)

    return whole("project", body, shape((CHIPS, nodes, w_one.shape[1])), flat, w_one)


def add(*terms):
    total = terms[0].astype(F32)
    for term in terms[1:]:
        total += term.astype(F32)
    return total


def forward_body(part, got, near, far, grads, inv, give, p_self, p_near, boxes):
    width = grads.shape[1]
    total = add(part[0], got[0], near[...], far[...])
    p_self[...] = total[:, :width]
    mine = total[:, width:].astype(BF16)
    p_near[...] = mine
    scaled = (grads[...].astype(F32) * inv[:, :1]).astype(BF16)
    boxes[...] = mm(give[...], jnp.concatenate([scaled, mine], axis=0)).astype(BF16)


def middle_body(
    recv, p_self, p_near, grads, inv, w_two, give, take, own, own_t,
    boxes, near_local, hidden_out, ahead, behind, third, mine, scratch,
):
    nodes, width = grads.shape
    scales = inv[:, :1]
    both = mm(take[...], recv[...])
    grad = grads[...]
    scaled = (grad.astype(F32) * scales).astype(BF16)
    pre = p_self[...] + scales * (both[:nodes] + mm(own[...], p_near[...]))
    back = (both[nodes:] + mm(own_t[...], scaled)).astype(BF16)
    d_hidden = mm(grad, w_two[:width, :], NT) + mm(back, w_two[width:, :], NT)
    sig = jax.nn.sigmoid(pre)
    hidden = (pre * sig).astype(BF16)
    hidden_out[...] = hidden
    d_pre = d_hidden * sig * (1.0 + pre * (1.0 - sig))
    term = (d_pre * scales).astype(BF16)
    boxes[...] = mm(give[...], jnp.concatenate([term, hidden], axis=0)).astype(BF16)
    near_local[...] = mm(own_t[...], term)
    half = scratch.shape[0] // 2
    for k, right in enumerate((grad, back)):
        piece = mm(hidden, right, TN).astype(BF16)
        scratch[k * half : (k + 1) * half] = piece.reshape(half, -1, width)
    ahead[0] = d_pre.astype(BF16)
    behind[0] = d_pre.astype(BF16)
    for k, other in enumerate((True, False)):
        away, back_to, on_to, here = places(SUM_MINE, other)
        ahead[1 + k] = scratch[away]
        behind[1 + k] = scratch[back_to]
        third[k] = scratch[on_to]
        mine[k] = scratch[here]


def near_body(recv, near_local, take, out):
    nodes = out.shape[0]
    out[...] = (near_local[...] + mm(take[nodes:, :], recv[...])).astype(BF16)


def out_body(recv, hidden, inv, take, own, w_two, out):
    nodes, width = hidden.shape
    total = mm(take[:nodes, :], recv[...]) + mm(own[...], hidden[...])
    agg = (inv[:, :1] * total).astype(BF16)
    out[...] = (mm(hidden[...], w_two[:width, :]) + mm(agg, w_two[width:, :])).astype(BF16)


def grad_body(flat_t, held, other, two, ahead, behind, third, own, stack, boxes):
    groups, nodes, both = stack.shape
    width = both // 2
    chips, deep, rows, cut = boxes.shape
    block = flat_t.shape[0] // chips
    part = block // deep
    ids = places(GET_MINE, False) + places(GET_OTHER, True)
    for k, g in enumerate(ids):
        source = held if k < chips else other
        stack[g, :, :width] = source[k % chips]
        stack[g, :, width:] = source[chips + k % chips]
    total = mm(flat_t[...], stack[...].reshape(groups * nodes, both)).astype(BF16)
    twos = add(two[...], other[2 * chips]).astype(BF16)
    tail = rows - 4 * part
    slab = deep * tail
    for x in range(chips):
        for q in range(4):
            piece = total[x * block : (x + 1) * block, q * cut : (q + 1) * cut]
            boxes[x, :, q * part : (q + 1) * part, :] = piece.reshape(deep, part, cut)
        piece = twos[x % 2 * slab : (x % 2 + 1) * slab, x // 2 * cut : (x // 2 + 1) * cut]
        boxes[x, :, 4 * part :, :] = piece.reshape(deep, tail, cut)
    for x, target in zip(places_x(SUM_MINE), (ahead, behind, third, own)):
        target[...] = boxes[x]


def chunk_body(b0, b1, b2, b3, out, scratch):
    deep, tail, cut = b0.shape
    chips, slab, _ = scratch.shape
    for x, block in zip(places_x(GET_MINE), (b0, b1, b2, b3)):
        scratch[x] = block[...].reshape(slab, cut)
    for x in range(chips):
        at = x % 2 * slab
        out[at : at + slab, x // 2 * cut : (x // 2 + 1) * cut] = scratch[x]


def spread_body(b0, b1, b2, b3, out):
    deep, rows, cut = b0.shape
    block = out.shape[0] // CHIPS
    part = block // deep
    for x, held in zip(places_x(GET_MINE), (b0, b1, b2, b3)):
        at = pl.ds(pl.multiple_of(x * block, block), block)
        for q in range(4):
            piece = held[:, q * part : (q + 1) * part, :].astype(F32)
            out[at, q * cut : (q + 1) * cut] = piece.reshape(block, cut)


def join_body(held, other, out):
    nodes = held.shape[1]

    def put(g, block):
        out[pl.ds(pl.multiple_of(g * nodes, nodes), nodes), :] = block.astype(F32)

    for k, g in enumerate(places(GET_MINE, False)):
        put(g, held[k])
    for k, g in enumerate(places(GET_OTHER, True)):
        put(g, other[k])


def on_device(features, w_one, w_two, neighbor, degree, send_rows, grad_out):
    groups, nodes, cols = features.shape
    width = w_two.shape[1]
    parts = lax.axis_size("dom")
    deep = parts // CHIPS
    sends = send_rows[0]
    kmax = sends.shape[1]
    span = 2 * sends.size
    grads = grad_out[0]
    scale = 1.0 / math.sqrt(groups * nodes * parts)
    y_ahead, y_behind = along_y(1), along_y(-1)
    x_ahead, x_behind = along_x(1, parts, groups), along_x(-1, parts, groups)
    lines = [[z * CHIPS + x for z in range(deep)] for x in range(CHIPS)]

    def forward(block):
        return lax.ppermute(block, "feat", y_ahead)

    def backward(block):
        return lax.ppermute(block, "feat", y_behind)

    def swap(block):
        return lax.ppermute(block, "feat", SWAP)

    def x_forward(block):
        return lax.ppermute(block, ("feat", "dom"), x_ahead)

    def x_backward(block):
        return lax.ppermute(block, ("feat", "dom"), x_behind)

    def gather(block):
        one = forward(block)
        two = backward(block)
        return jnp.stack([block, one, two, forward(one)])

    got = swap(project(features, w_one, True))
    mine = project(features, w_one, False)
    give, take, own, own_t, inv = whole(
        "tables",
        tables_body,
        (
            shape((span, 2 * nodes)),
            shape((2 * nodes, span)),
            shape((nodes, nodes)),
            shape((nodes, nodes)),
            shape((nodes, nodes), F32),
        ),
        neighbor[0].T, degree, sends.T,
    )
    flat_t = whole("turn", turn_body, shape((cols, groups * nodes)), features)
    relay = forward(add(mine[0], got[0]).astype(BF16))
    near = backward(add(mine[1], got[1]).astype(BF16))
    relay, give = lax.optimization_barrier((relay, give))
    far = forward(add(mine[2], got[2], relay).astype(BF16))
    far, flat_t = lax.optimization_barrier((far, flat_t))
    block = shape((nodes, width))

    def full(*dims):
        return pl.BlockSpec(dims, lambda i: (0,) * len(dims))

    last = pl.BlockSpec((1, nodes, 2 * width), lambda i: (CHIPS - 1, 0, 0))
    p_self, p_near, boxes = pl.pallas_call(
        forward_body,
        out_shape=(shape((nodes, width), F32), block, shape((span, width))),
        grid=(1,),
        in_specs=[
            last, last, full(nodes, 2 * width), full(nodes, 2 * width), full(nodes, width),
            full(nodes, nodes), full(span, 2 * nodes),
        ],
        out_specs=(full(nodes, width), full(nodes, width), full(span, width)),
        name="forward",
    )(mine, got, near, far, grads, inv, give)
    recv = trade(boxes.reshape(parts, 2 * kmax, width)).reshape(span, width)
    rows = 2 * width // groups
    boxes, near_local, hidden, ahead, behind, third, mine = whole(
        "middle",
        middle_body,
        (
            shape((span, width)),
            shape((nodes, width), F32),
            block,
            shape((3, rows, width)),
            shape((3, rows, width)),
            shape((2, rows, width)),
            shape((2, rows, width)),
        ),
        recv, p_self, p_near, grads, inv, w_two, give, take, own, own_t,
        scratch=[pltpu.VMEM((groups, rows, width), BF16)],
    )
    recv = trade(boxes.reshape(parts, 2 * kmax, width)).reshape(span, width)

    relay = forward(ahead)
    near = backward(behind)
    passed = add(third, relay[1:]).astype(BF16)
    d_near = whole("near", near_body, block, recv, near_local, take)
    message = jnp.concatenate([d_near[None], relay[:1], passed])
    far = forward(message)
    back = backward(d_near)
    last = forward(far[0])
    sums = add(mine, near[1:], far[2:])
    held = jnp.stack(
        [ahead[0], relay[0], near[0], far[1], d_near, far[0], back, last, sums[0].astype(BF16)]
    )
    other = swap(held)

    lot = shape((deep, 9 * cols // parts // 2, width // 2))
    ahead, behind, third, mine = whole(
        "grad",
        grad_body,
        (lot, lot, lot, lot),
        flat_t, held, other, sums[1],
        scratch=[
            pltpu.VMEM((groups, nodes, 2 * width), BF16),
            pltpu.VMEM((CHIPS, *lot.shape), BF16),
        ],
    )
    out = whole("out", out_body, block, recv, hidden, inv, take, own, w_two)
    relay = x_forward(ahead)
    near = x_backward(behind)
    far = x_forward(add(third, relay).astype(BF16))
    far, out = lax.optimization_barrier((far, out))
    terms = trade(add(mine, near, far).astype(BF16), lines)
    total = (jnp.sum(terms.astype(F32), axis=0) * scale).astype(BF16)
    total = trade(jnp.broadcast_to(total[None], terms.shape), lines)

    def x_gather(lot):
        one = x_forward(lot)
        return lot, one, x_backward(lot), x_forward(one)

    slab = 2 * width // groups // 2
    twos = x_gather(total[:, 8 * lot.shape[1] // 9 :, :])
    ones = x_gather(total)
    chunk = whole(
        "chunk", chunk_body, block, *twos, scratch=[pltpu.VMEM((CHIPS, slab, width // 2), BF16)]
    )
    held = gather(chunk)
    one = whole("spread", spread_body, shape((cols, 2 * width), F32), *ones)
    held, one = lax.optimization_barrier((held, one))
    two = whole("join", join_body, shape((2 * width, width), F32), held, swap(held))
    return out[None], one, two


def solution(mesh):
    in_specs = (
        P(None, "dom", "feat"),
        P("feat", None),
        P(),
        P("feat", "dom", None),
        P("feat", "dom"),
        P("feat", "dom", None),
        P("feat", "dom", None),
    )
    out_specs = (P("feat", "dom", None), P("feat", None), P())
    return jax.shard_map(
        on_device, mesh=mesh, in_specs=in_specs, out_specs=out_specs, check_vma=False
    )
```

```python
import math

import jax
import jax.numpy as jnp
from jax import lax
from jax.experimental import pallas as pl
from jax.experimental.pallas import tpu as pltpu
from jax.sharding import PartitionSpec as P

F32 = jnp.float32
BF16 = jnp.bfloat16
CHIPS = 4
NT = (((1,), (1,)), ((), ()))
TN = (((0,), (0,)), ((), ()))


def step(core):
    return 1 if core == 0 else -1


def along_y(sign):
    return [
        (y * 2 + c, (y + sign * step(c)) % CHIPS * 2 + c) for y in range(CHIPS) for c in range(2)
    ]


def along_x(sign, parts, feats):
    def device(f, z, x):
        return f * parts + z * CHIPS + x % CHIPS

    return [
        (device(f, z, x), device(f, z, x + sign * step(f % 2)))
        for f in range(feats)
        for z in range(parts // CHIPS)
        for x in range(CHIPS)
    ]


SWAP = [(i, i ^ 1) for i in range(2 * CHIPS)]


def mm(a, b, dims=(((1,), (0,)), ((), ()))):
    return lax.dot_general(a, b, dims, preferred_element_type=F32)


def whole(name, body, outs, *args, scratch=()):
    return pl.pallas_call(body, out_shape=outs, scratch_shapes=scratch, name=name)(*args)


def shape(dims, kind=BF16):
    return jax.ShapeDtypeStruct(dims, kind)


def trade(boxes, groups=None):
    return lax.all_to_all(
        boxes, "dom", split_axis=0, concat_axis=0, axis_index_groups=groups, tiled=True
    )


def tables_body(nbr_t, deg, sends_t, give, take, own, own_t, inv):
    fan, nodes = nbr_t.shape
    kmax, parts = sends_t.shape
    span = 2 * kmax * parts
    r = lax.broadcasted_iota(jnp.int32, (span, nodes), 0)
    j = r % (2 * kmax)
    entry = nodes + r // (2 * kmax) * kmax + j
    leave = jnp.where(j < kmax, entry, -2)
    arrive = jnp.where(j >= kmax, entry - kmax, -2)
    row = lax.broadcasted_iota(jnp.int32, (nodes, nodes), 0)
    leave_sum = jnp.zeros((span, nodes), F32)
    arrive_sum = jnp.zeros((span, nodes), F32)
    own_sum = jnp.zeros((nodes, nodes), F32)
    for s in range(fan):
        used = jnp.where(s < deg[...], nbr_t[s : s + 1, :], -1)
        leave_sum += jnp.where(leave == used, 1.0, 0.0)
        arrive_sum += jnp.where(arrive == used, 1.0, 0.0)
        own_sum += jnp.where(row == used, 1.0, 0.0)
    own_t[...] = own_sum.astype(BF16)
    own[...] = own_sum.T.astype(BF16)
    part = lax.broadcasted_iota(jnp.int32, (parts, span), 0)
    lane = lax.broadcasted_iota(jnp.int32, (parts, span), 1)
    spread = jnp.where(lane // (2 * kmax) == part, 1.0, 0.0).astype(BF16)
    ids = mm(sends_t[...].astype(F32).astype(BF16), spread)
    slot = lax.broadcasted_iota(jnp.int32, (kmax, span), 0)
    at = lax.broadcasted_iota(jnp.int32, (kmax, span), 1) % (2 * kmax)
    back_id = jnp.sum(jnp.where(slot == at, ids + 1.0, 0.0), axis=0, keepdims=True) - 1.0
    pick_id = jnp.sum(jnp.where(slot + kmax == at, ids + 1.0, 0.0), axis=0, keepdims=True) - 1.0
    node = lax.broadcasted_iota(jnp.int32, (nodes, span), 0).astype(F32)
    home = jnp.where(node == back_id, 1.0, 0.0)
    pick = jnp.where(node == pick_id, 1.0, 0.0)
    give[:, :nodes] = leave_sum.astype(BF16)
    give[:, nodes:] = pick.T.astype(BF16)
    take[:nodes, :] = arrive_sum.T.astype(BF16)
    take[nodes:, :] = home.astype(BF16)
    inv[...] = jnp.broadcast_to(1.0 / deg[...].astype(F32), (nodes, nodes)).T


def turn_body(flat, out):
    groups, nodes, cols = flat.shape
    for g in range(groups):
        out[:, g * nodes : (g + 1) * nodes] = flat[g].T


def ring_place(at, turn, offset):
    o, turned = offset
    return (at + CHIPS + o * (turn if turned else 1)) % CHIPS


def places(offsets, other):
    feat = lax.axis_index("feat")
    y, core = feat // 2, feat % 2
    held = 1 - core if other else core
    return [ring_place(y, 1 - 2 * core, o) * 2 + held for o in offsets]


def places_x(offsets):
    core = lax.axis_index("feat") % 2
    x = lax.axis_index("dom") % CHIPS
    return [ring_place(x, 1 - 2 * core, o) for o in offsets]


SUM_MINE = ((2, False), (-1, True), (1, True), (0, False))
SUM_OTHER = ((2, False), (1, True), (-1, True), (0, False))
GET_MINE = ((0, False), (-1, True), (1, True), (2, False))
GET_OTHER = ((0, False), (1, True), (-1, True), (2, False))


def project(flat, w_one, other):
    groups, nodes, cols = flat.shape

    def body(rows, w, out):
        ids = places(SUM_OTHER if other else SUM_MINE, other)
        picked = jnp.concatenate([rows[g] for g in ids], axis=0)
        out[...] = mm(picked, w[...]).astype(BF16).reshape(out.shape)

    return whole("project", body, shape((CHIPS, nodes, w_one.shape[1])), flat, w_one)


def add(*terms):
    total = terms[0].astype(F32)
    for term in terms[1:]:
        total += term.astype(F32)
    return total


def forward_body(part, got, near, far, grads, inv, give, p_self, p_near, boxes, mark):
    width = grads.shape[1]
    total = add(part[0], got[0], near[...], far[...])
    p_self[...] = total[:, :width]
    mark[...] = total[:8, :128]
    mine = total[:, width:].astype(BF16)
    p_near[...] = mine
    scaled = (grads[...].astype(F32) * inv[:, :1]).astype(BF16)
    boxes[...] = mm(give[...], jnp.concatenate([scaled, mine], axis=0)).astype(BF16)


def middle_body(
    recv, p_self, p_near, grads, inv, w_two, give, take, own, own_t, mark,
    boxes, near_local, hidden_out, ahead, behind, third, mine, scratch,
):
    nodes, width = grads.shape
    scales = inv[:, :1]
    both = mm(take[...], recv[...])
    grad = grads[...]
    scaled = (grad.astype(F32) * scales).astype(BF16)
    pre = p_self[...] + scales * (both[:nodes] + mm(own[...], p_near[...]))
    back = (both[nodes:] + mm(own_t[...], scaled)).astype(BF16)
    d_hidden = mm(grad, w_two[:width, :], NT) + mm(back, w_two[width:, :], NT)
    sig = jax.nn.sigmoid(pre)
    hidden = (pre * sig).astype(BF16)
    hidden_out[...] = hidden
    d_pre = d_hidden * sig * (1.0 + pre * (1.0 - sig))
    term = (d_pre * scales).astype(BF16)
    boxes[...] = mm(give[...], jnp.concatenate([term, hidden], axis=0)).astype(BF16)
    near_local[...] = mm(own_t[...], term)
    half = scratch.shape[0] // 2
    for k, right in enumerate((grad, back)):
        piece = mm(hidden, right, TN).astype(BF16)
        scratch[k * half : (k + 1) * half] = piece.reshape(half, -1, width)
    ahead[0] = d_pre.astype(BF16)
    behind[0] = d_pre.astype(BF16)
    for k, other in enumerate((True, False)):
        away, back_to, on_to, here = places(SUM_MINE, other)
        ahead[1 + k] = scratch[away]
        behind[1 + k] = scratch[back_to]
        third[k] = scratch[on_to]
        mine[k] = scratch[here]


def near_body(recv, near_local, take, out):
    nodes = out.shape[0]
    out[...] = (near_local[...] + mm(take[nodes:, :], recv[...])).astype(BF16)


def out_body(recv, hidden, inv, take, own, w_two, out):
    nodes, width = hidden.shape
    total = mm(take[:nodes, :], recv[...]) + mm(own[...], hidden[...])
    agg = (inv[:, :1] * total).astype(BF16)
    out[...] = (mm(hidden[...], w_two[:width, :]) + mm(agg, w_two[width:, :])).astype(BF16)


def grad_body(flat_t, held, other, two, ahead, behind, third, own, stack, boxes):
    groups, nodes, both = stack.shape
    width = both // 2
    chips, deep, rows, cut = boxes.shape
    block = flat_t.shape[0] // chips
    part = block // deep
    ids = places(GET_MINE, False) + places(GET_OTHER, True)
    for k, g in enumerate(ids):
        source = held if k < chips else other
        stack[g, :, :width] = source[k % chips]
        stack[g, :, width:] = source[chips + k % chips]
    total = mm(flat_t[...], stack[...].reshape(groups * nodes, both)).astype(BF16)
    for x in range(chips):
        for q in range(4):
            piece = total[x * block : (x + 1) * block, q * cut : (q + 1) * cut]
            boxes[x, :, q * part : (q + 1) * part, :] = piece.reshape(deep, part, cut)
    for x, target in zip(places_x(SUM_MINE), (ahead, behind, third, own)):
        target[:, :rows, :] = boxes[x]
    twos = add(two[...], other[2 * chips]).astype(BF16)
    tail = (ahead.shape[1] - rows) // 2
    for k in range(2):
        piece = twos[:, k * cut : (k + 1) * cut].reshape(deep, tail, cut)
        for target in (ahead, behind, own):
            target[:, rows + k * tail : rows + (k + 1) * tail, :] = piece
    third[:, rows:, :] = jnp.zeros_like(third[:, rows:, :])


def spread_body(b0, b1, b2, b3, out):
    deep, rows, cut = b0.shape
    block = out.shape[0] // CHIPS
    part = block // deep
    for x, held in zip(places_x(GET_MINE), (b0, b1, b2, b3)):
        at = pl.ds(pl.multiple_of(x * block, block), block)
        for q in range(4):
            piece = held[:, q * part : (q + 1) * part, :].astype(F32)
            out[at, q * cut : (q + 1) * cut] = piece.reshape(block, cut)


def join_body(held, other, out):
    nodes = held.shape[1]

    def put(g, block):
        out[pl.ds(pl.multiple_of(g * nodes, nodes), nodes), :] = block.astype(F32)

    for k, g in enumerate(places(GET_MINE, False)):
        put(g, held[k])
    for k, g in enumerate(places(GET_OTHER, True)):
        put(g, other[k])


def on_device(features, w_one, w_two, neighbor, degree, send_rows, grad_out):
    groups, nodes, cols = features.shape
    width = w_two.shape[1]
    parts = lax.axis_size("dom")
    deep = parts // CHIPS
    sends = send_rows[0]
    kmax = sends.shape[1]
    span = 2 * sends.size
    grads = grad_out[0]
    scale = 1.0 / math.sqrt(groups * nodes * parts)
    y_ahead, y_behind = along_y(1), along_y(-1)
    x_ahead, x_behind = along_x(1, parts, groups), along_x(-1, parts, groups)
    lines = [[z * CHIPS + x for z in range(deep)] for x in range(CHIPS)]

    def forward(block):
        return lax.ppermute(block, "feat", y_ahead)

    def backward(block):
        return lax.ppermute(block, "feat", y_behind)

    def swap(block):
        return lax.ppermute(block, "feat", SWAP)

    def x_forward(block):
        return lax.ppermute(block, ("feat", "dom"), x_ahead)

    def x_backward(block):
        return lax.ppermute(block, ("feat", "dom"), x_behind)

    def gather(block):
        one = forward(block)
        two = backward(block)
        return jnp.stack([block, one, two, forward(one)])

    got = swap(project(features, w_one, True))
    mine = project(features, w_one, False)
    give, take, own, own_t, inv = whole(
        "tables",
        tables_body,
        (
            shape((span, 2 * nodes)),
            shape((2 * nodes, span)),
            shape((nodes, nodes)),
            shape((nodes, nodes)),
            shape((nodes, nodes), F32),
        ),
        neighbor[0].T, degree, sends.T,
    )
    flat_t = whole("turn", turn_body, shape((cols, groups * nodes)), features)
    relay = forward(add(mine[0], got[0]).astype(BF16))
    near = backward(add(mine[1], got[1]).astype(BF16))
    relay, give = lax.optimization_barrier((relay, give))
    far = forward(add(mine[2], got[2], relay).astype(BF16))
    far, flat_t = lax.optimization_barrier((far, flat_t))
    block = shape((nodes, width))

    def full(*dims):
        return pl.BlockSpec(dims, lambda i: (0,) * len(dims))

    last = pl.BlockSpec((1, nodes, 2 * width), lambda i: (CHIPS - 1, 0, 0))
    p_self, p_near, boxes, mark = pl.pallas_call(
        forward_body,
        out_shape=(
            shape((nodes, width), F32), block, shape((span, width)), shape((8, 128), F32)
        ),
        grid=(1,),
        in_specs=[
            last, last, full(nodes, 2 * width), full(nodes, 2 * width), full(nodes, width),
            full(nodes, nodes), full(span, 2 * nodes),
        ],
        out_specs=(full(nodes, width), full(nodes, width), full(span, width), full(8, 128)),
        name="forward",
    )(mine, got, near, far, grads, inv, give)
    boxes, mark = lax.optimization_barrier((boxes, swap(mark)))
    recv = trade(boxes.reshape(parts, 2 * kmax, width)).reshape(span, width)
    rows = 2 * width // groups
    boxes, near_local, hidden, ahead, behind, third, mine = whole(
        "middle",
        middle_body,
        (
            shape((span, width)),
            shape((nodes, width), F32),
            block,
            shape((3, rows, width)),
            shape((3, rows, width)),
            shape((2, rows, width)),
            shape((2, rows, width)),
        ),
        recv, p_self, p_near, grads, inv, w_two, give, take, own, own_t, mark,
        scratch=[pltpu.VMEM((groups, rows, width), BF16)],
    )
    recv = trade(boxes.reshape(parts, 2 * kmax, width)).reshape(span, width)

    relay = forward(ahead)
    near = backward(behind)
    message = jnp.concatenate([relay[:1], add(third, relay[1:]).astype(BF16)])
    message, recv = lax.optimization_barrier((message, recv))
    d_near = whole("near", near_body, block, recv, near_local, take)
    one = forward(d_near)
    two = backward(d_near)
    far = forward(message)
    sums = add(mine, near[1:], far[1:])
    held = jnp.stack(
        [ahead[0], relay[0], near[0], far[0], d_near, one, two, forward(one), sums[0].astype(BF16)]
    )
    other = swap(held)

    kept = 8 * cols // parts // 2
    lot = shape((deep, kept + 4 * width // groups // deep, width // 2))
    ahead, behind, third, mine = whole(
        "grad",
        grad_body,
        (lot, lot, lot, lot),
        flat_t, held, other, sums[1],
        scratch=[
            pltpu.VMEM((groups, nodes, 2 * width), BF16),
            pltpu.VMEM((CHIPS, deep, kept, width // 2), BF16),
        ],
    )
    out = whole("out", out_body, block, recv, hidden, inv, take, own, w_two)
    relay = x_forward(ahead)
    near = x_backward(behind)
    far = x_forward(add(third, relay).astype(BF16))
    far, out = lax.optimization_barrier((far, out))
    last_rows = lax.broadcasted_iota(jnp.int32, lot.shape, 1) >= kept
    terms = add(mine, near, far) + jnp.where(last_rows, relay.astype(F32), 0.0)
    terms = trade(terms.astype(BF16), lines)
    total = (jnp.sum(terms.astype(F32), axis=0) * scale).astype(BF16)
    total = trade(jnp.broadcast_to(total[None], terms.shape), lines)
    tail = (lot.shape[1] - kept) // 2
    chunk = jnp.concatenate(
        [
            total[:, kept : kept + tail].reshape(deep * tail, -1),
            total[:, kept + tail :].reshape(deep * tail, -1),
        ],
        axis=1,
    )
    mine = total[:, :kept]
    relay = x_forward(mine)
    near = x_backward(mine)
    held, relay = lax.optimization_barrier((gather(chunk), relay))
    far = x_forward(relay)
    one = whole("spread", spread_body, shape((cols, 2 * width), F32), mine, relay, near, far)
    two = whole("join", join_body, shape((2 * width, width), F32), held, swap(held))
    return out[None], one, two


def solution(mesh):
    in_specs = (
        P(None, "dom", "feat"),
        P("feat", None),
        P(),
        P("feat", "dom", None),
        P("feat", "dom"),
        P("feat", "dom", None),
        P("feat", "dom", None),
    )
    out_specs = (P("feat", "dom", None), P("feat", None), P())
    return jax.shard_map(
        on_device, mesh=mesh, in_specs=in_specs, out_specs=out_specs, check_vma=False
    )
```

```python
import math

import jax
import jax.numpy as jnp
from jax import lax
from jax.experimental import pallas as pl
from jax.experimental.pallas import tpu as pltpu
from jax.sharding import PartitionSpec as P

F32 = jnp.float32
BF16 = jnp.bfloat16
CHIPS = 4
NT = (((1,), (1,)), ((), ()))
TN = (((0,), (0,)), ((), ()))


def step(core):
    return 1 if core == 0 else -1


def along_y(sign):
    return [
        (y * 2 + c, (y + sign * step(c)) % CHIPS * 2 + c) for y in range(CHIPS) for c in range(2)
    ]


def along_x(sign, parts, feats):
    def device(f, z, x):
        return f * parts + z * CHIPS + x % CHIPS

    return [
        (device(f, z, x), device(f, z, x + sign * step(f % 2)))
        for f in range(feats)
        for z in range(parts // CHIPS)
        for x in range(CHIPS)
    ]


SWAP = [(i, i ^ 1) for i in range(2 * CHIPS)]


def mm(a, b, dims=(((1,), (0,)), ((), ()))):
    return lax.dot_general(a, b, dims, preferred_element_type=F32)


def whole(name, body, outs, *args, scratch=(), last=False):
    many = isinstance(outs, tuple)
    outs = list(outs) if many else [outs]
    place = pl.BlockSpec(memory_space=pltpu.VMEM)
    if not last:
        outs = [pltpu.VMEM(o.shape, o.dtype) for o in outs]
    got = pl.pallas_call(
        body,
        out_shape=outs,
        in_specs=[place] * len(args),
        out_specs=[pl.BlockSpec() if last else place] * len(outs),
        scratch_shapes=scratch,
        name=name,
        compiler_params=pltpu.CompilerParams(vmem_limit_bytes=16 << 20),
    )(*[pltpu.with_memory_space_constraint(a, pltpu.VMEM) for a in args])
    return tuple(got) if many else got[0]


def shape(dims, kind=BF16):
    return jax.ShapeDtypeStruct(dims, kind)


def trade(boxes, groups=None):
    return lax.all_to_all(
        boxes, "dom", split_axis=0, concat_axis=0, axis_index_groups=groups, tiled=True
    )


def tables_body(nbr_t, deg, sends_t, give, take, own, own_t, inv):
    fan, nodes = nbr_t.shape
    kmax, parts = sends_t.shape
    span = 2 * kmax * parts
    r = lax.broadcasted_iota(jnp.int32, (span, nodes), 0)
    j = r % (2 * kmax)
    entry = nodes + r // (2 * kmax) * kmax + j
    leave = jnp.where(j < kmax, entry, -2)
    arrive = jnp.where(j >= kmax, entry - kmax, -2)
    row = lax.broadcasted_iota(jnp.int32, (nodes, nodes), 0)
    leave_sum = jnp.zeros((span, nodes), F32)
    arrive_sum = jnp.zeros((span, nodes), F32)
    own_sum = jnp.zeros((nodes, nodes), F32)
    for s in range(fan):
        used = jnp.where(s < deg[...], nbr_t[s : s + 1, :], -1)
        leave_sum += jnp.where(leave == used, 1.0, 0.0)
        arrive_sum += jnp.where(arrive == used, 1.0, 0.0)
        own_sum += jnp.where(row == used, 1.0, 0.0)
    own_t[...] = own_sum.astype(BF16)
    own[...] = own_sum.T.astype(BF16)
    part = lax.broadcasted_iota(jnp.int32, (parts, span), 0)
    lane = lax.broadcasted_iota(jnp.int32, (parts, span), 1)
    spread = jnp.where(lane // (2 * kmax) == part, 1.0, 0.0).astype(BF16)
    ids = mm(sends_t[...].astype(F32).astype(BF16), spread)
    slot = lax.broadcasted_iota(jnp.int32, (kmax, span), 0)
    at = lax.broadcasted_iota(jnp.int32, (kmax, span), 1) % (2 * kmax)
    back_id = jnp.sum(jnp.where(slot == at, ids + 1.0, 0.0), axis=0, keepdims=True) - 1.0
    pick_id = jnp.sum(jnp.where(slot + kmax == at, ids + 1.0, 0.0), axis=0, keepdims=True) - 1.0
    node = lax.broadcasted_iota(jnp.int32, (nodes, span), 0).astype(F32)
    home = jnp.where(node == back_id, 1.0, 0.0)
    pick = jnp.where(node == pick_id, 1.0, 0.0)
    give[:, :nodes] = leave_sum.astype(BF16)
    give[:, nodes:] = pick.T.astype(BF16)
    take[:nodes, :] = arrive_sum.T.astype(BF16)
    take[nodes:, :] = home.astype(BF16)
    inv[...] = jnp.broadcast_to(1.0 / deg[...].astype(F32), (nodes, nodes)).T


def turn_body(flat, out):
    groups, nodes, cols = flat.shape
    for g in range(groups):
        out[:, g * nodes : (g + 1) * nodes] = flat[g].T


def ring_place(at, turn, offset):
    o, turned = offset
    return (at + CHIPS + o * (turn if turned else 1)) % CHIPS


def places(offsets, other):
    feat = lax.axis_index("feat")
    y, core = feat // 2, feat % 2
    held = 1 - core if other else core
    return [ring_place(y, 1 - 2 * core, o) * 2 + held for o in offsets]


def places_x(offsets):
    core = lax.axis_index("feat") % 2
    x = lax.axis_index("dom") % CHIPS
    return [ring_place(x, 1 - 2 * core, o) for o in offsets]


SUM_MINE = ((2, False), (-1, True), (1, True), (0, False))
SUM_OTHER = ((2, False), (1, True), (-1, True), (0, False))
GET_MINE = ((0, False), (-1, True), (1, True), (2, False))
GET_OTHER = ((0, False), (1, True), (-1, True), (2, False))


def project(flat, w_one, other):
    groups, nodes, cols = flat.shape

    def body(rows, w, out):
        ids = places(SUM_OTHER if other else SUM_MINE, other)
        picked = jnp.concatenate([rows[g] for g in ids], axis=0)
        out[...] = mm(picked, w[...]).astype(BF16).reshape(out.shape)

    return whole("project", body, shape((CHIPS, nodes, w_one.shape[1])), flat, w_one)


def add(*terms):
    total = terms[0].astype(F32)
    for term in terms[1:]:
        total += term.astype(F32)
    return total


def forward_body(part, got, near, far, grads, inv, give, p_self, p_near, boxes):
    width = grads.shape[1]
    total = add(part[3], got[3], near[...], far[...])
    p_self[...] = total[:, :width]
    mine = total[:, width:].astype(BF16)
    p_near[...] = mine
    scaled = (grads[...].astype(F32) * inv[:, :1]).astype(BF16)
    boxes[...] = mm(give[...], jnp.concatenate([scaled, mine], axis=0)).astype(BF16)


def middle_body(
    recv, p_self, p_near, grads, inv, w_two, give, take, own, own_t,
    boxes, near_local, hidden_out, ahead, behind, third, mine, scratch,
):
    nodes, width = grads.shape
    scales = inv[:, :1]
    both = mm(take[...], recv[...])
    grad = grads[...]
    scaled = (grad.astype(F32) * scales).astype(BF16)
    pre = p_self[...] + scales * (both[:nodes] + mm(own[...], p_near[...]))
    back = (both[nodes:] + mm(own_t[...], scaled)).astype(BF16)
    d_hidden = mm(grad, w_two[:width, :], NT) + mm(back, w_two[width:, :], NT)
    sig = jax.nn.sigmoid(pre)
    hidden = (pre * sig).astype(BF16)
    hidden_out[...] = hidden
    d_pre = d_hidden * sig * (1.0 + pre * (1.0 - sig))
    term = (d_pre * scales).astype(BF16)
    boxes[...] = mm(give[...], jnp.concatenate([term, hidden], axis=0)).astype(BF16)
    near_local[...] = mm(own_t[...], term)
    half = scratch.shape[0] // 2
    for k, right in enumerate((grad, back)):
        piece = mm(hidden, right, TN).astype(BF16)
        scratch[k * half : (k + 1) * half] = piece.reshape(half, -1, width)
    ahead[0] = d_pre.astype(BF16)
    behind[0] = d_pre.astype(BF16)
    for k, other in enumerate((True, False)):
        away, back_to, on_to, here = places(SUM_MINE, other)
        ahead[1 + k] = scratch[away]
        behind[1 + k] = scratch[back_to]
        third[k] = scratch[on_to]
        mine[k] = scratch[here]


def near_body(recv, near_local, take, out):
    nodes = out.shape[0]
    out[...] = (near_local[...] + mm(take[nodes:, :], recv[...])).astype(BF16)


def out_body(recv, hidden, inv, take, own, w_two, out):
    nodes, width = hidden.shape
    total = mm(take[:nodes, :], recv[...]) + mm(own[...], hidden[...])
    agg = (inv[:, :1] * total).astype(BF16)
    out[...] = (mm(hidden[...], w_two[:width, :]) + mm(agg, w_two[width:, :])).astype(BF16)


def grad_body(flat_t, held, other, two, ahead, behind, third, own, stack, boxes):
    groups, nodes, both = stack.shape
    width = both // 2
    chips, deep, rows, cut = boxes.shape
    block = flat_t.shape[0] // chips
    part = block // deep
    ids = places(GET_MINE, False) + places(GET_OTHER, True)
    for k, g in enumerate(ids):
        source = held if k < chips else other
        stack[g, :, :width] = source[k % chips]
        stack[g, :, width:] = source[chips + k % chips]
    total = mm(flat_t[...], stack[...].reshape(groups * nodes, both)).astype(BF16)
    for x in range(chips):
        for q in range(4):
            piece = total[x * block : (x + 1) * block, q * cut : (q + 1) * cut]
            boxes[x, :, q * part : (q + 1) * part, :] = piece.reshape(deep, part, cut)
    for x, target in zip(places_x(SUM_MINE), (ahead, behind, third, own)):
        target[:, :rows, :] = boxes[x]
    twos = add(two[...], other[2 * chips]).astype(BF16)
    tail = (ahead.shape[1] - rows) // 2
    for k in range(2):
        piece = twos[:, k * cut : (k + 1) * cut].reshape(deep, tail, cut)
        for target in (ahead, behind, own):
            target[:, rows + k * tail : rows + (k + 1) * tail, :] = piece
    third[:, rows:, :] = jnp.zeros_like(third[:, rows:, :])


def spread_body(b0, b1, b2, b3, out):
    deep, rows, cut = b0.shape
    block = out.shape[0] // CHIPS
    part = block // deep
    for x, held in zip(places_x(GET_MINE), (b0, b1, b2, b3)):
        at = pl.ds(pl.multiple_of(x * block, block), block)
        for q in range(4):
            piece = held[:, q * part : (q + 1) * part, :].astype(F32)
            out[at, q * cut : (q + 1) * cut] = piece.reshape(block, cut)


def join_body(held, other, out):
    nodes = held.shape[1]

    def put(g, block):
        out[pl.ds(pl.multiple_of(g * nodes, nodes), nodes), :] = block.astype(F32)

    for k, g in enumerate(places(GET_MINE, False)):
        put(g, held[k])
    for k, g in enumerate(places(GET_OTHER, True)):
        put(g, other[k])


def on_device(features, w_one, w_two, neighbor, degree, send_rows, grad_out):
    groups, nodes, cols = features.shape
    width = w_two.shape[1]
    parts = lax.axis_size("dom")
    deep = parts // CHIPS
    sends = send_rows[0]
    kmax = sends.shape[1]
    span = 2 * sends.size
    grads = grad_out[0]
    scale = 1.0 / math.sqrt(groups * nodes * parts)
    y_ahead, y_behind = along_y(1), along_y(-1)
    x_ahead, x_behind = along_x(1, parts, groups), along_x(-1, parts, groups)
    lines = [[z * CHIPS + x for z in range(deep)] for x in range(CHIPS)]

    def forward(block):
        return lax.ppermute(block, "feat", y_ahead)

    def backward(block):
        return lax.ppermute(block, "feat", y_behind)

    def swap(block):
        return lax.ppermute(block, "feat", SWAP)

    def x_forward(block):
        return lax.ppermute(block, ("feat", "dom"), x_ahead)

    def x_backward(block):
        return lax.ppermute(block, ("feat", "dom"), x_behind)

    def gather(block):
        one = forward(block)
        two = backward(block)
        return jnp.stack([block, one, two, forward(one)])

    got = swap(project(features, w_one, True))
    mine = project(features, w_one, False)
    give, take, own, own_t, inv = whole(
        "tables",
        tables_body,
        (
            shape((span, 2 * nodes)),
            shape((2 * nodes, span)),
            shape((nodes, nodes)),
            shape((nodes, nodes)),
            shape((nodes, nodes), F32),
        ),
        neighbor[0].T, degree, sends.T,
    )
    flat_t = whole("turn", turn_body, shape((cols, groups * nodes)), features)
    relay = forward(add(mine[0], got[0]).astype(BF16))
    near = backward(add(mine[1], got[1]).astype(BF16))
    relay, give = lax.optimization_barrier((relay, give))
    far = forward(add(mine[2], got[2], relay).astype(BF16))
    far, flat_t = lax.optimization_barrier((far, flat_t))
    block = shape((nodes, width))

    p_self, p_near, boxes = whole(
        "forward",
        forward_body,
        (shape((nodes, width), F32), block, shape((span, width))),
        mine, got, near, far, grads, inv, give,
    )
    recv = trade(boxes.reshape(parts, 2 * kmax, width)).reshape(span, width)
    rows = 2 * width // groups
    boxes, near_local, hidden, ahead, behind, third, mine = whole(
        "middle",
        middle_body,
        (
            shape((span, width)),
            shape((nodes, width), F32),
            block,
            shape((3, rows, width)),
            shape((3, rows, width)),
            shape((2, rows, width)),
            shape((2, rows, width)),
        ),
        recv, p_self, p_near, grads, inv, w_two, give, take, own, own_t,
        scratch=[pltpu.VMEM((groups, rows, width), BF16)],
    )
    recv = trade(boxes.reshape(parts, 2 * kmax, width)).reshape(span, width)

    relay = forward(ahead)
    near = backward(behind)
    message = jnp.concatenate([relay[:1], add(third, relay[1:]).astype(BF16)])
    message, recv = lax.optimization_barrier((message, recv))
    d_near = whole("near", near_body, block, recv, near_local, take)
    one = forward(d_near)
    two = backward(d_near)
    far = forward(message)
    sums = add(mine, near[1:], far[1:])
    held = jnp.stack(
        [ahead[0], relay[0], near[0], far[0], d_near, one, two, forward(one), sums[0].astype(BF16)]
    )
    other = swap(held)

    kept = 8 * cols // parts // 2
    lot = shape((deep, kept + 4 * width // groups // deep, width // 2))
    ahead, behind, third, mine = whole(
        "grad",
        grad_body,
        (lot, lot, lot, lot),
        flat_t, held, other, sums[1],
        scratch=[
            pltpu.VMEM((groups, nodes, 2 * width), BF16),
            pltpu.VMEM((CHIPS, deep, kept, width // 2), BF16),
        ],
    )
    out = whole("out", out_body, block, recv, hidden, inv, take, own, w_two, last=True)
    relay = x_forward(ahead)
    near = x_backward(behind)
    far = x_forward(add(third, relay).astype(BF16))
    far, out = lax.optimization_barrier((far, out))
    last_rows = lax.broadcasted_iota(jnp.int32, lot.shape, 1) >= kept
    terms = add(mine, near, far) + jnp.where(last_rows, relay.astype(F32), 0.0)
    terms = trade(terms.astype(BF16), lines)
    total = (jnp.sum(terms.astype(F32), axis=0) * scale).astype(BF16)
    total = trade(jnp.broadcast_to(total[None], terms.shape), lines)
    tail = (lot.shape[1] - kept) // 2
    chunk = jnp.concatenate(
        [
            total[:, kept : kept + tail].reshape(deep * tail, -1),
            total[:, kept + tail :].reshape(deep * tail, -1),
        ],
        axis=1,
    )
    mine = total[:, :kept]
    relay = x_forward(mine)
    near = x_backward(mine)
    held, relay = lax.optimization_barrier((gather(chunk), relay))
    far = x_forward(relay)
    one = whole("spread", spread_body, shape((cols, 2 * width), F32), mine, relay, near, far, last=True)
    two = whole("join", join_body, shape((2 * width, width), F32), held, swap(held), last=True)
    return out[None], one, two


def solution(mesh):
    in_specs = (
        P(None, "dom", "feat"),
        P("feat", None),
        P(),
        P("feat", "dom", None),
        P("feat", "dom"),
        P("feat", "dom", None),
        P("feat", "dom", None),
    )
    out_specs = (P("feat", "dom", None), P("feat", None), P())
    return jax.shard_map(
        on_device, mesh=mesh, in_specs=in_specs, out_specs=out_specs, check_vma=False
    )
```

```python
import math

import jax
import jax.numpy as jnp
from jax import lax
from jax.experimental import pallas as pl
from jax.experimental.pallas import tpu as pltpu
from jax.sharding import PartitionSpec as P

F32 = jnp.float32
BF16 = jnp.bfloat16
CHIPS = 4
NT = (((1,), (1,)), ((), ()))
TN = (((0,), (0,)), ((), ()))


def beside(at):
    return at + 1 - 2 * (at % 2), CHIPS - 1 - at


def along_y(turn):
    return [
        (y * 2 + c, beside(y)[(turn + c) % 2] * 2 + c) for y in range(CHIPS) for c in range(2)
    ]


def along_x(turn, parts, feats):
    return [
        (f * parts + z * CHIPS + x, f * parts + z * CHIPS + beside(x)[(turn + f) % 2])
        for f in range(feats)
        for z in range(parts // CHIPS)
        for x in range(CHIPS)
    ]


SWAP = [(i, i ^ 1) for i in range(2 * CHIPS)]


def mm(a, b, dims=(((1,), (0,)), ((), ()))):
    return lax.dot_general(a, b, dims, preferred_element_type=F32)


def whole(name, body, outs, *args, scratch=(), far=()):
    many = isinstance(outs, tuple)
    outs = list(outs) if many else [outs]
    place = pl.BlockSpec(memory_space=pltpu.VMEM)
    kinds = [o if k in far else pltpu.VMEM(o.shape, o.dtype) for k, o in enumerate(outs)]
    got = pl.pallas_call(
        body,
        out_shape=kinds,
        in_specs=[place] * len(args),
        out_specs=[pl.BlockSpec() if k in far else place for k in range(len(outs))],
        scratch_shapes=scratch,
        name=name,
        compiler_params=pltpu.CompilerParams(vmem_limit_bytes=16 << 20),
    )(*[pltpu.with_memory_space_constraint(a, pltpu.VMEM) for a in args])
    return tuple(got) if many else got[0]


def shape(dims, kind=BF16):
    return jax.ShapeDtypeStruct(dims, kind)


def trade(boxes, groups=None):
    return lax.all_to_all(
        boxes, "dom", split_axis=0, concat_axis=0, axis_index_groups=groups, tiled=True
    )


def tables_body(nbr_t, deg, sends_t, give, take, own, own_t, inv):
    fan, nodes = nbr_t.shape
    kmax, parts = sends_t.shape
    span = 2 * kmax * parts
    r = lax.broadcasted_iota(jnp.int32, (span, nodes), 0)
    j = r % (2 * kmax)
    entry = nodes + r // (2 * kmax) * kmax + j
    leave = jnp.where(j < kmax, entry, -2)
    arrive = jnp.where(j >= kmax, entry - kmax, -2)
    row = lax.broadcasted_iota(jnp.int32, (nodes, nodes), 0)
    leave_sum = jnp.zeros((span, nodes), F32)
    arrive_sum = jnp.zeros((span, nodes), F32)
    own_sum = jnp.zeros((nodes, nodes), F32)
    for s in range(fan):
        used = jnp.where(s < deg[...], nbr_t[s : s + 1, :], -1)
        leave_sum += jnp.where(leave == used, 1.0, 0.0)
        arrive_sum += jnp.where(arrive == used, 1.0, 0.0)
        own_sum += jnp.where(row == used, 1.0, 0.0)
    own_t[...] = own_sum.astype(BF16)
    own[...] = own_sum.T.astype(BF16)
    part = lax.broadcasted_iota(jnp.int32, (parts, span), 0)
    lane = lax.broadcasted_iota(jnp.int32, (parts, span), 1)
    spread = jnp.where(lane // (2 * kmax) == part, 1.0, 0.0).astype(BF16)
    ids = mm(sends_t[...].astype(F32).astype(BF16), spread)
    slot = lax.broadcasted_iota(jnp.int32, (kmax, span), 0)
    at = lax.broadcasted_iota(jnp.int32, (kmax, span), 1) % (2 * kmax)
    back_id = jnp.sum(jnp.where(slot == at, ids + 1.0, 0.0), axis=0, keepdims=True) - 1.0
    pick_id = jnp.sum(jnp.where(slot + kmax == at, ids + 1.0, 0.0), axis=0, keepdims=True) - 1.0
    node = lax.broadcasted_iota(jnp.int32, (nodes, span), 0).astype(F32)
    home = jnp.where(node == back_id, 1.0, 0.0)
    pick = jnp.where(node == pick_id, 1.0, 0.0)
    give[:, :nodes] = leave_sum.astype(BF16)
    give[:, nodes:] = pick.T.astype(BF16)
    take[:nodes, :] = arrive_sum.T.astype(BF16)
    take[nodes:, :] = home.astype(BF16)
    inv[...] = jnp.broadcast_to(1.0 / deg[...].astype(F32), (nodes, nodes)).T


def turn_body(flat, out):
    groups, nodes, cols = flat.shape
    for g in range(groups):
        out[:, g * nodes : (g + 1) * nodes] = flat[g].T


def around(at, core):
    left, right = beside(at)
    first = jnp.where(core == 0, left, right)
    return at, first, left + right - first, (at + 2) % CHIPS


SUM_MINE = (1, 3, 2, 0)
SUM_OTHER = (2, 3, 1, 0)
GET_MINE = (0, 1, 2, 3)
GET_OTHER = (0, 2, 1, 3)


def places(order, other):
    feat = lax.axis_index("feat")
    core = feat % 2
    held = 1 - core if other else core
    ring = around(feat // 2, core)
    return [ring[k] * 2 + held for k in order]


def places_x(order):
    ring = around(lax.axis_index("dom") % CHIPS, lax.axis_index("feat") % 2)
    return [ring[k] for k in order]


def project(flat, w_one, other):
    groups, nodes, cols = flat.shape

    def body(rows, w, out):
        ids = places(SUM_OTHER if other else SUM_MINE, other)
        picked = jnp.concatenate([rows[g] for g in ids], axis=0)
        out[...] = mm(picked, w[...]).astype(BF16).reshape(out.shape)

    return whole("project", body, shape((CHIPS, nodes, w_one.shape[1])), flat, w_one)


def add(*terms):
    total = terms[0].astype(F32)
    for term in terms[1:]:
        total += term.astype(F32)
    return total


def forward_body(part, got, near, far, grads, inv, give, p_self, p_near, boxes):
    width = grads.shape[1]
    total = add(part[3], got[3], near[0], far[...])
    p_self[...] = total[:, :width]
    mine = total[:, width:].astype(BF16)
    p_near[...] = mine
    scaled = (grads[...].astype(F32) * inv[:, :1]).astype(BF16)
    boxes[...] = mm(give[...], jnp.concatenate([scaled, mine], axis=0)).astype(BF16)


def middle_body(
    recv, p_self, p_near, grads, inv, w_two, give, take, own, own_t,
    boxes, term_out, hidden_out, first, second, mine, scratch,
):
    nodes, width = grads.shape
    scales = inv[:, :1]
    both = mm(take[...], recv[...])
    grad = grads[...]
    scaled = (grad.astype(F32) * scales).astype(BF16)
    pre = p_self[...] + scales * (both[:nodes] + mm(own[...], p_near[...]))
    back = (both[nodes:] + mm(own_t[...], scaled)).astype(BF16)
    d_hidden = mm(grad, w_two[:width, :], NT) + mm(back, w_two[width:, :], NT)
    sig = jax.nn.sigmoid(pre)
    hidden = (pre * sig).astype(BF16)
    hidden_out[...] = hidden
    d_pre = d_hidden * sig * (1.0 + pre * (1.0 - sig))
    term = (d_pre * scales).astype(BF16)
    boxes[...] = mm(give[...], jnp.concatenate([term, hidden], axis=0)).astype(BF16)
    term_out[...] = term
    half = scratch.shape[0] // 2
    for k, right in enumerate((grad, back)):
        piece = mm(hidden, right, TN).astype(BF16)
        scratch[k * half : (k + 1) * half] = piece.reshape(half, -1, width)
    first[0] = d_pre.astype(BF16)
    for k, other in enumerate((True, False)):
        partner, opposite, later, here = places(SUM_MINE, other)
        first[1 + k] = scratch[partner]
        first[3 + k] = scratch[opposite]
        second[k] = scratch[later]
        mine[k] = scratch[here]


def near_body(recv, term, own_t, take, out):
    nodes = out.shape[0]
    out[...] = (mm(own_t[...], term[...]) + mm(take[nodes:, :], recv[...])).astype(BF16)


def out_body(recv, hidden, inv, take, own, w_two, out):
    nodes, width = hidden.shape
    total = mm(take[:nodes, :], recv[...]) + mm(own[...], hidden[...])
    agg = (inv[:, :1] * total).astype(BF16)
    out[...] = (mm(hidden[...], w_two[:width, :]) + mm(agg, w_two[width:, :])).astype(BF16)


def grad_body(flat_t, held, other, two, first, second, own, stack, boxes):
    groups, nodes, both = stack.shape
    width = both // 2
    chips, deep, rows, cut = boxes.shape
    block = flat_t.shape[0] // chips
    part = block // deep
    ids = places(GET_MINE, False) + places(GET_OTHER, True)
    for k, g in enumerate(ids):
        source = held if k < chips else other
        stack[g, :, :width] = source[k % chips]
        stack[g, :, width:] = source[chips + k % chips]
    total = mm(flat_t[...], stack[...].reshape(groups * nodes, both)).astype(BF16)
    for x in range(chips):
        for q in range(4):
            piece = total[x * block : (x + 1) * block, q * cut : (q + 1) * cut]
            boxes[x, :, q * part : (q + 1) * part, :] = piece.reshape(deep, part, cut)
    partner, opposite, later, here = places_x(SUM_MINE)
    first[:, :rows, :] = boxes[partner]
    first[:, rows : 2 * rows, :] = boxes[opposite]
    second[...] = boxes[later]
    own[:, :rows, :] = boxes[here]
    twos = add(two[...], other[2 * chips]).astype(BF16)
    tail = (own.shape[1] - rows) // 2
    for k in range(2):
        piece = twos[:, k * cut : (k + 1) * cut].reshape(deep, tail, cut)
        first[:, 2 * rows + k * tail : 2 * rows + (k + 1) * tail, :] = piece
        own[:, rows + k * tail : rows + (k + 1) * tail, :] = piece


def x_pass_body(second, own, got, out):
    rows = second.shape[1]
    out[:, :rows, :] = add(second[...], got[:, rows : 2 * rows, :]).astype(BF16)
    out[:, rows:, :] = add(own[:, rows:, :], got[:, 2 * rows :, :]).astype(BF16)


def x_sum_body(own, got, sent, last, out):
    rows = got.shape[1] - own.shape[1]
    out[:, :rows, :] = add(own[:, :rows, :], got[:, :rows, :], last[:, :rows, :]).astype(BF16)
    out[:, rows:, :] = add(sent[:, rows:, :], last[:, rows:, :]).astype(BF16)


def spread_body(held, last, out):
    _, deep, rows, cut = held.shape
    block = out.shape[0] // CHIPS
    part = block // deep
    for k, x in enumerate(places_x(GET_MINE)):
        source = held if k < 2 else last
        at = pl.ds(pl.multiple_of(x * block, block), block)
        for q in range(4):
            piece = source[k % 2, :, q * part : (q + 1) * part, :].astype(F32)
            out[at, q * cut : (q + 1) * cut] = piece.reshape(block, cut)


def join_body(held, other, out):
    nodes = held.shape[1]

    def put(g, block):
        out[pl.ds(pl.multiple_of(g * nodes, nodes), nodes), :] = block.astype(F32)

    for k, g in enumerate(places(GET_MINE, False)):
        put(g, held[k])
    for k, g in enumerate(places(GET_OTHER, True)):
        put(g, other[k])


def on_device(features, w_one, w_two, neighbor, degree, send_rows, grad_out):
    groups, nodes, cols = features.shape
    width = w_two.shape[1]
    parts = lax.axis_size("dom")
    deep = parts // CHIPS
    sends = send_rows[0]
    kmax = sends.shape[1]
    span = 2 * sends.size
    grads = grad_out[0]
    scale = 1.0 / math.sqrt(groups * nodes * parts)
    y_first, y_second = along_y(0), along_y(1)
    x_first, x_second = along_x(0, parts, groups), along_x(1, parts, groups)
    lines = [[z * CHIPS + x for z in range(deep)] for x in range(CHIPS)]

    def y_move(block, pairs):
        return lax.ppermute(block, "feat", pairs)

    def x_move(block, pairs):
        return lax.ppermute(block, ("feat", "dom"), pairs)

    def swap(block):
        return lax.ppermute(block, "feat", SWAP)

    got = swap(project(features, w_one, True))
    mine = project(features, w_one, False)
    give, take, own, own_t, inv = whole(
        "tables",
        tables_body,
        (
            shape((span, 2 * nodes)),
            shape((2 * nodes, span)),
            shape((nodes, nodes)),
            shape((nodes, nodes)),
            shape((nodes, nodes), F32),
        ),
        neighbor[0].T, degree, sends.T,
    )
    flat_t = whole("turn", turn_body, shape((cols, groups * nodes)), features)
    near = y_move(add(mine[:2], got[:2]).astype(BF16), y_first)
    near, give = lax.optimization_barrier((near, give))
    far = y_move(add(mine[2], got[2], near[1]).astype(BF16), y_second)
    far, flat_t = lax.optimization_barrier((far, flat_t))
    block = shape((nodes, width))
    p_self, p_near, boxes = whole(
        "forward",
        forward_body,
        (shape((nodes, width), F32), block, shape((span, width))),
        mine, got, near, far, grads, inv, give,
    )
    recv = trade(boxes.reshape(parts, 2 * kmax, width)).reshape(span, width)
    rows = 2 * width // groups
    boxes, term, hidden, first, second, mine = whole(
        "middle",
        middle_body,
        (
            shape((span, width)),
            block,
            block,
            shape((5, rows, width)),
            shape((2, rows, width)),
            shape((2, rows, width)),
        ),
        recv, p_self, p_near, grads, inv, w_two, give, take, own, own_t,
        scratch=[pltpu.VMEM((groups, rows, width), BF16)],
        far=(0, 1, 2, 3, 4, 5),
    )
    recv = trade(boxes.reshape(parts, 2 * kmax, width)).reshape(span, width)

    got = y_move(first, y_first)
    message = jnp.concatenate([first[:1], got[:1], add(second, got[3:]).astype(BF16)])
    message, recv = lax.optimization_barrier((message, recv))
    d_near = whole("near", near_body, block, recv, term, own_t, take)
    one = y_move(d_near, y_first)
    last = y_move(message, y_second)
    sums = add(mine, got[1:3], last[2:])
    near = jnp.stack([d_near, one])
    held = jnp.concatenate(
        [message[:2], last[:2], near, y_move(near, y_second), sums[:1].astype(BF16)]
    )

    kept = 8 * cols // parts // 2
    tail = 4 * width // groups // deep
    first, second, mine = whole(
        "grad",
        grad_body,
        (
            shape((deep, 2 * kept + tail, width // 2)),
            shape((deep, kept, width // 2)),
            shape((deep, kept + tail, width // 2)),
        ),
        flat_t, held, swap(held), sums[1],
        scratch=[
            pltpu.VMEM((groups, nodes, 2 * width), BF16),
            pltpu.VMEM((CHIPS, deep, kept, width // 2), BF16),
        ],
    )
    out = whole("out", out_body, block, recv, hidden, inv, take, own, w_two, far=(0,))
    lot = shape((deep, kept + tail, width // 2))
    got = x_move(first, x_first)
    sent = whole("x_pass", x_pass_body, lot, second, mine, got)
    last = x_move(sent, x_second)
    last, out = lax.optimization_barrier((last, out))
    terms = trade(whole("x_sum", x_sum_body, lot, mine, got, sent, last), lines)
    total = (jnp.sum(terms.astype(F32), axis=0) * scale).astype(BF16)
    total = trade(jnp.broadcast_to(total[None], terms.shape), lines)
    half = kept + tail // 2
    chunk = jnp.concatenate(
        [total[:, kept:half].reshape(nodes, -1), total[:, half:].reshape(nodes, -1)], axis=1
    )
    mine = total[:, :kept]
    one_y = y_move(chunk, y_first)
    one_x = x_move(mine, x_first)
    one_y, one_x = lax.optimization_barrier((one_y, one_x))
    held_y = jnp.stack([chunk, one_y])
    held_y = jnp.concatenate([held_y, y_move(held_y, y_second)])
    held_x = jnp.stack([mine, one_x])
    last_x = x_move(held_x, x_second)
    held_y, last_x = lax.optimization_barrier((held_y, last_x))
    one = whole(
        "spread", spread_body, shape((cols, 2 * width), F32), held_x, last_x, far=(0,)
    )
    two = whole(
        "join", join_body, shape((2 * width, width), F32), held_y, swap(held_y), far=(0,)
    )
    return out[None], one, two


def solution(mesh):
    in_specs = (
        P(None, "dom", "feat"),
        P("feat", None),
        P(),
        P("feat", "dom", None),
        P("feat", "dom"),
        P("feat", "dom", None),
        P("feat", "dom", None),
    )
    out_specs = (P("feat", "dom", None), P("feat", None), P())
    return jax.shard_map(
        on_device, mesh=mesh, in_specs=in_specs, out_specs=out_specs, check_vma=False
    )
```

```python
import math

import jax
import jax.numpy as jnp
from jax import lax
from jax.experimental import pallas as pl
from jax.experimental.pallas import tpu as pltpu
from jax.sharding import PartitionSpec as P

F32 = jnp.float32
BF16 = jnp.bfloat16
CHIPS = 4
NT = (((1,), (1,)), ((), ()))
TN = (((0,), (0,)), ((), ()))


def beside(at):
    return at + 1 - 2 * (at % 2), CHIPS - 1 - at


def along_y(turn):
    return [
        (y * 2 + c, beside(y)[(turn + c) % 2] * 2 + c) for y in range(CHIPS) for c in range(2)
    ]


def along_x(turn, parts, feats):
    return [
        (f * parts + z * CHIPS + x, f * parts + z * CHIPS + beside(x)[(turn + f) % 2])
        for f in range(feats)
        for z in range(parts // CHIPS)
        for x in range(CHIPS)
    ]


SWAP = [(i, i ^ 1) for i in range(2 * CHIPS)]


def mm(a, b, dims=(((1,), (0,)), ((), ()))):
    return lax.dot_general(a, b, dims, preferred_element_type=F32)


def whole(name, body, outs, *args, scratch=(), far=(), kept=(), raw=()):
    many = isinstance(outs, tuple)
    outs = list(outs) if many else [outs]
    place = pl.BlockSpec(memory_space=pltpu.VMEM)
    kinds = [
        o if k in far else (pltpu.HBM if k in kept else pltpu.VMEM)(o.shape, o.dtype)
        for k, o in enumerate(outs)
    ]
    anywhere = pl.BlockSpec(memory_space=pltpu.HBM)
    got = pl.pallas_call(
        body,
        out_shape=kinds,
        in_specs=[anywhere if k in raw else place for k in range(len(args))],
        out_specs=[
            pl.BlockSpec() if k in far or k in kept else place for k in range(len(outs))
        ],
        scratch_shapes=scratch,
        name=name,
        compiler_params=pltpu.CompilerParams(vmem_limit_bytes=16 << 20),
    )(
        *[
            pltpu.with_memory_space_constraint(a, pltpu.HBM if k in raw else pltpu.VMEM)
            for k, a in enumerate(args)
        ]
    )
    return tuple(got) if many else got[0]


def shape(dims, kind=BF16):
    return jax.ShapeDtypeStruct(dims, kind)


def trade(boxes, groups=None):
    return lax.all_to_all(
        boxes, "dom", split_axis=0, concat_axis=0, axis_index_groups=groups, tiled=True
    )


def tables_body(nbr_t, deg, sends_t, give, take, own, own_t, inv):
    fan, nodes = nbr_t.shape
    kmax, parts = sends_t.shape
    span = 2 * kmax * parts
    r = lax.broadcasted_iota(jnp.int32, (span, nodes), 0)
    j = r % (2 * kmax)
    entry = nodes + r // (2 * kmax) * kmax + j
    leave = jnp.where(j < kmax, entry, -2)
    arrive = jnp.where(j >= kmax, entry - kmax, -2)
    row = lax.broadcasted_iota(jnp.int32, (nodes, nodes), 0)
    leave_sum = jnp.zeros((span, nodes), F32)
    arrive_sum = jnp.zeros((span, nodes), F32)
    own_sum = jnp.zeros((nodes, nodes), F32)
    for s in range(fan):
        used = jnp.where(s < deg[...], nbr_t[s : s + 1, :], -1)
        leave_sum += jnp.where(leave == used, 1.0, 0.0)
        arrive_sum += jnp.where(arrive == used, 1.0, 0.0)
        own_sum += jnp.where(row == used, 1.0, 0.0)
    own_t[...] = own_sum.astype(BF16)
    own[...] = own_sum.T.astype(BF16)
    part = lax.broadcasted_iota(jnp.int32, (parts, span), 0)
    lane = lax.broadcasted_iota(jnp.int32, (parts, span), 1)
    spread = jnp.where(lane // (2 * kmax) == part, 1.0, 0.0).astype(BF16)
    ids = mm(sends_t[...].astype(F32).astype(BF16), spread)
    slot = lax.broadcasted_iota(jnp.int32, (kmax, span), 0)
    at = lax.broadcasted_iota(jnp.int32, (kmax, span), 1) % (2 * kmax)
    back_id = jnp.sum(jnp.where(slot == at, ids + 1.0, 0.0), axis=0, keepdims=True) - 1.0
    pick_id = jnp.sum(jnp.where(slot + kmax == at, ids + 1.0, 0.0), axis=0, keepdims=True) - 1.0
    node = lax.broadcasted_iota(jnp.int32, (nodes, span), 0).astype(F32)
    home = jnp.where(node == back_id, 1.0, 0.0)
    pick = jnp.where(node == pick_id, 1.0, 0.0)
    give[:, :nodes] = leave_sum.astype(BF16)
    give[:, nodes:] = pick.T.astype(BF16)
    take[:nodes, :] = arrive_sum.T.astype(BF16)
    take[nodes:, :] = home.astype(BF16)
    inv[...] = jnp.broadcast_to(1.0 / deg[...].astype(F32), (nodes, nodes)).T


def turn_body(flat, out):
    groups, nodes, cols = flat.shape
    for g in range(groups):
        out[:, g * nodes : (g + 1) * nodes] = flat[g].T


def around(at, core):
    left, right = beside(at)
    first = jnp.where(core == 0, left, right)
    return at, first, left + right - first, (at + 2) % CHIPS


SUM_MINE = (1, 3, 2, 0)
SUM_OTHER = (2, 3, 1, 0)
GET_MINE = (0, 1, 2, 3)
GET_OTHER = (0, 2, 1, 3)


def places(order, other):
    feat = lax.axis_index("feat")
    core = feat % 2
    held = 1 - core if other else core
    ring = around(feat // 2, core)
    return [ring[k] * 2 + held for k in order]


def places_x(order):
    ring = around(lax.axis_index("dom") % CHIPS, lax.axis_index("feat") % 2)
    return [ring[k] for k in order]


def project(flat, w_one, other):
    groups, nodes, cols = flat.shape
    width = w_one.shape[1]
    cut = width // 4
    held = pltpu.VMEM((CHIPS, nodes, cols), BF16)
    sems = pltpu.SemaphoreType.DMA((2, CHIPS))
    picks = shape((CHIPS, nodes, width))

    def fetch(rows, mine, sem):
        ids = places(SUM_OTHER if other else SUM_MINE, other)
        moves = [
            pltpu.make_async_copy(rows.at[g], mine.at[k], sem.at[0, k]) for k, g in enumerate(ids)
        ]
        for move in moves:
            move.start()
        return moves

    def other_body(rows, w, out, w_out, mine, sem):
        moves = fetch(rows, mine, sem)
        cuts = [slice(k * cut, (k + 1) * cut) for k in range(4)]
        loads = [
            pltpu.make_async_copy(w.at[:, c], w_out.at[:, c], sem.at[1, k])
            for k, c in enumerate(cuts)
        ]
        for load in loads:
            load.start()
        for move in moves:
            move.wait()
        picked = mine[...].reshape(CHIPS * nodes, cols)
        for load, c in zip(loads, cuts):
            load.wait()
            out[:, :, c] = mm(picked, w_out[:, c]).astype(BF16).reshape(CHIPS, nodes, cut)

    def mine_body(rows, w, out, mine, sem):
        for move in fetch(rows, mine, sem):
            move.wait()
        picked = mine[...].reshape(CHIPS * nodes, cols)
        out[...] = mm(picked, w[...]).astype(BF16).reshape(out.shape)

    if other:
        outs = (picks, shape(w_one.shape))
        return whole("project", other_body, outs, flat, w_one, scratch=[held, sems], raw=(0, 1))
    return whole("project", mine_body, picks, flat, w_one, scratch=[held, sems], raw=(0,))


def add(*terms):
    total = terms[0].astype(F32)
    for term in terms[1:]:
        total += term.astype(F32)
    return total


def forward_body(part, got, near, far, grads, inv, give, p_self, p_near, boxes):
    width = grads.shape[1]
    total = add(part[3], got[3], near[0], far[...])
    p_self[...] = total[:, :width]
    mine = total[:, width:].astype(BF16)
    p_near[...] = mine
    scaled = (grads[...].astype(F32) * inv[:, :1]).astype(BF16)
    boxes[...] = mm(give[...], jnp.concatenate([scaled, mine], axis=0)).astype(BF16)


def middle_body(
    recv, p_self, p_near, grads, inv, w_two, give, take, own, own_t,
    boxes, term_out, hidden_out, first, second, mine, scratch,
):
    nodes, width = grads.shape
    scales = inv[:, :1]
    both = mm(take[...], recv[...])
    grad = grads[...]
    scaled = (grad.astype(F32) * scales).astype(BF16)
    pre = p_self[...] + scales * (both[:nodes] + mm(own[...], p_near[...]))
    back = (both[nodes:] + mm(own_t[...], scaled)).astype(BF16)
    d_hidden = mm(grad, w_two[:width, :], NT) + mm(back, w_two[width:, :], NT)
    sig = jax.nn.sigmoid(pre)
    hidden = (pre * sig).astype(BF16)
    hidden_out[...] = hidden
    d_pre = d_hidden * sig * (1.0 + pre * (1.0 - sig))
    term = (d_pre * scales).astype(BF16)
    boxes[...] = mm(give[...], jnp.concatenate([term, hidden], axis=0)).astype(BF16)
    term_out[...] = term
    half = scratch.shape[0] // 2
    for k, right in enumerate((grad, back)):
        piece = mm(hidden, right, TN).astype(BF16)
        scratch[k * half : (k + 1) * half] = piece.reshape(half, -1, width)
    first[0] = d_pre.astype(BF16)
    for k, other in enumerate((True, False)):
        partner, opposite, later, here = places(SUM_MINE, other)
        first[1 + k] = scratch[partner]
        first[3 + k] = scratch[opposite]
        second[k] = scratch[later]
        mine[k] = scratch[here]


def near_body(recv, term, own_t, take, out):
    nodes = out.shape[0]
    out[...] = (mm(own_t[...], term[...]) + mm(take[nodes:, :], recv[...])).astype(BF16)


def out_body(recv, hidden, inv, take, own, w_two, out):
    nodes, width = hidden.shape
    total = mm(take[:nodes, :], recv[...]) + mm(own[...], hidden[...])
    agg = (inv[:, :1] * total).astype(BF16)
    out[...] = (mm(hidden[...], w_two[:width, :]) + mm(agg, w_two[width:, :])).astype(BF16)


def grad_body(flat_t, held, other, two, first, second, own, stack, boxes):
    groups, nodes, both = stack.shape
    width = both // 2
    chips, deep, rows, cut = boxes.shape
    block = flat_t.shape[0] // chips
    part = block // deep
    ids = places(GET_MINE, False) + places(GET_OTHER, True)
    for k, g in enumerate(ids):
        source = held if k < chips else other
        stack[g, :, :width] = source[k % chips]
        stack[g, :, width:] = source[chips + k % chips]
    total = mm(flat_t[...], stack[...].reshape(groups * nodes, both)).astype(BF16)
    for x in range(chips):
        for q in range(4):
            piece = total[x * block : (x + 1) * block, q * cut : (q + 1) * cut]
            boxes[x, :, q * part : (q + 1) * part, :] = piece.reshape(deep, part, cut)
    partner, opposite, later, here = places_x(SUM_MINE)
    first[:, :rows, :] = boxes[partner]
    first[:, rows : 2 * rows, :] = boxes[opposite]
    second[...] = boxes[later]
    own[:, :rows, :] = boxes[here]
    twos = add(two[...], other[2 * chips]).astype(BF16)
    tail = (own.shape[1] - rows) // 2
    for k in range(2):
        piece = twos[:, k * cut : (k + 1) * cut].reshape(deep, tail, cut)
        first[:, 2 * rows + k * tail : 2 * rows + (k + 1) * tail, :] = piece
        own[:, rows + k * tail : rows + (k + 1) * tail, :] = piece


def x_pass_body(second, own, got, out):
    rows = second.shape[1]
    out[:, :rows, :] = add(second[...], got[:, rows : 2 * rows, :]).astype(BF16)
    out[:, rows:, :] = add(own[:, rows:, :], got[:, 2 * rows :, :]).astype(BF16)


def x_sum_body(own, got, sent, last, out):
    rows = got.shape[1] - own.shape[1]
    out[:, :rows, :] = add(own[:, :rows, :], got[:, :rows, :], last[:, :rows, :]).astype(BF16)
    out[:, rows:, :] = add(sent[:, rows:, :], last[:, rows:, :]).astype(BF16)


def spread_body(held, last, out):
    _, deep, rows, cut = held.shape
    block = out.shape[0] // CHIPS
    part = block // deep
    for k, x in enumerate(places_x(GET_MINE)):
        source = held if k < 2 else last
        at = pl.ds(pl.multiple_of(x * block, block), block)
        for q in range(4):
            piece = source[k % 2, :, q * part : (q + 1) * part, :].astype(F32)
            out[at, q * cut : (q + 1) * cut] = piece.reshape(block, cut)


def join_body(held, other, out):
    nodes = held.shape[1]

    def put(g, block):
        out[pl.ds(pl.multiple_of(g * nodes, nodes), nodes), :] = block.astype(F32)

    for k, g in enumerate(places(GET_MINE, False)):
        put(g, held[k])
    for k, g in enumerate(places(GET_OTHER, True)):
        put(g, other[k])


def on_device(features, w_one, w_two, neighbor, degree, send_rows, grad_out):
    groups, nodes, cols = features.shape
    width = w_two.shape[1]
    parts = lax.axis_size("dom")
    deep = parts // CHIPS
    sends = send_rows[0]
    kmax = sends.shape[1]
    span = 2 * sends.size
    grads = grad_out[0]
    scale = 1.0 / math.sqrt(groups * nodes * parts)
    y_first, y_second = along_y(0), along_y(1)
    x_first, x_second = along_x(0, parts, groups), along_x(1, parts, groups)
    lines = [[z * CHIPS + x for z in range(deep)] for x in range(CHIPS)]

    def y_move(block, pairs):
        return lax.ppermute(block, "feat", pairs)

    def x_move(block, pairs):
        return lax.ppermute(block, ("feat", "dom"), pairs)

    def swap(block):
        return lax.ppermute(block, "feat", SWAP)

    theirs, w_one = project(features, w_one, True)
    got = swap(theirs)
    mine = project(features, w_one, False)
    give, take, own, own_t, inv = whole(
        "tables",
        tables_body,
        (
            shape((span, 2 * nodes)),
            shape((2 * nodes, span)),
            shape((nodes, nodes)),
            shape((nodes, nodes)),
            shape((nodes, nodes), F32),
        ),
        neighbor[0].T, degree, sends.T,
    )
    flat_t = whole("turn", turn_body, shape((cols, groups * nodes)), features)
    near = y_move(add(mine[:2], got[:2]).astype(BF16), y_first)
    near, give = lax.optimization_barrier((near, give))
    far = y_move(add(mine[2], got[2], near[1]).astype(BF16), y_second)
    far, flat_t = lax.optimization_barrier((far, flat_t))
    block = shape((nodes, width))
    p_self, p_near, boxes = whole(
        "forward",
        forward_body,
        (shape((nodes, width), F32), block, shape((span, width))),
        mine, got, near, far, grads, inv, give,
    )
    recv = trade(boxes.reshape(parts, 2 * kmax, width)).reshape(span, width)
    rows = 2 * width // groups
    boxes, term, hidden, first, second, mine = whole(
        "middle",
        middle_body,
        (
            shape((span, width)),
            block,
            block,
            shape((5, rows, width)),
            shape((2, rows, width)),
            shape((2, rows, width)),
        ),
        recv, p_self, p_near, grads, inv, w_two, give, take, own, own_t,
        scratch=[pltpu.VMEM((groups, rows, width), BF16)],
        far=(0, 3, 4, 5),
        kept=(1, 2),
    )
    recv = trade(boxes.reshape(parts, 2 * kmax, width)).reshape(span, width)

    got = y_move(first, y_first)
    message = jnp.concatenate([first[:1], got[:1], add(second, got[3:]).astype(BF16)])
    message, recv = lax.optimization_barrier((message, recv))
    d_near = whole("near", near_body, block, recv, term, own_t, take)
    one = y_move(d_near, y_first)
    last = y_move(message, y_second)
    sums = add(mine, got[1:3], last[2:])
    near = jnp.stack([d_near, one])
    held = jnp.concatenate(
        [message[:2], last[:2], near, y_move(near, y_second), sums[:1].astype(BF16)]
    )

    kept = 8 * cols // parts // 2
    tail = 4 * width // groups // deep
    first, second, mine = whole(
        "grad",
        grad_body,
        (
            shape((deep, 2 * kept + tail, width // 2)),
            shape((deep, kept, width // 2)),
            shape((deep, kept + tail, width // 2)),
        ),
        flat_t, held, swap(held), sums[1],
        scratch=[
            pltpu.VMEM((groups, nodes, 2 * width), BF16),
            pltpu.VMEM((CHIPS, deep, kept, width // 2), BF16),
        ],
    )
    out = whole("out", out_body, block, recv, hidden, inv, take, own, w_two, far=(0,))
    lot = shape((deep, kept + tail, width // 2))
    got = x_move(first, x_first)
    sent = whole("x_pass", x_pass_body, lot, second, mine, got)
    last = x_move(sent, x_second)
    last, out = lax.optimization_barrier((last, out))
    terms = trade(whole("x_sum", x_sum_body, lot, mine, got, sent, last), lines)
    total = (jnp.sum(terms.astype(F32), axis=0) * scale).astype(BF16)
    total = trade(jnp.broadcast_to(total[None], terms.shape), lines)
    half = kept + tail // 2
    chunk = jnp.concatenate(
        [total[:, kept:half].reshape(nodes, -1), total[:, half:].reshape(nodes, -1)], axis=1
    )
    mine = total[:, :kept]
    one_y = y_move(chunk, y_first)
    one_x = x_move(mine, x_first)
    one_y, one_x = lax.optimization_barrier((one_y, one_x))
    held_y = jnp.stack([chunk, one_y])
    held_y = jnp.concatenate([held_y, y_move(held_y, y_second)])
    held_x = jnp.stack([mine, one_x])
    last_x = x_move(held_x, x_second)
    one = whole(
        "spread", spread_body, shape((cols, 2 * width), F32), held_x, last_x, far=(0,)
    )
    two = whole(
        "join", join_body, shape((2 * width, width), F32), held_y, swap(held_y), far=(0,)
    )
    return out[None], one, two


def solution(mesh):
    in_specs = (
        P(None, "dom", "feat"),
        P("feat", None),
        P(),
        P("feat", "dom", None),
        P("feat", "dom"),
        P("feat", "dom", None),
        P("feat", "dom", None),
    )
    out_specs = (P("feat", "dom", None), P("feat", None), P())
    return jax.shard_map(
        on_device, mesh=mesh, in_specs=in_specs, out_specs=out_specs, check_vma=False
    )
```

```python
import math

import jax
import jax.numpy as jnp
from jax import lax
from jax.experimental import pallas as pl
from jax.experimental.pallas import tpu as pltpu
from jax.sharding import PartitionSpec as P

F32 = jnp.float32
BF16 = jnp.bfloat16
CHIPS = 4
NT = (((1,), (1,)), ((), ()))
TN = (((0,), (0,)), ((), ()))


def beside(at):
    return at + 1 - 2 * (at % 2), CHIPS - 1 - at


def along_y(turn):
    return [
        (y * 2 + c, beside(y)[(turn + c) % 2] * 2 + c) for y in range(CHIPS) for c in range(2)
    ]


def along_x(turn, parts, feats):
    return [
        (f * parts + z * CHIPS + x, f * parts + z * CHIPS + beside(x)[(turn + f) % 2])
        for f in range(feats)
        for z in range(parts // CHIPS)
        for x in range(CHIPS)
    ]


SWAP = [(i, i ^ 1) for i in range(2 * CHIPS)]


def mm(a, b, dims=(((1,), (0,)), ((), ()))):
    return lax.dot_general(a, b, dims, preferred_element_type=F32)


def whole(name, body, outs, *args, scratch=(), far=(), kept=(), raw=()):
    many = isinstance(outs, tuple)
    outs = list(outs) if many else [outs]
    place = pl.BlockSpec(memory_space=pltpu.VMEM)
    kinds = [
        o if k in far else (pltpu.HBM if k in kept else pltpu.VMEM)(o.shape, o.dtype)
        for k, o in enumerate(outs)
    ]
    anywhere = pl.BlockSpec(memory_space=pltpu.HBM)
    got = pl.pallas_call(
        body,
        out_shape=kinds,
        in_specs=[anywhere if k in raw else place for k in range(len(args))],
        out_specs=[
            pl.BlockSpec() if k in far or k in kept else place for k in range(len(outs))
        ],
        scratch_shapes=scratch,
        name=name,
        compiler_params=pltpu.CompilerParams(vmem_limit_bytes=16 << 20),
    )(
        *[
            pltpu.with_memory_space_constraint(a, pltpu.HBM if k in raw else pltpu.VMEM)
            for k, a in enumerate(args)
        ]
    )
    return tuple(got) if many else got[0]


def shape(dims, kind=BF16):
    return jax.ShapeDtypeStruct(dims, kind)


def trade(boxes, groups=None):
    return lax.all_to_all(
        boxes, "dom", split_axis=0, concat_axis=0, axis_index_groups=groups, tiled=True
    )


def tables_body(
    nbr_t, deg, sends_t, grads, pick, mean, back, home, own, own_t, inv, boxes
):
    fan, nodes = nbr_t.shape
    kmax, parts = sends_t.shape
    span = kmax * parts
    entry = lax.broadcasted_iota(jnp.int32, (nodes + span, nodes), 0)
    count = jnp.zeros((nodes + span, nodes), F32)
    for s in range(fan):
        used = jnp.where(s < deg[...], nbr_t[s : s + 1, :], -1)
        count += jnp.where(entry == used, 1.0, 0.0)
    own_t[...] = count[:nodes].astype(BF16)
    own[...] = count[:nodes].T.astype(BF16)
    back[...] = count[nodes:].astype(BF16)
    mean[...] = count[nodes:].T.astype(BF16)
    part = lax.broadcasted_iota(jnp.int32, (parts, span), 0)
    lane = lax.broadcasted_iota(jnp.int32, (parts, span), 1)
    spread = jnp.where(lane // kmax == part, 1.0, 0.0).astype(BF16)
    ids = mm(sends_t[...].astype(F32).astype(BF16), spread)
    slot = lax.broadcasted_iota(jnp.int32, (kmax, span), 0)
    at = lax.broadcasted_iota(jnp.int32, (kmax, span), 1) % kmax
    sent = jnp.sum(jnp.where(slot == at, ids, 0.0), axis=0, keepdims=True)
    node = lax.broadcasted_iota(jnp.int32, (nodes, span), 0).astype(F32)
    chosen = jnp.where(node == sent, 1.0, 0.0)
    home[...] = chosen.astype(BF16)
    pick[...] = chosen.T.astype(BF16)
    scales = jnp.broadcast_to(1.0 / deg[...].astype(F32), (nodes, nodes)).T
    inv[...] = scales
    scaled = (grads[...].astype(F32) * scales[:, :1]).astype(BF16)
    boxes[...] = mm(count[nodes:].astype(BF16), scaled).astype(BF16)


def turn_body(flat, out):
    groups, nodes, cols = flat.shape
    for g in range(groups):
        out[:, g * nodes : (g + 1) * nodes] = flat[g].T


def around(at, core):
    left, right = beside(at)
    first = jnp.where(core == 0, left, right)
    return at, first, left + right - first, (at + 2) % CHIPS


SUM_MINE = (1, 3, 2, 0)
SUM_OTHER = (2, 3, 1, 0)
GET_MINE = (0, 1, 2, 3)
GET_OTHER = (0, 2, 1, 3)


def places(order, other):
    feat = lax.axis_index("feat")
    core = feat % 2
    held = 1 - core if other else core
    ring = around(feat // 2, core)
    return [ring[k] * 2 + held for k in order]


def places_x(order):
    ring = around(lax.axis_index("dom") % CHIPS, lax.axis_index("feat") % 2)
    return [ring[k] for k in order]


def project(flat, w_one, other):
    groups, nodes, cols = flat.shape
    width = w_one.shape[1]
    cut = width // 4
    held = pltpu.VMEM((CHIPS, nodes, cols), BF16)
    sems = pltpu.SemaphoreType.DMA((2, CHIPS))
    picks = shape((CHIPS, nodes, width))

    def fetch(rows, mine, sem):
        ids = places(SUM_OTHER if other else SUM_MINE, other)
        moves = [
            pltpu.make_async_copy(rows.at[g], mine.at[k], sem.at[0, k]) for k, g in enumerate(ids)
        ]
        for move in moves:
            move.start()
        return moves

    def other_body(rows, w, out, w_out, mine, sem):
        moves = fetch(rows, mine, sem)
        cuts = [slice(k * cut, (k + 1) * cut) for k in range(4)]
        loads = [
            pltpu.make_async_copy(w.at[:, c], w_out.at[:, c], sem.at[1, k])
            for k, c in enumerate(cuts)
        ]
        for load in loads:
            load.start()
        for move in moves:
            move.wait()
        picked = mine[...].reshape(CHIPS * nodes, cols)
        for load, c in zip(loads, cuts):
            load.wait()
            out[:, :, c] = mm(picked, w_out[:, c]).astype(BF16).reshape(CHIPS, nodes, cut)

    def mine_body(rows, w, out, mine, sem):
        for move in fetch(rows, mine, sem):
            move.wait()
        picked = mine[...].reshape(CHIPS * nodes, cols)
        out[...] = mm(picked, w[...]).astype(BF16).reshape(out.shape)

    if other:
        outs = (picks, shape(w_one.shape))
        return whole("project", other_body, outs, flat, w_one, scratch=[held, sems], raw=(0, 1))
    return whole("project", mine_body, picks, flat, w_one, scratch=[held, sems], raw=(0,))


def add(*terms):
    total = terms[0].astype(F32)
    for term in terms[1:]:
        total += term.astype(F32)
    return total


def forward_body(part, got, near, far, pick, p_self, p_near, boxes):
    width = p_near.shape[1]
    total = add(part[3], got[3], near[0], far[...])
    p_self[...] = total[:, :width]
    mine = total[:, width:].astype(BF16)
    p_near[...] = mine
    boxes[...] = mm(pick[...], mine).astype(BF16)


def middle_body(
    recv, recv_back, p_self, p_near, grads, inv, w_two, pick, mean, back_t, home, own, own_t,
    boxes, hidden_boxes, term_out, hidden_out, first, second, mine, scratch,
):
    nodes, width = grads.shape
    scales = inv[:, :1]
    grad = grads[...]
    scaled = (grad.astype(F32) * scales).astype(BF16)
    pre = p_self[...] + scales * (mm(mean[...], recv[...]) + mm(own[...], p_near[...]))
    back = (mm(home[...], recv_back[...]) + mm(own_t[...], scaled)).astype(BF16)
    d_hidden = mm(grad, w_two[:width, :], NT) + mm(back, w_two[width:, :], NT)
    sig = jax.nn.sigmoid(pre)
    hidden = (pre * sig).astype(BF16)
    hidden_out[...] = hidden
    d_pre = d_hidden * sig * (1.0 + pre * (1.0 - sig))
    term = (d_pre * scales).astype(BF16)
    boxes[...] = mm(back_t[...], term).astype(BF16)
    hidden_boxes[...] = mm(pick[...], hidden).astype(BF16)
    term_out[...] = term
    half = scratch.shape[0] // 2
    for k, right in enumerate((grad, back)):
        piece = mm(hidden, right, TN).astype(BF16)
        scratch[k * half : (k + 1) * half] = piece.reshape(half, -1, width)
    first[0] = d_pre.astype(BF16)
    for k, other in enumerate((True, False)):
        partner, opposite, later, here = places(SUM_MINE, other)
        first[1 + k] = scratch[partner]
        first[3 + k] = scratch[opposite]
        second[k] = scratch[later]
        mine[k] = scratch[here]


def near_body(recv, term, own_t, home, out):
    out[...] = (mm(own_t[...], term[...]) + mm(home[...], recv[...])).astype(BF16)


def out_body(recv, hidden, inv, mean, own, w_two, out):
    width = hidden.shape[1]
    total = mm(mean[...], recv[...]) + mm(own[...], hidden[...])
    agg = (inv[:, :1] * total).astype(BF16)
    out[...] = (mm(hidden[...], w_two[:width, :]) + mm(agg, w_two[width:, :])).astype(BF16)


def grad_body(flat_t, held, other, two, first, second, own, stack, boxes):
    groups, nodes, both = stack.shape
    width = both // 2
    chips, deep, rows, cut = boxes.shape
    block = flat_t.shape[0] // chips
    part = block // deep
    ids = places(GET_MINE, False) + places(GET_OTHER, True)
    for k, g in enumerate(ids):
        source = held if k < chips else other
        stack[g, :, :width] = source[k % chips]
        stack[g, :, width:] = source[chips + k % chips]
    total = mm(flat_t[...], stack[...].reshape(groups * nodes, both)).astype(BF16)
    for x in range(chips):
        for q in range(4):
            piece = total[x * block : (x + 1) * block, q * cut : (q + 1) * cut]
            boxes[x, :, q * part : (q + 1) * part, :] = piece.reshape(deep, part, cut)
    partner, opposite, later, here = places_x(SUM_MINE)
    first[:, :rows, :] = boxes[partner]
    first[:, rows : 2 * rows, :] = boxes[opposite]
    second[...] = boxes[later]
    own[:, :rows, :] = boxes[here]
    twos = add(two[...], other[2 * chips]).astype(BF16)
    tail = (own.shape[1] - rows) // 2
    for k in range(2):
        piece = twos[:, k * cut : (k + 1) * cut].reshape(deep, tail, cut)
        first[:, 2 * rows + k * tail : 2 * rows + (k + 1) * tail, :] = piece
        own[:, rows + k * tail : rows + (k + 1) * tail, :] = piece


def x_pass_body(second, own, got, out):
    rows = second.shape[1]
    out[:, :rows, :] = add(second[...], got[:, rows : 2 * rows, :]).astype(BF16)
    out[:, rows:, :] = add(own[:, rows:, :], got[:, 2 * rows :, :]).astype(BF16)


def x_sum_body(own, got, sent, last, out):
    rows = got.shape[1] - own.shape[1]
    out[:, :rows, :] = add(own[:, :rows, :], got[:, :rows, :], last[:, :rows, :]).astype(BF16)
    out[:, rows:, :] = add(sent[:, rows:, :], last[:, rows:, :]).astype(BF16)


def spread_body(held, last, out):
    _, deep, rows, cut = held.shape
    block = out.shape[0] // CHIPS
    part = block // deep
    for k, x in enumerate(places_x(GET_MINE)):
        source = held if k < 2 else last
        at = pl.ds(pl.multiple_of(x * block, block), block)
        for q in range(4):
            piece = source[k % 2, :, q * part : (q + 1) * part, :].astype(F32)
            out[at, q * cut : (q + 1) * cut] = piece.reshape(block, cut)


def join_body(held, other, out):
    nodes = held.shape[1]

    def put(g, block):
        out[pl.ds(pl.multiple_of(g * nodes, nodes), nodes), :] = block.astype(F32)

    for k, g in enumerate(places(GET_MINE, False)):
        put(g, held[k])
    for k, g in enumerate(places(GET_OTHER, True)):
        put(g, other[k])


def on_device(features, w_one, w_two, neighbor, degree, send_rows, grad_out):
    groups, nodes, cols = features.shape
    width = w_two.shape[1]
    parts = lax.axis_size("dom")
    deep = parts // CHIPS
    sends = send_rows[0]
    kmax = sends.shape[1]
    span = sends.size
    grads = grad_out[0]
    scale = 1.0 / math.sqrt(groups * nodes * parts)
    y_first, y_second = along_y(0), along_y(1)
    x_first, x_second = along_x(0, parts, groups), along_x(1, parts, groups)
    lines = [[z * CHIPS + x for z in range(deep)] for x in range(CHIPS)]

    def y_move(block, pairs):
        return lax.ppermute(block, "feat", pairs)

    def x_move(block, pairs):
        return lax.ppermute(block, ("feat", "dom"), pairs)

    def swap(block):
        return lax.ppermute(block, "feat", SWAP)

    theirs, w_one = project(features, w_one, True)
    got = swap(theirs)
    mine = project(features, w_one, False)
    block = shape((nodes, width))
    lot = shape((span, width))
    pick, mean, back_t, home, own, own_t, inv, boxes = whole(
        "tables",
        tables_body,
        (
            shape((span, nodes)),
            shape((nodes, span)),
            shape((span, nodes)),
            shape((nodes, span)),
            shape((nodes, nodes)),
            shape((nodes, nodes)),
            shape((nodes, nodes), F32),
            lot,
        ),
        neighbor[0].T, degree, sends.T, grads,
    )

    def exchange(boxes):
        return trade(boxes.reshape(parts, kmax, width)).reshape(span, width)

    recv_back = exchange(boxes)
    flat_t = whole("turn", turn_body, shape((cols, groups * nodes)), features)
    near = y_move(add(mine[:2], got[:2]).astype(BF16), y_first)
    near, pick = lax.optimization_barrier((near, pick))
    far = y_move(add(mine[2], got[2], near[1]).astype(BF16), y_second)
    far, flat_t, recv_back = lax.optimization_barrier((far, flat_t, recv_back))
    p_self, p_near, boxes = whole(
        "forward",
        forward_body,
        (shape((nodes, width), F32), block, lot),
        mine, got, near, far, pick,
    )
    recv = exchange(boxes)
    rows = 2 * width // groups
    boxes, hidden_boxes, term, hidden, first, second, mine = whole(
        "middle",
        middle_body,
        (
            lot,
            lot,
            block,
            block,
            shape((5, rows, width)),
            shape((2, rows, width)),
            shape((2, rows, width)),
        ),
        recv, recv_back, p_self, p_near, grads, inv, w_two, pick, mean, back_t, home, own, own_t,
        scratch=[pltpu.VMEM((groups, rows, width), BF16)],
        far=(0, 4, 5, 6),
        kept=(1, 2, 3),
    )
    recv = exchange(boxes)

    got = y_move(first, y_first)
    message = jnp.concatenate([first[:1], got[:1], add(second, got[3:]).astype(BF16)])
    message, recv = lax.optimization_barrier((message, recv))
    hidden_boxes, message = lax.optimization_barrier((hidden_boxes, message))
    d_near = whole("near", near_body, block, recv, term, own_t, home)
    one = y_move(d_near, y_first)
    last = y_move(message, y_second)
    sums = add(mine, got[1:3], last[2:])
    near = jnp.stack([d_near, one])
    held = jnp.concatenate(
        [message[:2], last[:2], near, y_move(near, y_second), sums[:1].astype(BF16)]
    )

    recv = exchange(hidden_boxes)

    kept = 8 * cols // parts // 2
    tail = 4 * width // groups // deep
    first, second, mine = whole(
        "grad",
        grad_body,
        (
            shape((deep, 2 * kept + tail, width // 2)),
            shape((deep, kept, width // 2)),
            shape((deep, kept + tail, width // 2)),
        ),
        flat_t, held, swap(held), sums[1],
        scratch=[
            pltpu.VMEM((groups, nodes, 2 * width), BF16),
            pltpu.VMEM((CHIPS, deep, kept, width // 2), BF16),
        ],
    )
    out = whole("out", out_body, block, recv, hidden, inv, mean, own, w_two, far=(0,))
    lot = shape((deep, kept + tail, width // 2))
    got = x_move(first, x_first)
    sent = whole("x_pass", x_pass_body, lot, second, mine, got)
    last = x_move(sent, x_second)
    last, out = lax.optimization_barrier((last, out))
    terms = trade(whole("x_sum", x_sum_body, lot, mine, got, sent, last), lines)
    total = (jnp.sum(terms.astype(F32), axis=0) * scale).astype(BF16)
    total = trade(jnp.broadcast_to(total[None], terms.shape), lines)
    half = kept + tail // 2
    chunk = jnp.concatenate(
        [total[:, kept:half].reshape(nodes, -1), total[:, half:].reshape(nodes, -1)], axis=1
    )
    mine = total[:, :kept]
    one_y = y_move(chunk, y_first)
    one_x = x_move(mine, x_first)
    one_y, one_x = lax.optimization_barrier((one_y, one_x))
    held_y = jnp.stack([chunk, one_y])
    held_y = jnp.concatenate([held_y, y_move(held_y, y_second)])
    held_x = jnp.stack([mine, one_x])
    last_x = x_move(held_x, x_second)
    one = whole(
        "spread", spread_body, shape((cols, 2 * width), F32), held_x, last_x, far=(0,)
    )
    two = whole(
        "join", join_body, shape((2 * width, width), F32), held_y, swap(held_y), far=(0,)
    )
    return out[None], one, two


def solution(mesh):
    in_specs = (
        P(None, "dom", "feat"),
        P("feat", None),
        P(),
        P("feat", "dom", None),
        P("feat", "dom"),
        P("feat", "dom", None),
        P("feat", "dom", None),
    )
    out_specs = (P("feat", "dom", None), P("feat", None), P())
    return jax.shard_map(
        on_device, mesh=mesh, in_specs=in_specs, out_specs=out_specs, check_vma=False
    )
```

```python
import math

import jax
import jax.numpy as jnp
from jax import lax
from jax.experimental import pallas as pl
from jax.experimental.pallas import tpu as pltpu
from jax.sharding import PartitionSpec as P

F32 = jnp.float32
BF16 = jnp.bfloat16
CHIPS = 4
NT = (((1,), (1,)), ((), ()))
TN = (((0,), (0,)), ((), ()))


def beside(at):
    return at + 1 - 2 * (at % 2), CHIPS - 1 - at


def along_y(turn):
    return [
        (y * 2 + c, beside(y)[(turn + c) % 2] * 2 + c) for y in range(CHIPS) for c in range(2)
    ]


def along_x(turn, parts, feats):
    return [
        (f * parts + z * CHIPS + x, f * parts + z * CHIPS + beside(x)[(turn + f) % 2])
        for f in range(feats)
        for z in range(parts // CHIPS)
        for x in range(CHIPS)
    ]


SWAP = [(i, i ^ 1) for i in range(2 * CHIPS)]


def mm(a, b, dims=(((1,), (0,)), ((), ()))):
    return lax.dot_general(a, b, dims, preferred_element_type=F32)


def whole(name, body, outs, *args, scratch=(), far=(), kept=(), raw=(), load=()):
    many = isinstance(outs, tuple)
    outs = list(outs) if many else [outs]
    place = pl.BlockSpec(memory_space=pltpu.VMEM)
    kinds = [
        o if k in far else (pltpu.HBM if k in kept else pltpu.VMEM)(o.shape, o.dtype)
        for k, o in enumerate(outs)
    ]
    anywhere = pl.BlockSpec(memory_space=pltpu.HBM)
    got = pl.pallas_call(
        body,
        out_shape=kinds,
        in_specs=[
            anywhere if k in raw else pl.BlockSpec() if k in load else place
            for k in range(len(args))
        ],
        out_specs=[
            pl.BlockSpec() if k in far or k in kept else place for k in range(len(outs))
        ],
        scratch_shapes=scratch,
        name=name,
        compiler_params=pltpu.CompilerParams(vmem_limit_bytes=16 << 20),
    )(
        *[
            pltpu.with_memory_space_constraint(
                a, pltpu.HBM if k in raw or k in load else pltpu.VMEM
            )
            for k, a in enumerate(args)
        ]
    )
    return tuple(got) if many else got[0]


def shape(dims, kind=BF16):
    return jax.ShapeDtypeStruct(dims, kind)


def trade(boxes, groups=None):
    return lax.all_to_all(
        boxes, "dom", split_axis=0, concat_axis=0, axis_index_groups=groups, tiled=True
    )


def tables_body(
    nbr_t, deg, sends_t, give, take, own, own_t, inv, pick_out, mean, back, home_out
):
    fan, nodes = nbr_t.shape
    kmax, parts = sends_t.shape
    span = 2 * kmax * parts
    r = lax.broadcasted_iota(jnp.int32, (span, nodes), 0)
    j = r % (2 * kmax)
    entry = nodes + r // (2 * kmax) * kmax + j
    leave = jnp.where(j < kmax, entry, -2)
    arrive = jnp.where(j >= kmax, entry - kmax, -2)
    half = span // 2
    row = lax.broadcasted_iota(jnp.int32, (nodes + half, nodes), 0)
    leave_sum = jnp.zeros((span, nodes), F32)
    arrive_sum = jnp.zeros((span, nodes), F32)
    own_sum = jnp.zeros((nodes + half, nodes), F32)
    for s in range(fan):
        used = jnp.where(s < deg[...], nbr_t[s : s + 1, :], -1)
        leave_sum += jnp.where(leave == used, 1.0, 0.0)
        arrive_sum += jnp.where(arrive == used, 1.0, 0.0)
        own_sum += jnp.where(row == used, 1.0, 0.0)
    own_t[...] = own_sum[:nodes].astype(BF16)
    own[...] = own_sum[:nodes].T.astype(BF16)
    back[...] = own_sum[nodes:].astype(BF16)
    mean[...] = own_sum[nodes:].T.astype(BF16)
    part = lax.broadcasted_iota(jnp.int32, (parts, span), 0)
    lane = lax.broadcasted_iota(jnp.int32, (parts, span), 1)
    spread = jnp.where(lane // (2 * kmax) == part, 1.0, 0.0).astype(BF16)
    ids = mm(sends_t[...].astype(F32).astype(BF16), spread)
    slot = lax.broadcasted_iota(jnp.int32, (kmax, span), 0)
    at = lax.broadcasted_iota(jnp.int32, (kmax, span), 1) % (2 * kmax)
    back_id = jnp.sum(jnp.where(slot == at, ids + 1.0, 0.0), axis=0, keepdims=True) - 1.0
    pick_id = jnp.sum(jnp.where(slot + kmax == at, ids + 1.0, 0.0), axis=0, keepdims=True) - 1.0
    node = lax.broadcasted_iota(jnp.int32, (nodes, span), 0).astype(F32)
    home = jnp.where(node == back_id, 1.0, 0.0)
    pick = jnp.where(node == pick_id, 1.0, 0.0)
    give[:, :nodes] = leave_sum.astype(BF16)
    give[:, nodes:] = pick.T.astype(BF16)
    take[:nodes, :] = arrive_sum.T.astype(BF16)
    take[nodes:, :] = home.astype(BF16)
    inv[...] = jnp.broadcast_to(1.0 / deg[...].astype(F32), (nodes, nodes)).T
    part = lax.broadcasted_iota(jnp.int32, (parts, half), 0)
    lane = lax.broadcasted_iota(jnp.int32, (parts, half), 1)
    spread = jnp.where(lane // kmax == part, 1.0, 0.0).astype(BF16)
    ids = mm(sends_t[...].astype(F32).astype(BF16), spread)
    slot = lax.broadcasted_iota(jnp.int32, (kmax, half), 0)
    sent = jnp.sum(jnp.where(slot == lane[:kmax] % kmax, ids, 0.0), axis=0, keepdims=True)
    node = lax.broadcasted_iota(jnp.int32, (nodes, half), 0).astype(F32)
    chosen = jnp.where(node == sent, 1.0, 0.0)
    home_out[...] = chosen.astype(BF16)
    pick_out[...] = chosen.T.astype(BF16)


def turn_body(flat, out):
    groups, nodes, cols = flat.shape
    for g in range(groups):
        out[:, g * nodes : (g + 1) * nodes] = flat[g].T


def around(at, core):
    left, right = beside(at)
    first = jnp.where(core == 0, left, right)
    return at, first, left + right - first, (at + 2) % CHIPS


SUM_MINE = (1, 3, 2, 0)
SUM_OTHER = (2, 3, 1, 0)
GET_MINE = (0, 1, 2, 3)
GET_OTHER = (0, 2, 1, 3)


def places(order, other):
    feat = lax.axis_index("feat")
    core = feat % 2
    held = 1 - core if other else core
    ring = around(feat // 2, core)
    return [ring[k] * 2 + held for k in order]


def places_x(order):
    ring = around(lax.axis_index("dom") % CHIPS, lax.axis_index("feat") % 2)
    return [ring[k] for k in order]


def project(flat, w_one, other):
    groups, nodes, cols = flat.shape
    width = w_one.shape[1]
    cut = width // 4
    held = pltpu.VMEM((CHIPS, nodes, cols), BF16)
    sems = pltpu.SemaphoreType.DMA((2, CHIPS))
    picks = shape((CHIPS, nodes, width))

    def fetch(rows, mine, sem):
        ids = places(SUM_OTHER if other else SUM_MINE, other)
        moves = [
            pltpu.make_async_copy(rows.at[g], mine.at[k], sem.at[0, k]) for k, g in enumerate(ids)
        ]
        for move in moves:
            move.start()
        return moves

    def other_body(rows, w, out, w_out, mine, sem):
        moves = fetch(rows, mine, sem)
        cuts = [slice(k * cut, (k + 1) * cut) for k in range(4)]
        loads = [
            pltpu.make_async_copy(w.at[:, c], w_out.at[:, c], sem.at[1, k])
            for k, c in enumerate(cuts)
        ]
        for load in loads:
            load.start()
        for move in moves:
            move.wait()
        picked = mine[...].reshape(CHIPS * nodes, cols)
        for load, c in zip(loads, cuts):
            load.wait()
            out[:, :, c] = mm(picked, w_out[:, c]).astype(BF16).reshape(CHIPS, nodes, cut)

    def mine_body(rows, w, out, mine, sem):
        for move in fetch(rows, mine, sem):
            move.wait()
        picked = mine[...].reshape(CHIPS * nodes, cols)
        out[...] = mm(picked, w[...]).astype(BF16).reshape(out.shape)

    if other:
        outs = (picks, shape(w_one.shape))
        return whole("project", other_body, outs, flat, w_one, scratch=[held, sems], raw=(0, 1))
    return whole("project", mine_body, picks, flat, w_one, scratch=[held, sems], raw=(0,))


def add(*terms):
    total = terms[0].astype(F32)
    for term in terms[1:]:
        total += term.astype(F32)
    return total


def forward_body(part, got, near, far, grads, inv, give, p_self, p_near, boxes):
    width = grads.shape[1]
    total = add(part[3], got[3], near[0], far[...])
    p_self[...] = total[:, :width]
    mine = total[:, width:].astype(BF16)
    p_near[...] = mine
    scaled = (grads[...].astype(F32) * inv[:, :1]).astype(BF16)
    boxes[...] = mm(give[...], jnp.concatenate([scaled, mine], axis=0)).astype(BF16)


def middle_body(
    recv, p_self, p_near, grads, inv, w_two, pick, back_t, take, own, own_t,
    boxes, hidden_boxes, term_out, hidden_out, first, second, mine, scratch,
):
    nodes, width = grads.shape
    scales = inv[:, :1]
    both = mm(take[...], recv[...])
    grad = grads[...]
    scaled = (grad.astype(F32) * scales).astype(BF16)
    pre = p_self[...] + scales * (both[:nodes] + mm(own[...], p_near[...]))
    back = (both[nodes:] + mm(own_t[...], scaled)).astype(BF16)
    d_hidden = mm(grad, w_two[:width, :], NT) + mm(back, w_two[width:, :], NT)
    sig = jax.nn.sigmoid(pre)
    hidden = (pre * sig).astype(BF16)
    hidden_out[...] = hidden
    d_pre = d_hidden * sig * (1.0 + pre * (1.0 - sig))
    term = (d_pre * scales).astype(BF16)
    boxes[...] = mm(back_t[...], term).astype(BF16)
    hidden_boxes[...] = mm(pick[...], hidden).astype(BF16)
    term_out[...] = term
    half = scratch.shape[0] // 2
    for k, right in enumerate((grad, back)):
        piece = mm(hidden, right, TN).astype(BF16)
        scratch[k * half : (k + 1) * half] = piece.reshape(half, -1, width)
    first[0] = d_pre.astype(BF16)
    for k, other in enumerate((True, False)):
        partner, opposite, later, here = places(SUM_MINE, other)
        first[1 + k] = scratch[partner]
        first[3 + k] = scratch[opposite]
        second[k] = scratch[later]
        mine[k] = scratch[here]


def near_body(recv, term, own_t, home, out):
    out[...] = (mm(own_t[...], term[...]) + mm(home[...], recv[...])).astype(BF16)


def out_body(recv, hidden, inv, mean, own, w_two, out):
    width = hidden.shape[1]
    total = mm(mean[...], recv[...]) + mm(own[...], hidden[...])
    agg = (inv[:, :1] * total).astype(BF16)
    out[...] = (mm(hidden[...], w_two[:width, :]) + mm(agg, w_two[width:, :])).astype(BF16)


def grad_body(flat_t, held, other, two, first, second, own, stack, boxes):
    groups, nodes, both = stack.shape
    width = both // 2
    chips, deep, rows, cut = boxes.shape
    block = flat_t.shape[0] // chips
    part = block // deep
    ids = places(GET_MINE, False) + places(GET_OTHER, True)
    for k, g in enumerate(ids):
        source = held if k < chips else other
        stack[g, :, :width] = source[k % chips]
        stack[g, :, width:] = source[chips + k % chips]
    total = mm(flat_t[...], stack[...].reshape(groups * nodes, both)).astype(BF16)
    for x in range(chips):
        for q in range(4):
            piece = total[x * block : (x + 1) * block, q * cut : (q + 1) * cut]
            boxes[x, :, q * part : (q + 1) * part, :] = piece.reshape(deep, part, cut)
    partner, opposite, later, here = places_x(SUM_MINE)
    first[:, :rows, :] = boxes[partner]
    first[:, rows : 2 * rows, :] = boxes[opposite]
    second[...] = boxes[later]
    own[:, :rows, :] = boxes[here]
    twos = add(two[...], other[2 * chips]).astype(BF16)
    tail = (own.shape[1] - rows) // 2
    for k in range(2):
        piece = twos[:, k * cut : (k + 1) * cut].reshape(deep, tail, cut)
        first[:, 2 * rows + k * tail : 2 * rows + (k + 1) * tail, :] = piece
        own[:, rows + k * tail : rows + (k + 1) * tail, :] = piece


def x_pass_body(second, own, got, out):
    rows = second.shape[1]
    out[:, :rows, :] = add(second[...], got[:, rows : 2 * rows, :]).astype(BF16)
    out[:, rows:, :] = add(own[:, rows:, :], got[:, 2 * rows :, :]).astype(BF16)


def x_sum_body(own, got, sent, last, out):
    rows = got.shape[1] - own.shape[1]
    out[:, :rows, :] = add(own[:, :rows, :], got[:, :rows, :], last[:, :rows, :]).astype(BF16)
    out[:, rows:, :] = add(sent[:, rows:, :], last[:, rows:, :]).astype(BF16)


def spread_body(held, last, out):
    _, deep, rows, cut = held.shape
    block = out.shape[0] // CHIPS
    part = block // deep
    for k, x in enumerate(places_x(GET_MINE)):
        source = held if k < 2 else last
        at = pl.ds(pl.multiple_of(x * block, block), block)
        for q in range(4):
            piece = source[k % 2, :, q * part : (q + 1) * part, :].astype(F32)
            out[at, q * cut : (q + 1) * cut] = piece.reshape(block, cut)


def join_body(held, other, out):
    nodes = held.shape[1]

    def put(g, block):
        out[pl.ds(pl.multiple_of(g * nodes, nodes), nodes), :] = block.astype(F32)

    for k, g in enumerate(places(GET_MINE, False)):
        put(g, held[k])
    for k, g in enumerate(places(GET_OTHER, True)):
        put(g, other[k])


def on_device(features, w_one, w_two, neighbor, degree, send_rows, grad_out):
    groups, nodes, cols = features.shape
    width = w_two.shape[1]
    parts = lax.axis_size("dom")
    deep = parts // CHIPS
    sends = send_rows[0]
    kmax = sends.shape[1]
    span = 2 * sends.size
    grads = grad_out[0]
    scale = 1.0 / math.sqrt(groups * nodes * parts)
    y_first, y_second = along_y(0), along_y(1)
    x_first, x_second = along_x(0, parts, groups), along_x(1, parts, groups)
    lines = [[z * CHIPS + x for z in range(deep)] for x in range(CHIPS)]

    def y_move(block, pairs):
        return lax.ppermute(block, "feat", pairs)

    def x_move(block, pairs):
        return lax.ppermute(block, ("feat", "dom"), pairs)

    def swap(block):
        return lax.ppermute(block, "feat", SWAP)

    theirs, w_one = project(features, w_one, True)
    got = swap(theirs)
    mine = project(features, w_one, False)
    give, take, own, own_t, inv, pick, mean, back_t, home = whole(
        "tables",
        tables_body,
        (
            shape((span, 2 * nodes)),
            shape((2 * nodes, span)),
            shape((nodes, nodes)),
            shape((nodes, nodes)),
            shape((nodes, nodes), F32),
            shape((span // 2, nodes)),
            shape((nodes, span // 2)),
            shape((span // 2, nodes)),
            shape((nodes, span // 2)),
        ),
        neighbor[0].T, degree, sends.T,
    )
    flat_t = whole("turn", turn_body, shape((cols, groups * nodes)), features)
    near = y_move(add(mine[:2], got[:2]).astype(BF16), y_first)
    near, give = lax.optimization_barrier((near, give))
    far = y_move(add(mine[2], got[2], near[1]).astype(BF16), y_second)
    far, flat_t = lax.optimization_barrier((far, flat_t))
    block = shape((nodes, width))
    p_self, p_near, boxes = whole(
        "forward",
        forward_body,
        (shape((nodes, width), F32), block, shape((span, width))),
        mine, got, near, far, grads, inv, give,
    )
    recv = trade(boxes.reshape(parts, 2 * kmax, width)).reshape(span, width)
    rows = 2 * width // groups
    lot = shape((span // 2, width))
    boxes, hidden_boxes, term, hidden, first, second, mine = whole(
        "middle",
        middle_body,
        (
            lot,
            lot,
            block,
            block,
            shape((5, rows, width)),
            shape((2, rows, width)),
            shape((2, rows, width)),
        ),
        recv, p_self, p_near, grads, inv, w_two, pick, back_t, take, own, own_t,
        scratch=[pltpu.VMEM((groups, rows, width), BF16)],
        far=(0, 4, 5, 6),
        kept=(1, 2, 3),
    )

    def exchange(boxes):
        return trade(boxes.reshape(parts, kmax, width)).reshape(span // 2, width)

    recv = exchange(boxes)

    got = y_move(first, y_first)
    message = jnp.concatenate([first[:1], got[:1], add(second, got[3:]).astype(BF16)])
    message, recv = lax.optimization_barrier((message, recv))
    hidden_boxes, message = lax.optimization_barrier((hidden_boxes, message))
    d_near = whole("near", near_body, block, recv, term, own_t, home)
    one = y_move(d_near, y_first)
    last = y_move(message, y_second)
    sums = add(mine, got[1:3], last[2:])
    near = jnp.stack([d_near, one])
    held = jnp.concatenate(
        [message[:2], last[:2], near, y_move(near, y_second), sums[:1].astype(BF16)]
    )

    recv = exchange(hidden_boxes)

    kept = 8 * cols // parts // 2
    tail = 4 * width // groups // deep
    first, second, mine = whole(
        "grad",
        grad_body,
        (
            shape((deep, 2 * kept + tail, width // 2)),
            shape((deep, kept, width // 2)),
            shape((deep, kept + tail, width // 2)),
        ),
        flat_t, held, swap(held), sums[1],
        scratch=[
            pltpu.VMEM((groups, nodes, 2 * width), BF16),
            pltpu.VMEM((CHIPS, deep, kept, width // 2), BF16),
        ],
    )
    lot = shape((deep, kept + tail, width // 2))
    got = x_move(first, x_first)
    sent = whole("x_pass", x_pass_body, lot, second, mine, got)
    last = x_move(sent, x_second)
    last, recv = lax.optimization_barrier((last, recv))
    terms = trade(whole("x_sum", x_sum_body, lot, mine, got, sent, last, load=(3,)), lines)
    total = (jnp.sum(terms.astype(F32), axis=0) * scale).astype(BF16)
    total = trade(jnp.broadcast_to(total[None], terms.shape), lines)
    half = kept + tail // 2
    chunk = jnp.concatenate(
        [total[:, kept:half].reshape(nodes, -1), total[:, half:].reshape(nodes, -1)], axis=1
    )
    mine = total[:, :kept]
    one_y = y_move(chunk, y_first)
    one_x = x_move(mine, x_first)
    out = whole("out", out_body, block, recv, hidden, inv, mean, own, w_two, far=(0,))
    one_y, one_x = lax.optimization_barrier((one_y, one_x))
    held_y = jnp.stack([chunk, one_y])
    held_y = jnp.concatenate([held_y, y_move(held_y, y_second)])
    held_y, out = lax.optimization_barrier((held_y, out))
    held_x = jnp.stack([mine, one_x])
    last_x = x_move(held_x, x_second)
    one = whole(
        "spread", spread_body, shape((cols, 2 * width), F32), held_x, last_x, far=(0,)
    )
    two = whole(
        "join", join_body, shape((2 * width, width), F32), held_y, swap(held_y), far=(0,)
    )
    return out[None], one, two


def solution(mesh):
    in_specs = (
        P(None, "dom", "feat"),
        P("feat", None),
        P(),
        P("feat", "dom", None),
        P("feat", "dom"),
        P("feat", "dom", None),
        P("feat", "dom", None),
    )
    out_specs = (P("feat", "dom", None), P("feat", None), P())
    return jax.shard_map(
        on_device, mesh=mesh, in_specs=in_specs, out_specs=out_specs, check_vma=False
    )
```

```python
import math

import jax
import jax.numpy as jnp
from jax import lax
from jax.experimental import pallas as pl
from jax.experimental.pallas import tpu as pltpu
from jax.sharding import PartitionSpec as P

F32 = jnp.float32
BF16 = jnp.bfloat16
CHIPS = 4
NT = (((1,), (1,)), ((), ()))
TN = (((0,), (0,)), ((), ()))


def beside(at):
    return at + 1 - 2 * (at % 2), CHIPS - 1 - at


def along_y(turn):
    return [
        (y * 2 + c, beside(y)[(turn + c) % 2] * 2 + c) for y in range(CHIPS) for c in range(2)
    ]


def along_x(turn, parts, feats):
    return [
        (f * parts + z * CHIPS + x, f * parts + z * CHIPS + beside(x)[(turn + f) % 2])
        for f in range(feats)
        for z in range(parts // CHIPS)
        for x in range(CHIPS)
    ]


SWAP = [(i, i ^ 1) for i in range(2 * CHIPS)]


def mm(a, b, dims=(((1,), (0,)), ((), ()))):
    return lax.dot_general(a, b, dims, preferred_element_type=F32)


def whole(name, body, outs, *args, scratch=(), far=(), kept=(), raw=(), load=()):
    many = isinstance(outs, tuple)
    outs = list(outs) if many else [outs]
    place = pl.BlockSpec(memory_space=pltpu.VMEM)
    kinds = [
        o if k in far else (pltpu.HBM if k in kept else pltpu.VMEM)(o.shape, o.dtype)
        for k, o in enumerate(outs)
    ]
    anywhere = pl.BlockSpec(memory_space=pltpu.HBM)
    got = pl.pallas_call(
        body,
        out_shape=kinds,
        in_specs=[
            anywhere if k in raw else pl.BlockSpec() if k in load else place
            for k in range(len(args))
        ],
        out_specs=[
            pl.BlockSpec() if k in far or k in kept else place for k in range(len(outs))
        ],
        scratch_shapes=scratch,
        name=name,
        compiler_params=pltpu.CompilerParams(vmem_limit_bytes=16 << 20),
    )(
        *[
            pltpu.with_memory_space_constraint(
                a, pltpu.HBM if k in raw or k in load else pltpu.VMEM
            )
            for k, a in enumerate(args)
        ]
    )
    return tuple(got) if many else got[0]


def shape(dims, kind=BF16):
    return jax.ShapeDtypeStruct(dims, kind)


def trade(boxes, groups=None):
    return lax.all_to_all(
        boxes, "dom", split_axis=0, concat_axis=0, axis_index_groups=groups, tiled=True
    )


def tables_body(
    nbr_t, deg, sends_t, give, take, own, own_t, inv, pick_out, mean, back, home_out
):
    fan, nodes = nbr_t.shape
    kmax, parts = sends_t.shape
    span = 2 * kmax * parts
    r = lax.broadcasted_iota(jnp.int32, (span, nodes), 0)
    j = r % (2 * kmax)
    entry = nodes + r // (2 * kmax) * kmax + j
    leave = jnp.where(j < kmax, entry, -2)
    arrive = jnp.where(j >= kmax, entry - kmax, -2)
    half = span // 2
    row = lax.broadcasted_iota(jnp.int32, (nodes + half, nodes), 0)
    leave_sum = jnp.zeros((span, nodes), F32)
    arrive_sum = jnp.zeros((span, nodes), F32)
    own_sum = jnp.zeros((nodes + half, nodes), F32)
    for s in range(fan):
        used = jnp.where(s < deg[...], nbr_t[s : s + 1, :], -1)
        leave_sum += jnp.where(leave == used, 1.0, 0.0)
        arrive_sum += jnp.where(arrive == used, 1.0, 0.0)
        own_sum += jnp.where(row == used, 1.0, 0.0)
    own_t[...] = own_sum[:nodes].astype(BF16)
    own[...] = own_sum[:nodes].T.astype(BF16)
    back[...] = own_sum[nodes:].astype(BF16)
    mean[...] = own_sum[nodes:].T.astype(BF16)
    part = lax.broadcasted_iota(jnp.int32, (parts, span), 0)
    lane = lax.broadcasted_iota(jnp.int32, (parts, span), 1)
    spread = jnp.where(lane // (2 * kmax) == part, 1.0, 0.0).astype(BF16)
    ids = mm(sends_t[...].astype(F32).astype(BF16), spread)
    slot = lax.broadcasted_iota(jnp.int32, (kmax, span), 0)
    at = lax.broadcasted_iota(jnp.int32, (kmax, span), 1) % (2 * kmax)
    back_id = jnp.sum(jnp.where(slot == at, ids + 1.0, 0.0), axis=0, keepdims=True) - 1.0
    pick_id = jnp.sum(jnp.where(slot + kmax == at, ids + 1.0, 0.0), axis=0, keepdims=True) - 1.0
    node = lax.broadcasted_iota(jnp.int32, (nodes, span), 0).astype(F32)
    home = jnp.where(node == back_id, 1.0, 0.0)
    pick = jnp.where(node == pick_id, 1.0, 0.0)
    give[:, :nodes] = leave_sum.astype(BF16)
    give[:, nodes:] = pick.T.astype(BF16)
    take[:nodes, :] = arrive_sum.T.astype(BF16)
    take[nodes:, :] = home.astype(BF16)
    inv[...] = jnp.broadcast_to(1.0 / deg[...].astype(F32), (nodes, nodes)).T
    part = lax.broadcasted_iota(jnp.int32, (parts, half), 0)
    lane = lax.broadcasted_iota(jnp.int32, (parts, half), 1)
    spread = jnp.where(lane // kmax == part, 1.0, 0.0).astype(BF16)
    ids = mm(sends_t[...].astype(F32).astype(BF16), spread)
    slot = lax.broadcasted_iota(jnp.int32, (kmax, half), 0)
    sent = jnp.sum(jnp.where(slot == lane[:kmax] % kmax, ids, 0.0), axis=0, keepdims=True)
    node = lax.broadcasted_iota(jnp.int32, (nodes, half), 0).astype(F32)
    chosen = jnp.where(node == sent, 1.0, 0.0)
    home_out[...] = chosen.astype(BF16)
    pick_out[...] = chosen.T.astype(BF16)


def turn_body(flat, out):
    groups, nodes, cols = flat.shape
    for g in range(groups):
        out[:, g * nodes : (g + 1) * nodes] = flat[g].T


def around(at, core):
    left, right = beside(at)
    first = jnp.where(core == 0, left, right)
    return at, first, left + right - first, (at + 2) % CHIPS


SUM_MINE = (1, 3, 2, 0)
SUM_OTHER = (2, 3, 1, 0)
GET_MINE = (0, 1, 2, 3)
GET_OTHER = (0, 2, 1, 3)


def places(order, other):
    feat = lax.axis_index("feat")
    core = feat % 2
    held = 1 - core if other else core
    ring = around(feat // 2, core)
    return [ring[k] * 2 + held for k in order]


def places_x(order):
    ring = around(lax.axis_index("dom") % CHIPS, lax.axis_index("feat") % 2)
    return [ring[k] for k in order]


def project(flat, w_one, other):
    groups, nodes, cols = flat.shape
    width = w_one.shape[1]
    held = pltpu.VMEM((CHIPS, nodes, cols), BF16)
    sems = pltpu.SemaphoreType.DMA((2, CHIPS))
    picks = shape((CHIPS, nodes, width))

    def fetch(rows, mine, sem):
        ids = places(SUM_OTHER if other else SUM_MINE, other)
        moves = [
            pltpu.make_async_copy(rows.at[g], mine.at[k], sem.at[0, k]) for k, g in enumerate(ids)
        ]
        for move in moves:
            move.start()
        return moves

    def other_body(rows, w, out, w_out, mine, sem):
        moves = fetch(rows, mine, sem)
        depth = cols // CHIPS
        loads = [
            pltpu.make_async_copy(w.at[c], w_out.at[c], sem.at[1, k])
            for k, c in enumerate([pl.ds(k * depth, depth) for k in range(CHIPS)])
        ]
        for load in loads:
            load.start()
        for move in moves:
            move.wait()
        half = cols // 2
        picked = mine[...].reshape(CHIPS * nodes, cols)
        total = None
        for k in range(2):
            for load in loads[2 * k : 2 * k + 2]:
                load.wait()
            at = slice(k * half, (k + 1) * half)
            term = mm(picked[:, at], w_out[at, :])
            total = term if total is None else total + term
        out[...] = total.astype(BF16).reshape(out.shape)

    def mine_body(rows, w, out, mine, sem):
        for move in fetch(rows, mine, sem):
            move.wait()
        picked = mine[...].reshape(CHIPS * nodes, cols)
        out[...] = mm(picked, w[...]).astype(BF16).reshape(out.shape)

    if other:
        outs = (picks, shape(w_one.shape))
        return whole("project", other_body, outs, flat, w_one, scratch=[held, sems], raw=(0, 1))
    return whole("project", mine_body, picks, flat, w_one, scratch=[held, sems], raw=(0,))


def add(*terms):
    total = terms[0].astype(F32)
    for term in terms[1:]:
        total += term.astype(F32)
    return total


def forward_body(part, got, near, far, grads, inv, give, p_self, p_near, boxes):
    width = grads.shape[1]
    total = add(part[3], got[3], near[0], far[...])
    p_self[...] = total[:, :width]
    mine = total[:, width:].astype(BF16)
    p_near[...] = mine
    scaled = (grads[...].astype(F32) * inv[:, :1]).astype(BF16)
    boxes[...] = mm(give[...], jnp.concatenate([scaled, mine], axis=0)).astype(BF16)


def middle_body(
    recv, p_self, p_near, grads, inv, w_two, pick, back_t, take, own, own_t,
    boxes, hidden_boxes, term_out, hidden_out, first, second, mine, scratch,
):
    nodes, width = grads.shape
    scales = inv[:, :1]
    both = mm(take[...], recv[...])
    grad = grads[...]
    scaled = (grad.astype(F32) * scales).astype(BF16)
    pre = p_self[...] + scales * (both[:nodes] + mm(own[...], p_near[...]))
    back = (both[nodes:] + mm(own_t[...], scaled)).astype(BF16)
    d_hidden = mm(grad, w_two[:width, :], NT) + mm(back, w_two[width:, :], NT)
    sig = jax.nn.sigmoid(pre)
    hidden = (pre * sig).astype(BF16)
    hidden_out[...] = hidden
    d_pre = d_hidden * sig * (1.0 + pre * (1.0 - sig))
    term = (d_pre * scales).astype(BF16)
    boxes[...] = mm(back_t[...], term).astype(BF16)
    hidden_boxes[...] = mm(pick[...], hidden).astype(BF16)
    term_out[...] = term
    half = scratch.shape[0] // 2
    for k, right in enumerate((grad, back)):
        piece = mm(hidden, right, TN).astype(BF16)
        scratch[k * half : (k + 1) * half] = piece.reshape(half, -1, width)
    first[0] = d_pre.astype(BF16)
    for k, other in enumerate((True, False)):
        partner, opposite, later, here = places(SUM_MINE, other)
        first[1 + k] = scratch[partner]
        first[3 + k] = scratch[opposite]
        second[k] = scratch[later]
        mine[k] = scratch[here]


def near_body(recv, term, own_t, home, out):
    out[...] = (mm(own_t[...], term[...]) + mm(home[...], recv[...])).astype(BF16)


def out_body(recv, hidden, inv, mean, own, w_two, out):
    width = hidden.shape[1]
    total = mm(mean[...], recv[...]) + mm(own[...], hidden[...])
    agg = (inv[:, :1] * total).astype(BF16)
    out[...] = (mm(hidden[...], w_two[:width, :]) + mm(agg, w_two[width:, :])).astype(BF16)


def grad_body(flat_t, held, other, two, first, second, own, stack, boxes):
    groups, nodes, both = stack.shape
    width = both // 2
    chips, deep, rows, cut = boxes.shape
    block = flat_t.shape[0] // chips
    part = block // deep
    ids = places(GET_MINE, False) + places(GET_OTHER, True)
    for k, g in enumerate(ids):
        source = held if k < chips else other
        stack[g, :, :width] = source[k % chips]
        stack[g, :, width:] = source[chips + k % chips]
    total = mm(flat_t[...], stack[...].reshape(groups * nodes, both)).astype(BF16)
    for x in range(chips):
        for q in range(4):
            piece = total[x * block : (x + 1) * block, q * cut : (q + 1) * cut]
            boxes[x, :, q * part : (q + 1) * part, :] = piece.reshape(deep, part, cut)
    partner, opposite, later, here = places_x(SUM_MINE)
    first[:, :rows, :] = boxes[partner]
    first[:, rows : 2 * rows, :] = boxes[opposite]
    second[...] = boxes[later]
    own[:, :rows, :] = boxes[here]
    twos = add(two[...], other[2 * chips]).astype(BF16)
    tail = (own.shape[1] - rows) // 2
    for k in range(2):
        piece = twos[:, k * cut : (k + 1) * cut].reshape(deep, tail, cut)
        first[:, 2 * rows + k * tail : 2 * rows + (k + 1) * tail, :] = piece
        own[:, rows + k * tail : rows + (k + 1) * tail, :] = piece


def x_pass_body(second, own, got, out):
    rows = second.shape[1]
    out[:, :rows, :] = add(second[...], got[:, rows : 2 * rows, :]).astype(BF16)
    out[:, rows:, :] = add(own[:, rows:, :], got[:, 2 * rows :, :]).astype(BF16)


def x_sum_body(own, got, sent, last, out):
    rows = got.shape[1] - own.shape[1]
    out[:, :rows, :] = add(own[:, :rows, :], got[:, :rows, :], last[:, :rows, :]).astype(BF16)
    out[:, rows:, :] = add(sent[:, rows:, :], last[:, rows:, :]).astype(BF16)


def spread_body(held, last, out):
    _, deep, rows, cut = held.shape
    block = out.shape[0] // CHIPS
    part = block // deep
    for k, x in enumerate(places_x(GET_MINE)):
        source = held if k < 2 else last
        at = pl.ds(pl.multiple_of(x * block, block), block)
        for q in range(4):
            piece = source[k % 2, :, q * part : (q + 1) * part, :].astype(F32)
            out[at, q * cut : (q + 1) * cut] = piece.reshape(block, cut)


def join_body(held, other, out):
    nodes = held.shape[1]

    def put(g, block):
        out[pl.ds(pl.multiple_of(g * nodes, nodes), nodes), :] = block.astype(F32)

    for k, g in enumerate(places(GET_MINE, False)):
        put(g, held[k])
    for k, g in enumerate(places(GET_OTHER, True)):
        put(g, other[k])


def on_device(features, w_one, w_two, neighbor, degree, send_rows, grad_out):
    groups, nodes, cols = features.shape
    width = w_two.shape[1]
    parts = lax.axis_size("dom")
    deep = parts // CHIPS
    sends = send_rows[0]
    kmax = sends.shape[1]
    span = 2 * sends.size
    grads = grad_out[0]
    scale = 1.0 / math.sqrt(groups * nodes * parts)
    y_first, y_second = along_y(0), along_y(1)
    x_first, x_second = along_x(0, parts, groups), along_x(1, parts, groups)
    lines = [[z * CHIPS + x for z in range(deep)] for x in range(CHIPS)]

    def y_move(block, pairs):
        return lax.ppermute(block, "feat", pairs)

    def x_move(block, pairs):
        return lax.ppermute(block, ("feat", "dom"), pairs)

    def swap(block):
        return lax.ppermute(block, "feat", SWAP)

    theirs, w_one = project(features, w_one, True)
    got = swap(theirs)
    mine = project(features, w_one, False)
    give, take, own, own_t, inv, pick, mean, back_t, home = whole(
        "tables",
        tables_body,
        (
            shape((span, 2 * nodes)),
            shape((2 * nodes, span)),
            shape((nodes, nodes)),
            shape((nodes, nodes)),
            shape((nodes, nodes), F32),
            shape((span // 2, nodes)),
            shape((nodes, span // 2)),
            shape((span // 2, nodes)),
            shape((nodes, span // 2)),
        ),
        neighbor[0].T, degree, sends.T,
    )
    flat_t = whole("turn", turn_body, shape((cols, groups * nodes)), features)
    near = y_move(add(mine[:2], got[:2]).astype(BF16), y_first)
    near, give = lax.optimization_barrier((near, give))
    far = y_move(add(mine[2], got[2], near[1]).astype(BF16), y_second)
    far, flat_t = lax.optimization_barrier((far, flat_t))
    block = shape((nodes, width))
    p_self, p_near, boxes = whole(
        "forward",
        forward_body,
        (shape((nodes, width), F32), block, shape((span, width))),
        mine, got, near, far, grads, inv, give,
    )
    recv = trade(boxes.reshape(parts, 2 * kmax, width)).reshape(span, width)
    rows = 2 * width // groups
    lot = shape((span // 2, width))
    boxes, hidden_boxes, term, hidden, first, second, mine = whole(
        "middle",
        middle_body,
        (
            lot,
            lot,
            block,
            block,
            shape((5, rows, width)),
            shape((2, rows, width)),
            shape((2, rows, width)),
        ),
        recv, p_self, p_near, grads, inv, w_two, pick, back_t, take, own, own_t,
        scratch=[pltpu.VMEM((groups, rows, width), BF16)],
        far=(0, 4, 5, 6),
        kept=(1, 2, 3),
    )

    def exchange(boxes):
        return trade(boxes.reshape(parts, kmax, width)).reshape(span // 2, width)

    recv = exchange(boxes)

    got = y_move(first, y_first)
    message = jnp.concatenate([first[:1], got[:1], add(second, got[3:]).astype(BF16)])
    message, recv = lax.optimization_barrier((message, recv))
    hidden_boxes, message = lax.optimization_barrier((hidden_boxes, message))
    d_near = whole("near", near_body, block, recv, term, own_t, home)
    one = y_move(d_near, y_first)
    last = y_move(message, y_second)
    sums = add(mine, got[1:3], last[2:])
    near = jnp.stack([d_near, one])
    held = jnp.concatenate(
        [message[:2], last[:2], near, y_move(near, y_second), sums[:1].astype(BF16)]
    )

    recv = exchange(hidden_boxes)

    kept = 8 * cols // parts // 2
    tail = 4 * width // groups // deep
    first, second, mine = whole(
        "grad",
        grad_body,
        (
            shape((deep, 2 * kept + tail, width // 2)),
            shape((deep, kept, width // 2)),
            shape((deep, kept + tail, width // 2)),
        ),
        flat_t, held, swap(held), sums[1],
        scratch=[
            pltpu.VMEM((groups, nodes, 2 * width), BF16),
            pltpu.VMEM((CHIPS, deep, kept, width // 2), BF16),
        ],
    )
    lot = shape((deep, kept + tail, width // 2))
    got = x_move(first, x_first)
    sent = whole("x_pass", x_pass_body, lot, second, mine, got)
    last = x_move(sent, x_second)
    last, recv = lax.optimization_barrier((last, recv))
    terms = trade(whole("x_sum", x_sum_body, lot, mine, got, sent, last, load=(3,)), lines)
    total = (jnp.sum(terms.astype(F32), axis=0) * scale).astype(BF16)
    total = trade(jnp.broadcast_to(total[None], terms.shape), lines)
    half = kept + tail // 2
    chunk = jnp.concatenate(
        [total[:, kept:half].reshape(nodes, -1), total[:, half:].reshape(nodes, -1)], axis=1
    )
    mine = total[:, :kept]
    one_y = y_move(chunk, y_first)
    one_x = x_move(mine, x_first)
    out = whole("out", out_body, block, recv, hidden, inv, mean, own, w_two, far=(0,))
    one_y, one_x, out = lax.optimization_barrier((one_y, one_x, out))
    held_y = jnp.stack([chunk, one_y])
    held_y = jnp.concatenate([held_y, y_move(held_y, y_second)])
    held_x = jnp.stack([mine, one_x])
    last_x = x_move(held_x, x_second)
    one = whole(
        "spread", spread_body, shape((cols, 2 * width), F32), held_x, last_x, far=(0,)
    )
    two = whole(
        "join", join_body, shape((2 * width, width), F32), held_y, swap(held_y), far=(0,)
    )
    return out[None], one, two


def solution(mesh):
    in_specs = (
        P(None, "dom", "feat"),
        P("feat", None),
        P(),
        P("feat", "dom", None),
        P("feat", "dom"),
        P("feat", "dom", None),
        P("feat", "dom", None),
    )
    out_specs = (P("feat", "dom", None), P("feat", None), P())
    return jax.shard_map(
        on_device, mesh=mesh, in_specs=in_specs, out_specs=out_specs, check_vma=False
    )
```
